32 devices in a mesh: blk: 16 (over z, y, core), fsdp: 2 (over x).
Axes of the slice: x: 2, y: 2, z: 4, core: 2. Of those that a mesh axis runs over, the one named last changes fastest.
Arguments:
- tokens: bfloat16 [2, 2048, 1536], P('fsdp', 'blk'), may hold values from -6 to 6
- cotangent: bfloat16 [2, 2048, 1536], P('fsdp', 'blk'), may hold values from -6 to 6
- segments: int32 [2, 2048], P('fsdp'), may hold values from 0 to 3, as said below
- positions: int32 [2, 2048], P('fsdp', 'blk'), may hold values from 0 to 1919, as said below
- gain_attn: bfloat16 [1536], P(('blk', 'fsdp')), may hold values from 0.5 to 1.5
- gain_ffn: bfloat16 [1536], P(('blk', 'fsdp')), may hold values from 0.5 to 1.5
- w_query: bfloat16 [1536, 1536], P(('blk', 'fsdp')), may hold values from -0.15625 to 0.15625
- w_key: bfloat16 [768, 1536], P(('blk', 'fsdp')), may hold values from -0.15625 to 0.15625
- w_value: bfloat16 [768, 1536], P(('blk', 'fsdp')), may hold values from -0.15625 to 0.15625
- w_output: bfloat16 [1536, 1536], P(('blk', 'fsdp')), may hold values from -2.5 to 2.5
- w_gate: bfloat16 [4096, 1536], P(('blk', 'fsdp')), may hold values from -0.15625 to 0.15625
- w_up: bfloat16 [4096, 1536], P(('blk', 'fsdp')), may hold values from -0.15625 to 0.15625
- w_down: bfloat16 [4096, 1536], P(('blk', 'fsdp')), may hold values from -0.09375 to 0.09375
Outputs:
- result: bfloat16 [2, 2048, 1536], P('fsdp', 'blk')
- grad_tokens: float32 [2, 2048, 1536], P('fsdp', 'blk')
- grad_gain_attn: float32 [1536], P(('blk', 'fsdp'))
- grad_gain_ffn: float32 [1536], P(('blk', 'fsdp'))
- grad_query: float32 [1536, 1536], P(('blk', 'fsdp'))
- grad_key: float32 [768, 1536], P(('blk', 'fsdp'))
- grad_value: float32 [768, 1536], P(('blk', 'fsdp'))
- grad_output: float32 [1536, 1536], P(('blk', 'fsdp'))
- grad_gate: float32 [4096, 1536], P(('blk', 'fsdp'))
- grad_up: float32 [4096, 1536], P(('blk', 'fsdp'))
- grad_down: float32 [4096, 1536], P(('blk', 'fsdp'))
The draws below stay inside these ranges and needn't reach their ends.
Inputs may be any that keep to these rules, and one draw needn't show every extreme that they name: `segments`: in each group, segment numbers never fall along the tokens and every one of the 4 numbers has at least one token; sequence 1 has exactly 1920 tokens and begins within the first 128 tokens. `positions`: A token's offset from the first token of its sequence in the same group.
All inputs are finite; a program needn't handle non-finite values.
Results may differ from the reference program's by a relative error of at most 0.02.
Values may be sent and summed in bfloat16 or wider, within the bound.
No kernel may reach another device: no remote copies, remote signals or barrier semaphores. Data moves between devices by JAX's collectives and lax.ppermute only.
A program may use at most 320 MiB of HBM per device.

```python
import jax
import jax.numpy as jnp
from jax import lax

D = 1536
HEADS = 16
KVH = 8
HD = 96
FF = 4096
TOK_DEV = 128
SEGS = 4
GROUPS = 2
GROUP_TOK = 2048


def pack_layout(key):
    base = jax.random.fold_in(key, 31)
    total = GROUP_TOK
    longest = total - TOK_DEV

    def one_group(group):
        group_key = jax.random.fold_in(base, group)
        order = jax.random.permutation(jax.random.fold_in(group_key, 1), TOK_DEV - 1)
        cuts = jnp.sort(order[:SEGS - 2]).astype(jnp.int32) + 1
        bounds = jnp.concatenate([jnp.zeros((1,), jnp.int32), cuts, jnp.full((1,), TOK_DEV, jnp.int32)])
        pieces = bounds[1:] - bounds[:-1]
        lengths = jnp.concatenate([pieces[:1], jnp.full((1,), longest, jnp.int32), pieces[1:]])
        ends = jnp.cumsum(lengths).astype(jnp.int32)
        starts = ends - lengths
        index = jnp.arange(total, dtype=jnp.int32)
        segs = jnp.sum((index[:, None] >= ends[None, :]).astype(jnp.int32), axis=1)
        numbers = jnp.arange(SEGS, dtype=jnp.int32)
        begin = jnp.sum(jnp.where(segs[:, None] == numbers[None, :], starts[None, :], 0), axis=1)
        return (segs, index - begin)
    return jax.vmap(one_group)(jnp.arange(GROUPS, dtype=jnp.int32))


def draw_segments(key, part):
    return pack_layout(key)[0]


def draw_positions(key, part):
    return pack_layout(key)[1]


def strengthened(values, own_key, source, target, parts, factor):
    def block_of(axis_at):
        return (jnp.arange(values.shape[axis_at]) // (values.shape[axis_at] // parts)).reshape((-1,) + (1,) * (values.ndim - 1 - axis_at))

    one_side = jax.random.permutation(own_key, parts)[block_of(target)]
    far = (block_of(target) + parts // 2) % parts
    return jnp.where((block_of(source) == one_side) | (block_of(source) == far), factor * values, values)


def level_of(stream_key, dims, cuts, least, high):
    loudness = 1.0
    for dim, blocks in cuts:
        heights = jax.random.uniform(jax.random.fold_in(jax.random.fold_in(stream_key, 6), dim), (blocks,), jnp.float32, least / len(cuts), high / len(cuts))
        loudness = loudness * jnp.repeat(jnp.exp(heights), dims[dim] // blocks).reshape((-1,) + (1,) * (len(dims) - 1 - dim))
    return loudness


def bell_draw(own_key, extent, scale, most, cuts=(), held_as=jnp.bfloat16):
    result = scale * jax.random.normal(own_key, extent, jnp.float32)
    if cuts:
        result = result * level_of(own_key, extent, cuts, -0.22, 0.18)
    return jnp.clip(result, -most, most).astype(held_as)


def bell_draw_with(stream_key, shape, deviation, limit, cuts, heavy, held_as=jnp.bfloat16):
    array = deviation * jax.random.normal(stream_key, shape, jnp.float32)
    if cuts:
        array = array * level_of(stream_key, shape, cuts, -0.22, 0.18)
    return jnp.clip(strengthened(array, jax.random.fold_in(stream_key, 3), *heavy), -limit, limit).astype(held_as)


def setup_inputs(seed: int = 0) -> dict:
    seeds = jax.random.split(jax.random.key(seed), 14)
    tokens = bell_draw(seeds[0], (GROUPS, GROUP_TOK, D), 1.0, 6.0, ((0, 2), (1, 16)))
    cotangent = bell_draw_with(seeds[1], (GROUPS, GROUP_TOK, D), 1.0, 6.0, ((0, 2), (1, 16)), (1, 2, 16, 2.0))
    segments = draw_segments(jax.random.fold_in(seeds[13], 71), 0)
    positions = draw_positions(jax.random.fold_in(seeds[13], 71), 0)
    gain_attn = jnp.clip(1.0 + 0.1 * jax.random.normal(seeds[4], (D,), jnp.float32), 0.5, 1.5).astype(jnp.bfloat16)
    gain_ffn = jnp.clip(1.0 + 0.1 * jax.random.normal(seeds[5], (D,), jnp.float32), 0.5, 1.5).astype(jnp.bfloat16)
    w_query = bell_draw(seeds[6], (HEADS * HD, D), D ** -0.5, 0.15625, ((0, 32),))
    w_key = bell_draw(seeds[7], (KVH * HD, D), D ** -0.5, 0.15625, ((0, 32),))
    w_value = bell_draw(seeds[8], (KVH * HD, D), D ** -0.5, 0.15625, ((0, 32),))
    w_output = bell_draw(seeds[9], (D, HEADS * HD), 6 ** -0.5, 2.5, ((0, 32),))
    w_gate = bell_draw(seeds[10], (FF, D), D ** -0.5, 0.15625, ((0, 32),))
    w_up = bell_draw(seeds[11], (FF, D), D ** -0.5, 0.15625, ((0, 32),))
    w_down = bell_draw(seeds[12], (FF, D), FF ** -0.5, 0.09375, ((0, 32),))
    return {"tokens": tokens, "cotangent": cotangent, "segments": segments, "positions": positions, "gain_attn": gain_attn, "gain_ffn": gain_ffn, "w_query": w_query, "w_key": w_key, "w_value": w_value, "w_output": w_output, "w_gate": w_gate, "w_up": w_up, "w_down": w_down}


EPS = 1e-05
ROPE_BASE = 100000.0
NEG = -1e+30
HIGH = lax.Precision.HIGHEST

@jax.custom_vjp
def low(v):
    return lax.optimization_barrier(v.astype(jnp.bfloat16)).astype(jnp.float32)

@jax.custom_vjp
def low_back(v):
    return v

def low_keep(v):
    return (low(v), None)

def low_pass(kept, grad):
    return (grad,)

def back_keep(v):
    return (v, None)

def back_low(kept, grad):
    return (low(grad),)
low.defvjp(low_keep, low_pass)
low_back.defvjp(back_keep, back_low)

def product_t(left, right):
    return lax.dot_general(left, right, (((1,), (1,)), ((), ())), precision=HIGH)

def rms_scale(values):
    return lax.rsqrt(lax.optimization_barrier(jnp.mean(values * values, axis=-1, keepdims=True)) + EPS)

def rotation(positions):
    half = HD // 2
    freqs = ROPE_BASE ** (-(jnp.arange(half, dtype=jnp.float32) * 2.0 / HD))
    angles = positions.astype(jnp.float32)[:, None] * freqs[None, :]
    return (jnp.cos(angles)[:, None, :], jnp.sin(angles)[:, None, :])

def rotate(values, cosine, sine, heads):
    count = values.shape[0]
    split = values.reshape(count, heads, HD)
    half = HD // 2
    first = split[..., :half]
    second = split[..., half:]
    turned = jnp.concatenate([first * cosine - second * sine, second * cosine + first * sine], axis=-1)
    return turned.reshape(count, heads * HD)

def attention(queries, keys, values, segs):
    total = queries.shape[0]
    groups = HEADS // KVH
    size = min(512, total)
    query_heads = queries.reshape(total // size, size, KVH, groups, HD)
    key_heads = keys.reshape(total, KVH, HD)
    value_heads = values.reshape(total, KVH, HD)
    index = jnp.arange(total, dtype=jnp.int32)

    def block(inputs):
        query_block, query_seg, query_idx = inputs
        raw = jnp.einsum('qhgd,khd->hgqk', query_block, key_heads, precision=HIGH) * HD ** (-0.5)
        scores = low_back(raw)
        allowed = (query_seg[:, None] == segs[None, :]) & (index[None, :] <= query_idx[:, None])
        scores = jnp.where(allowed[None, None], scores, NEG)
        top = lax.optimization_barrier(jnp.max(scores, axis=-1, keepdims=True))
        expo = jnp.exp(scores - top)
        probs = expo / lax.optimization_barrier(jnp.sum(expo, axis=-1, keepdims=True))
        return jnp.einsum('hgqk,khd->qhgd', low(probs), value_heads, precision=HIGH)
    mixed = lax.map(jax.checkpoint(block), (query_heads, segs.reshape(total // size, size), index.reshape(total // size, size)))
    return mixed.reshape(total, HEADS * HD)

def group_layer(inputs, segs, positions, gain_one, gain_two, w_query, w_key, w_value, w_output, w_gate, w_up, w_down):
    cosine, sine = rotation(positions)
    normed = low(inputs * rms_scale(inputs) * gain_one)
    query_pre = low_back(product_t(normed, w_query))
    key_pre = low_back(product_t(normed, w_key))
    values = low(low_back(product_t(normed, w_value)))
    queries = low(rotate(query_pre, cosine, sine, HEADS))
    keys = low(rotate(key_pre, cosine, sine, KVH))
    attended = low(low_back(attention(queries, keys, values, segs)))
    middle = inputs + low_back(product_t(attended, w_output))
    normed_two = low(middle * rms_scale(middle) * gain_two)
    gate = low_back(product_t(normed_two, w_gate))
    up = low_back(product_t(normed_two, w_up))
    hidden = low(jax.nn.silu(gate) * up)
    branch = low_back(jnp.dot(hidden, w_down, precision=HIGH))
    return middle + branch

def reference(tokens, cotangent, segments, positions, gain_attn, gain_ffn, w_query, w_key, w_value, w_output, w_gate, w_up, w_down):
    weights = tuple((weight.astype(jnp.float32) for weight in (gain_attn, gain_ffn, w_query, w_key, w_value, w_output, w_gate, w_up, w_down)))
    layer = jax.checkpoint(group_layer)

    def forward(inputs, *params):

        def step(carry, group):
            return (carry, layer(group[0], group[1], group[2], *params))
        return lax.scan(step, jnp.zeros((), jnp.float32), (inputs, segments, positions))[1]
    outputs, pullback = jax.vjp(forward, tokens.astype(jnp.float32), *weights)
    grads = pullback(cotangent.astype(jnp.float32))
    return (outputs.astype(jnp.bfloat16), grads[0], grads[1], grads[2], grads[3], grads[4], grads[5], grads[6], grads[7], grads[8], grads[9])
```

```python
import jax
import jax.numpy as jnp
from jax import lax
from jax.experimental import pallas as pl
from jax.experimental.pallas import tpu as pltpu
from jax.sharding import PartitionSpec as P

HEADS = 16
KVH = 8
HD = 96


EPS = 1e-05
ROPE_BASE = 100000.0
NEG = -1e30


def passed_along(block, axis, distance):
    devices = range(lax.axis_size(axis))
    route = [(i - distance, i) for i in devices if i - distance in devices]
    return lax.ppermute(block, axis, route)


def passed_along_2(x, axis, by):
    length = lax.axis_size(axis)
    return lax.ppermute(x, axis, [(i, (i + by) % length) for i in range(length)])


def product_t(left, right):
    return lax.dot_general(
        left, right, (((1,), (1,)), ((), ())), preferred_element_type=jnp.float32
    )


def product(left, right):
    return jnp.dot(left, right, preferred_element_type=jnp.float32)


def product_tn(left, right):
    return lax.dot_general(
        left, right, (((0,), (0,)), ((), ())), preferred_element_type=jnp.float32
    )


def rms_scale(values):
    return lax.rsqrt(jnp.mean(values * values, axis=-1, keepdims=True) + EPS)


def norm_back(grad, values, scale, gain):
    weighted = grad * gain
    inner = jnp.mean(weighted * values, axis=-1, keepdims=True)
    return (scale * weighted - values * scale**3 * inner, jnp.sum(grad * values * scale, axis=0))


def rotation(positions):
    half = HD // 2
    freqs = ROPE_BASE ** (-(jnp.arange(half, dtype=jnp.float32) * 2.0 / HD))
    angles = positions.astype(jnp.float32)[:, None] * freqs[None, :]
    return (jnp.cos(angles)[:, None, :], jnp.sin(angles)[:, None, :])


def rotate(values, cosine, sine, heads, sign):
    count = values.shape[0]
    split = values.reshape(count, heads, HD)
    half = HD // 2
    first = split[..., :half]
    second = split[..., half:]
    turned = jnp.concatenate(
        [first * cosine - sign * second * sine, second * cosine + sign * first * sine], axis=-1
    )
    return turned.reshape(count, heads * HD)


def block_mask(query_seg, query_idx, key_seg, key_idx):
    return (query_seg[:, None] == key_seg[None, :]) & (key_idx[None, :] <= query_idx[:, None])


def scores_of(queries, keys, allowed):
    raw = jnp.einsum("qhgd,khd->hgqk", queries, keys, preferred_element_type=jnp.float32) * HD ** (
        -0.5
    )
    return jnp.where(allowed[None, None], raw, NEG)


def key_blocks(keys_seen, values_seen, key_segs):
    total = keys_seen.shape[0]
    size = min(512, total)
    count = total // size
    return (
        keys_seen.reshape(count, size, KVH, HD),
        values_seen.reshape(count, size, KVH, HD),
        key_segs.reshape(count, size),
        jnp.arange(total, dtype=jnp.int32).reshape(count, size),
    )


def attend(queries, blocks, query_seg, query_idx):
    rows = queries.shape[0]
    groups = HEADS // KVH
    start = (
        jnp.full((KVH, groups, rows, 1), NEG, jnp.float32),
        jnp.zeros((KVH, groups, rows, 1), jnp.float32),
    )

    def stats_step(carry, block):
        keys, values, segs, idxs = block
        allowed = block_mask(query_seg, query_idx, segs, idxs)
        top, running = carry
        scores = scores_of(queries, keys, allowed)
        new_top = jnp.maximum(top, jnp.max(scores, axis=-1, keepdims=True))
        new_sum = running * jnp.exp(top - new_top) + jnp.sum(
            jnp.exp(scores - new_top), axis=-1, keepdims=True
        )
        return ((new_top, new_sum), None)

    (top, running), unused = lax.scan(stats_step, start, blocks)
    lse = top + jnp.log(running)

    def value_step(total_acc, block):
        keys, values, segs, idxs = block
        allowed = block_mask(query_seg, query_idx, segs, idxs)
        weights = jnp.exp(scores_of(queries, keys, allowed) - lse).astype(jnp.bfloat16)
        return (
            total_acc
            + jnp.einsum("hgqk,khd->qhgd", weights, values, preferred_element_type=jnp.float32),
            None,
        )

    mixed, unused = lax.scan(value_step, jnp.zeros((rows, KVH, groups, HD), jnp.float32), blocks)
    return (mixed, lse)


def cycle_back(queries, own_keys, own_values, key_segs, query_seg, query_idx, lse, grad_out, delta):
    rows = queries.shape[0]
    groups = HEADS // KVH
    scale = HD ** (-0.5)
    me = lax.axis_index("blk")
    count = lax.axis_size("blk")
    local = jnp.arange(rows, dtype=jnp.int32)

    def step(carry, turn):
        grad_q, key_blk, value_blk, grad_k, grad_v = carry
        anchor = (me - turn) % count
        begin = anchor * rows
        segs = lax.dynamic_slice_in_dim(key_segs, begin, rows)
        allowed = block_mask(query_seg, query_idx, segs, begin + local)
        acc_k = grad_k
        acc_v = grad_v
        probs = jnp.exp(scores_of(queries, key_blk, allowed) - lse)
        grad_probs = jnp.einsum(
            "qhgd,khd->hgqk", grad_out, value_blk, preferred_element_type=jnp.float32
        )
        grad_scores = (probs * (grad_probs - delta)).astype(jnp.bfloat16)
        new_acc = grad_q + jnp.einsum(
            "hgqk,khd->qhgd", grad_scores, key_blk, preferred_element_type=jnp.float32
        )
        new_k = (
            acc_k
            + jnp.einsum("hgqk,qhgd->khd", grad_scores, queries, preferred_element_type=jnp.float32)
            * scale
        )
        new_v = acc_v + jnp.einsum(
            "hgqk,qhgd->khd",
            probs.astype(jnp.bfloat16),
            grad_out,
            preferred_element_type=jnp.float32,
        )
        grad_k = new_k
        grad_v = new_v
        key_blk, value_blk = passed_along((key_blk, value_blk), "blk", 1)
        grad_k, grad_v = (
            passed_along_2(grad_k.astype(jnp.bfloat16), "blk", 1).astype(grad_k.dtype),
            passed_along_2(grad_v.astype(jnp.bfloat16), "blk", 1).astype(grad_v.dtype),
        )
        return ((new_acc, key_blk, value_blk, grad_k, grad_v), None)

    zero_kv = jnp.zeros((rows, KVH, HD), jnp.float32)
    start = (
        jnp.zeros((rows, KVH, groups, HD), jnp.float32),
        own_keys.reshape(rows, KVH, HD),
        own_values.reshape(rows, KVH, HD),
        zero_kv,
        zero_kv,
    )
    final, unused = lax.scan(step, start, jnp.arange(count, dtype=jnp.int32))
    grad_q, ignored_k, ignored_v, grad_k, grad_v = final
    return (grad_q * scale, grad_k.reshape(rows, KVH * HD), grad_v.reshape(rows, KVH * HD))


def fetch_attention(gain_attn, gain_ffn, w_query, w_key, w_value, w_output):
    return (
        lax.all_gather(gain_attn, ("blk", "fsdp"), axis=0, tiled=True),
        lax.all_gather(gain_ffn, ("blk", "fsdp"), axis=0, tiled=True),
        lax.all_gather(w_query, ("blk", "fsdp"), axis=0, tiled=True),
        lax.all_gather(w_key, ("blk", "fsdp"), axis=0, tiled=True),
        lax.all_gather(w_value, ("blk", "fsdp"), axis=0, tiled=True),
        lax.all_gather(w_output, ("blk", "fsdp"), axis=0, tiled=True),
    )


def fetch_ffn(w_gate, w_up, w_down):
    return (
        lax.all_gather(w_gate, ("blk", "fsdp"), axis=0, tiled=True),
        lax.all_gather(w_up, ("blk", "fsdp"), axis=0, tiled=True),
        lax.all_gather(w_down, ("blk", "fsdp"), axis=0, tiled=True),
    )


def shards(
    tokens,
    cotangent,
    segments,
    positions,
    gain_attn,
    gain_ffn,
    w_query,
    w_key,
    w_value,
    w_output,
    w_gate,
    w_up,
    w_down,
):
    rows = tokens.shape[1]
    groups = HEADS // KVH
    xin = tokens[0].astype(jnp.float32)
    offset = lax.axis_index("blk") * rows
    query_idx = offset + jnp.arange(rows, dtype=jnp.int32)
    key_segs = segments[0]
    query_seg = lax.dynamic_slice_in_dim(key_segs, offset, rows)
    cosine, sine = rotation(positions[0])
    gain_one, gain_two, query_all, key_all, value_all, output_all = fetch_attention(
        gain_attn, gain_ffn, w_query, w_key, w_value, w_output
    )
    first_gain = gain_one.astype(jnp.float32)
    second_gain = gain_two.astype(jnp.float32)
    first_scale = rms_scale(xin)
    normed = (xin * first_scale * first_gain).astype(jnp.bfloat16)
    queries = rotate(product_t(normed, query_all), cosine, sine, HEADS, 1.0).astype(jnp.bfloat16)
    keys = rotate(product_t(normed, key_all), cosine, sine, KVH, 1.0).astype(jnp.bfloat16)
    values = product_t(normed, value_all).astype(jnp.bfloat16)
    keys_seen, values_seen = (
        lax.all_gather(keys, "blk", axis=0, tiled=True),
        lax.all_gather(values, "blk", axis=0, tiled=True),
    )
    query_heads = queries.reshape(rows, KVH, groups, HD)
    mixed, lse = attend(
        query_heads, key_blocks(keys_seen, values_seen, key_segs), query_seg, query_idx
    )
    attended = mixed.reshape(rows, HEADS * HD).astype(jnp.bfloat16)
    middle = xin + product_t(attended, output_all)
    second_scale = rms_scale(middle)
    normed_two = (middle * second_scale * second_gain).astype(jnp.bfloat16)
    gate_rows, up_rows, down_rows = fetch_ffn(w_gate, w_up, w_down)
    gate = product_t(normed_two, gate_rows)
    up = product_t(normed_two, up_rows)
    sigma = jax.nn.sigmoid(gate)
    activated = gate * sigma
    hidden = (activated * up).astype(jnp.bfloat16)
    branch = product(hidden, down_rows)
    result = (middle + branch).astype(jnp.bfloat16)
    grad_in = cotangent[0]
    gate_rows, up_rows, down_rows = fetch_ffn(w_gate, w_up, w_down)
    grad_hidden = product_t(grad_in, down_rows)
    grad_gate = (grad_hidden * up * sigma * (1.0 + gate * (1.0 - sigma))).astype(jnp.bfloat16)
    grad_up = (grad_hidden * activated).astype(jnp.bfloat16)
    gate_grad = product_tn(grad_gate, normed_two)
    up_grad = product_tn(grad_up, normed_two)
    down_grad = product_tn(hidden, grad_in)
    grad_normed_two = product(grad_gate, gate_rows) + product(grad_up, up_rows)
    gate_grad, up_grad, down_grad = (
        lax.psum_scatter(gate_grad, ("blk", "fsdp"), scatter_dimension=0, tiled=True),
        lax.psum_scatter(up_grad, ("blk", "fsdp"), scatter_dimension=0, tiled=True),
        lax.psum_scatter(down_grad, ("blk", "fsdp"), scatter_dimension=0, tiled=True),
    )
    grad_middle_norm, second_gain_grad = norm_back(
        grad_normed_two, middle, second_scale, second_gain
    )
    grad_middle = grad_in.astype(jnp.float32) + grad_middle_norm
    grad_branch = grad_middle.astype(jnp.bfloat16)
    output_grad = product_tn(grad_branch, attended)
    grad_attended = product(grad_branch, output_all).astype(jnp.bfloat16)
    grad_heads = grad_attended.reshape(rows, KVH, groups, HD)
    delta = jnp.transpose(jnp.sum(grad_heads.astype(jnp.float32) * mixed, axis=-1), (1, 2, 0))[
        ..., None
    ]
    grad_q, grad_keys, grad_values = cycle_back(
        query_heads, keys, values, key_segs, query_seg, query_idx, lse, grad_heads, delta
    )
    grad_q_pre = rotate(grad_q.reshape(rows, HEADS * HD), cosine, sine, HEADS, -1.0).astype(
        jnp.bfloat16
    )
    grad_k_pre = rotate(grad_keys, cosine, sine, KVH, -1.0).astype(jnp.bfloat16)
    grad_v = grad_values.astype(jnp.bfloat16)
    query_grad = product_tn(grad_q_pre, normed)
    key_grad = product_tn(grad_k_pre, normed)
    value_grad = product_tn(grad_v, normed)
    grad_normed = (
        product(grad_q_pre, query_all) + product(grad_k_pre, key_all) + product(grad_v, value_all)
    )
    grad_x_norm, first_gain_grad = norm_back(grad_normed, xin, first_scale, first_gain)
    grad_tokens = grad_middle + grad_x_norm
    first_gain_grad, second_gain_grad, query_grad, key_grad, value_grad, output_grad = (
        lax.psum_scatter(first_gain_grad, ("blk", "fsdp"), scatter_dimension=0, tiled=True),
        lax.psum_scatter(second_gain_grad, ("blk", "fsdp"), scatter_dimension=0, tiled=True),
        lax.psum_scatter(query_grad, ("blk", "fsdp"), scatter_dimension=0, tiled=True),
        lax.psum_scatter(key_grad, ("blk", "fsdp"), scatter_dimension=0, tiled=True),
        lax.psum_scatter(value_grad, ("blk", "fsdp"), scatter_dimension=0, tiled=True),
        lax.psum_scatter(output_grad, ("blk", "fsdp"), scatter_dimension=0, tiled=True),
    )
    return (
        result[None],
        grad_tokens[None],
        first_gain_grad,
        second_gain_grad,
        query_grad,
        key_grad,
        value_grad,
        output_grad,
        gate_grad,
        up_grad,
        down_grad,
    )


CHIPS = 8
TOK = 128
PAIR = 2 * HD
LANES = 128
LOG2E = 1.4426950408889634
RING = (0, 2, 4, 6, 7, 5, 3, 1)
SAME_CORE = [[2 * c + core for c in range(CHIPS)] for core in range(2)]


def ring_route(step):
    return [
        (RING[k] * 2 + core, RING[(k + step) % CHIPS] * 2 + core)
        for k in range(CHIPS)
        for core in range(2)
    ]


def ring_up(value):
    return lax.ppermute(value, "blk", ring_route(1))


def ring_down(value):
    return lax.ppermute(value, "blk", ring_route(-1))


def flipped(value, bit):
    return lax.ppermute(value, "blk", [(i, i ^ bit) for i in range(2 * CHIPS)])


def core_swap(value):
    return flipped(value, 1)


def x_swap(value):
    return lax.ppermute(value, "fsdp", [(0, 1), (1, 0)])


def ring_gather(block):
    up = block
    down = block
    found = [None] * CHIPS
    found[0] = block
    for step in (1, 2, 3):
        up = ring_up(up)
        down = ring_down(down)
        found[CHIPS - step] = up
        found[step] = down
    half = block.shape[0] // 2
    found[4] = jnp.concatenate([ring_up(up[:half]), ring_down(down[half:])], axis=0)
    return found


def ring_scatter(parts):
    low = jnp.bfloat16
    full = jnp.float32
    half = parts[0].shape[0] // 2
    up = ring_up(parts[4][:half].astype(low)).astype(full)
    down = ring_down(parts[4][half:].astype(low)).astype(full)
    up = jnp.concatenate([parts[3][:half] + up, parts[3][half:]], axis=0)
    down = jnp.concatenate([parts[5][:half], parts[5][half:] + down], axis=0)
    for step in (2, 1, 0):
        up = ring_up(up.astype(low)).astype(full)
        down = ring_down(down.astype(low)).astype(full)
        if step:
            up = up + parts[step]
            down = down + parts[CHIPS - step]
    return parts[0] + (up + down)


def gathered_vector(local, bits):
    for bit, axis_bit in bits:
        other = x_swap(local) if axis_bit is None else flipped(local, axis_bit)
        local = jnp.where(
            bit == 0,
            jnp.concatenate([local, other], axis=-1),
            jnp.concatenate([other, local], axis=-1),
        )
    return local


def scattered_vector(whole, bits):
    for bit, axis_bit in reversed(bits):
        half = whole.shape[-1] // 2
        first, second = whole[..., :half], whole[..., half:]
        keep = jnp.where(bit == 0, first, second)
        send = jnp.where(bit == 0, second, first)
        other = x_swap(send) if axis_bit is None else flipped(send, axis_bit)
        whole = keep + other
    return whole


def dot_nt(left, right):
    return lax.dot_general(
        left, right, (((1,), (1,)), ((), ())), preferred_element_type=jnp.float32
    )


def dot_nn(left, right):
    return lax.dot_general(
        left, right, (((1,), (0,)), ((), ())), preferred_element_type=jnp.float32
    )


def project_kernel(table, *refs):
    blocks = refs[:CHIPS]
    gain, weight, cosine, sine, normed_out, query_out, kv_out = refs[CHIPS:]
    for j in range(CHIPS):
        values = blocks[j][...].astype(jnp.float32)
        scale = lax.rsqrt(jnp.mean(values * values, axis=-1, keepdims=True) + EPS)
        normed = (values * scale * gain[...]).astype(jnp.bfloat16)
        normed_out[j * TOK : (j + 1) * TOK, :] = normed
        pre = dot_nt(normed, weight[...])
        rows = pl.ds(pl.multiple_of(table[j] * TOK, TOK), TOK)
        cos = cosine[rows, :]
        sin = sine[rows, :]
        for head in range(3):
            part = pre[:, head * LANES : (head + 1) * LANES]
            turned = (part * cos + pltpu.roll(part, LANES // 2, 1) * sin).astype(jnp.bfloat16)
            if head < 2:
                query_out[rows, head * LANES : (head + 1) * LANES] = turned
            else:
                kv_out[rows, :LANES] = turned
        kv_out[rows, LANES:] = pre[:, 3 * LANES :].astype(jnp.bfloat16)


def project(table, blocks, gain, weight, cosine, sine):
    tokens = CHIPS * TOK
    width = blocks[0].shape[1]
    whole = pl.BlockSpec(memory_space=pltpu.VMEM)
    return pl.pallas_call(
        project_kernel,
        out_shape=(
            jax.ShapeDtypeStruct((tokens, width), jnp.bfloat16),
            jax.ShapeDtypeStruct((tokens, 2 * LANES), jnp.bfloat16),
            jax.ShapeDtypeStruct((tokens, 2 * LANES), jnp.bfloat16),
        ),
        in_specs=[pl.BlockSpec(memory_space=pltpu.SMEM)] + [whole] * (CHIPS + 4),
        out_specs=(whole, whole, whole),
        compiler_params=pltpu.CompilerParams(vmem_limit_bytes=48 << 20),
        cost_estimate=pl.CostEstimate(
            flops=2 * tokens * width * 4 * LANES, bytes_accessed=10 << 20, transcendentals=0
        ),
        name="project",
    )(table, *blocks, gain, weight, cosine, sine)


def key_index(core, count):
    row = lax.broadcasted_iota(jnp.int32, (count, 1), 0)
    return (row // TOK) * (2 * TOK) + core * TOK + row % TOK


def query_index(core, chip):
    lane = lax.broadcasted_iota(jnp.int32, (1, 2 * TOK), 1)
    return lane % TOK + (2 * chip + core) * TOK


def both_heads(ref, rows):
    return jnp.concatenate([ref[rows, :LANES], ref[rows, LANES:]], axis=0)


def attend_kernel(core_ref, query, own, peer, begin, attended, mixed, lse):
    core = core_ref[0]
    factor = HD ** (-0.5) * LOG2E
    sides = ((own, core), (peer, 1 - core))
    values_t = [jnp.transpose(kv[:, LANES:]) for kv, _ in sides]
    for chip in range(CHIPS):
        count = (chip + 1) * TOK
        rows = slice(chip * TOK, count)
        queries = both_heads(query, rows)
        at = query_index(core, chip)
        first = begin[chip]
        scores = []
        for kv, side in sides:
            raw = dot_nt(kv[:count, :LANES], queries) * factor
            keys_at = key_index(side, count)
            scores.append(jnp.where((keys_at <= at) & (keys_at >= first), raw, NEG))
        top = jnp.maximum(
            jnp.max(scores[0], axis=0, keepdims=True), jnp.max(scores[1], axis=0, keepdims=True)
        )
        weights = [jnp.exp2(part - top) for part in scores]
        total = jnp.sum(weights[0], axis=0, keepdims=True) + jnp.sum(
            weights[1], axis=0, keepdims=True
        )
        mix = dot_nn(values_t[0][:, :count], weights[0].astype(jnp.bfloat16)) + dot_nn(
            values_t[1][:, :count], weights[1].astype(jnp.bfloat16)
        )
        mix = mix / total
        mixed[chip] = mix
        lse[chip] = top + jnp.log2(total)
        back = jnp.transpose(mix).astype(jnp.bfloat16)
        attended[rows, :HD] = back[:TOK, :HD]
        attended[rows, HD:] = back[TOK:, :HD]


def attend_heads(core, query, own, peer, begin):
    tokens = CHIPS * TOK
    whole = pl.BlockSpec(memory_space=pltpu.VMEM)
    return pl.pallas_call(
        attend_kernel,
        out_shape=(
            jax.ShapeDtypeStruct((tokens, PAIR), jnp.bfloat16),
            jax.ShapeDtypeStruct((CHIPS, LANES, 2 * TOK), jnp.float32),
            jax.ShapeDtypeStruct((CHIPS, 1, 2 * TOK), jnp.float32),
        ),
        in_specs=[pl.BlockSpec(memory_space=pltpu.SMEM)] + [whole] * 4,
        out_specs=(whole, whole, whole),
        compiler_params=pltpu.CompilerParams(vmem_limit_bytes=48 << 20),
        cost_estimate=pl.CostEstimate(
            flops=4 * 36 * 256 * 256 * LANES, bytes_accessed=5 << 20, transcendentals=36 * 256 * 256
        ),
        name="attend",
    )(core, query, own, peer, begin)


def attend_back_kernel(
    core_ref, query, own, peer, begin, grad_out, mixed, lse, cosine, sine,
    grad_query, grad_own, grad_peer,
):
    core = core_ref[0]
    scale = HD ** (-0.5)
    factor = scale * LOG2E
    sides = ((own, core, grad_own), (peer, 1 - core, grad_peer))
    keys_t = [jnp.transpose(kv[:, :LANES]) for kv, _, _ in sides]
    grad_own[...] = jnp.zeros_like(grad_own)
    grad_peer[...] = jnp.zeros_like(grad_peer)
    pad = jnp.zeros((TOK, LANES - HD), jnp.bfloat16)
    for chip in range(CHIPS):
        count = (chip + 1) * TOK
        rows = slice(chip * TOK, count)
        queries = both_heads(query, rows)
        grad_rows = grad_out[rows, :]
        grads = jnp.concatenate(
            [
                jnp.concatenate([grad_rows[:, :HD], pad], axis=1),
                jnp.concatenate([grad_rows[:, HD:], pad], axis=1),
            ],
            axis=0,
        )
        delta = jnp.sum(
            jnp.transpose(grads.astype(jnp.float32)) * mixed[chip], axis=0, keepdims=True
        )
        at = query_index(core, chip)
        first = begin[chip]
        level = lse[chip]
        grad_q = jnp.zeros((LANES, 2 * TOK), jnp.float32)
        for (kv, side, grad_kv), key_t in zip(sides, keys_t):
            raw = dot_nt(kv[:count, :LANES], queries) * factor
            keys_at = key_index(side, count)
            allowed = (keys_at <= at) & (keys_at >= first)
            probs = jnp.exp2(jnp.where(allowed, raw - level, NEG))
            grad_probs = dot_nt(kv[:count, LANES:], grads)
            grad_scores = (probs * (grad_probs - delta)).astype(jnp.bfloat16)
            grad_kv[:count, LANES:] += dot_nn(probs.astype(jnp.bfloat16), grads)
            grad_kv[:count, :LANES] += dot_nn(grad_scores, queries)
            grad_q += dot_nn(key_t[:, :count], grad_scores)
        grad_q = jnp.transpose(grad_q) * scale
        cos = cosine[rows, :]
        sin = sine[rows, :]
        for head in range(2):
            part = grad_q[head * TOK : (head + 1) * TOK]
            turned = part * cos - pltpu.roll(part, LANES // 2, 1) * sin
            grad_query[rows, head * LANES : (head + 1) * LANES] = turned.astype(jnp.bfloat16)
    for grad_kv in (grad_own, grad_peer):
        grad_kv[:, :LANES] = grad_kv[:, :LANES] * scale


def attend_back(core, query, own, peer, begin, grad_out, mixed, lse, cosine, sine):
    tokens = CHIPS * TOK
    whole = pl.BlockSpec(memory_space=pltpu.VMEM)
    return pl.pallas_call(
        attend_back_kernel,
        out_shape=(
            jax.ShapeDtypeStruct((tokens, 2 * LANES), jnp.bfloat16),
            jax.ShapeDtypeStruct((tokens, 2 * LANES), jnp.float32),
            jax.ShapeDtypeStruct((tokens, 2 * LANES), jnp.float32),
        ),
        in_specs=[pl.BlockSpec(memory_space=pltpu.SMEM)] + [whole] * 9,
        out_specs=(whole, whole, whole),
        compiler_params=pltpu.CompilerParams(vmem_limit_bytes=48 << 20),
        cost_estimate=pl.CostEstimate(
            flops=10 * 36 * 256 * 256 * LANES, bytes_accessed=8 << 20, transcendentals=36 * 256 * 256
        ),
        name="attend_back",
    )(core, query, own, peer, begin, grad_out, mixed, lse, cosine, sine)


def collect_kernel(table, grad_query, grad_own, grad_other, cosine, sine, out):
    for j in range(CHIPS):
        rows = pl.ds(pl.multiple_of(table[j] * TOK, TOK), TOK)
        here = slice(j * TOK, (j + 1) * TOK)
        out[here, : 2 * LANES] = grad_query[rows, :]
        total = grad_own[rows, :] + grad_other[rows, :]
        part = total[:, :LANES]
        turned = part * cosine[rows, :] - pltpu.roll(part, LANES // 2, 1) * sine[rows, :]
        out[here, 2 * LANES : 3 * LANES] = turned.astype(jnp.bfloat16)
        out[here, 3 * LANES :] = total[:, LANES:].astype(jnp.bfloat16)


def collect(table, grad_query, grad_own, grad_other, cosine, sine):
    tokens = CHIPS * TOK
    whole = pl.BlockSpec(memory_space=pltpu.VMEM)
    return pl.pallas_call(
        collect_kernel,
        out_shape=jax.ShapeDtypeStruct((tokens, 4 * LANES), jnp.bfloat16),
        in_specs=[pl.BlockSpec(memory_space=pltpu.SMEM)] + [whole] * 5,
        out_specs=whole,
        compiler_params=pltpu.CompilerParams(vmem_limit_bytes=32 << 20),
        cost_estimate=pl.CostEstimate(
            flops=8 * tokens * LANES, bytes_accessed=5 << 20, transcendentals=0
        ),
        name="collect",
    )(table, grad_query, grad_own, grad_other, cosine, sine)


def head_weights(w_query, w_key, w_value, core, side):
    packed = jnp.concatenate([w_query, w_key, w_value], axis=0)
    other = x_swap(packed)
    pair = jnp.where(side == 0, jnp.stack([packed, other]), jnp.stack([other, packed]))
    far = core_swap(pair)
    quad = jnp.where(core == 0, jnp.stack([pair, far]), jnp.stack([far, pair]))
    width = w_query.shape[1]
    nq = w_query.shape[0]
    nk = w_key.shape[0]
    gap = jnp.zeros((LANES // 2 - HD // 2, width), w_query.dtype)
    rows = []
    for c in range(2):
        for f in range(2):
            rows += [quad[c, f, :nq], gap]
    for c in range(2):
        rows += [quad[c, 0, nq : nq + nk], quad[c, 1, nq : nq + nk], gap]
    for c in range(2):
        rows += [quad[c, 0, nq + nk :], quad[c, 1, nq + nk :]]
    rows += [gap, gap]
    return jnp.concatenate(rows, axis=0)


def head_gradient(grad, core, side):
    half = LANES // 2
    nq = HD // 2
    nk = HD // 4
    pieces = []
    for c in range(2):
        for f in range(2):
            piece = [
                grad[c * LANES + f * half : c * LANES + f * half + nq],
                grad[2 * LANES + c * half + f * nk : 2 * LANES + c * half + (f + 1) * nk],
                grad[3 * LANES + (2 * c + f) * nk : 3 * LANES + (2 * c + f + 1) * nk],
            ]
            pieces.append(jnp.concatenate(piece, axis=0))
    pairs = [jnp.stack(pieces[:2]), jnp.stack(pieces[2:])]
    mine = jnp.where(core == 0, pairs[0], pairs[1])
    mine = mine + core_swap(jnp.where(core == 0, pairs[1], pairs[0]))
    total = jnp.where(side == 0, mine[0], mine[1]) + x_swap(
        jnp.where(side == 0, mine[1], mine[0])
    )
    return total[:nq], total[nq : nq + nk], total[nq + nk :]


def plane_shards(
    tokens,
    cotangent,
    segments,
    positions,
    gain_attn,
    gain_ffn,
    w_query,
    w_key,
    w_value,
    w_output,
    w_gate,
    w_up,
    w_down,
):
    full = jnp.float32
    low = jnp.bfloat16
    block = tokens[0]
    width = block.shape[1]
    index = lax.axis_index("blk")
    side = lax.axis_index("fsdp")
    core = index % 2
    chip = index // 2
    spot = jnp.where(chip % 2 == 0, chip // 2, CHIPS - 1 - chip // 2)
    table = jnp.asarray(RING, jnp.int32)[(spot + jnp.arange(CHIPS, dtype=jnp.int32)) % CHIPS]
    core_id = core.astype(jnp.int32)[None]
    bits = [(side, None)] + [((index >> b) & 1, 1 << b) for b in range(4)]

    x_blocks = ring_gather(block)
    gains = gathered_vector(jnp.stack([gain_attn, gain_ffn]), bits).astype(full)
    gain_one = gains[:1]
    gain_two = gains[1:]
    w_heads = head_weights(w_query, w_key, w_value, core, side)
    w_out = lax.all_gather(w_output, ("blk", "fsdp"), axis=0, tiled=True)

    segs = segments[0]
    local = jnp.arange(TOK, dtype=jnp.int32)
    own_segs = lax.dynamic_index_in_dim(segs.reshape(CHIPS, 2, TOK), core, 1, keepdims=False)
    begin = jnp.zeros_like(own_segs)
    for number in range(1, 4):
        begin = jnp.where(own_segs == number, jnp.sum((segs < number).astype(jnp.int32)), begin)
    where = jnp.arange(CHIPS, dtype=jnp.int32)[:, None] * (2 * TOK) + core * TOK + local[None, :]
    place = (where - begin).reshape(CHIPS * TOK)
    half = HD // 2
    freqs = ROPE_BASE ** (-(jnp.arange(half, dtype=full) * 2.0 / HD))
    spare = jnp.zeros((LANES // 2 - half,), full)
    both = jnp.concatenate([freqs, spare, freqs, spare])
    angles = place.astype(full)[:, None] * both[None, :]
    sign = jnp.where(jnp.arange(LANES) < LANES // 2, -1.0, 1.0).astype(full)
    cosine = jnp.cos(angles)
    sine = jnp.sin(angles) * sign[None, :]
    begin2 = jnp.concatenate([begin, begin], axis=1)[:, None, :]

    normed, query, kv = project(table, x_blocks, gain_one, w_heads, cosine, sine)
    kv_peer = core_swap(kv)
    attended_heads, mixed, lse = attend_heads(core_id, query, kv, kv_peer, begin2)
    attended = lax.all_to_all(
        attended_heads.reshape(CHIPS, TOK, PAIR),
        "blk",
        split_axis=0,
        concat_axis=0,
        axis_index_groups=SAME_CORE,
        tiled=True,
    )
    attended = jnp.transpose(attended, (1, 0, 2)).reshape(TOK, CHIPS * PAIR)

    x_own = block.astype(full)
    middle = x_own + product_t(attended, w_out)
    second_scale = rms_scale(middle)
    normed_two = (middle * second_scale * gain_two).astype(low)

    count = w_gate.shape[0]
    packed = jnp.concatenate([w_gate, w_up, w_down], axis=0)
    packed_x = x_swap(packed)
    packed_c = core_swap(packed)
    packed_cx = core_swap(packed_x)
    four = (packed, packed_x, packed_c, packed_cx)
    gates = [p[:count] for p in four]
    ups = [p[count : 2 * count] for p in four]
    w_gu = jnp.concatenate(gates[:2] + ups[:2] + gates[2:] + ups[2:], axis=0)
    w_dn = jnp.concatenate([p[2 * count :] for p in four], axis=0)

    tied, _ = lax.optimization_barrier((cotangent[0], x_blocks[4]))
    e_blocks = ring_gather(tied)
    e_all = jnp.concatenate(e_blocks, axis=0)
    grad_hidden_all = product_t(e_all, w_dn)

    h_blocks = ring_gather(normed_two)
    wide = 2 * count
    groups = ((0, 1, 7), (2, 6), (3, 4, 5))
    z_parts = [None] * CHIPS
    d_parts = [None] * CHIPS
    hiddens = [None] * CHIPS
    grads_gu = [None] * CHIPS
    for group in groups:
        rows = jnp.concatenate([h_blocks[j] for j in group], axis=0)
        grad_hidden = jnp.concatenate(
            [grad_hidden_all[j * TOK : (j + 1) * TOK] for j in group], axis=0
        )
        pre = product_t(rows, w_gu)
        hid = []
        dgu = []
        for part in range(2):
            gate = pre[:, part * 2 * wide : part * 2 * wide + wide]
            up = pre[:, part * 2 * wide + wide : (part + 1) * 2 * wide]
            dhid = grad_hidden[:, part * wide : (part + 1) * wide]
            sigma = jax.nn.sigmoid(gate)
            activated = gate * sigma
            hid.append((activated * up).astype(low))
            dgu.append((dhid * up * sigma * (1.0 + gate * (1.0 - sigma))).astype(low))
            dgu.append((dhid * activated).astype(low))
        hid = jnp.concatenate(hid, axis=1)
        dgu = jnp.concatenate(dgu, axis=1)
        back = product(dgu, w_gu)
        branch = product(hid, w_dn)
        for n, j in enumerate(group):
            cut = slice(n * TOK, (n + 1) * TOK)
            d_parts[j] = back[cut]
            z_parts[j] = branch[cut]
            hiddens[j] = hid[cut]
            grads_gu[j] = dgu[cut]
    grad_normed_two = ring_scatter(d_parts)
    branch = ring_scatter(z_parts)
    result = (middle + branch).astype(low)

    h_all = jnp.concatenate(h_blocks, axis=0)
    hid_all = jnp.concatenate(hiddens, axis=0)
    dgu_all = jnp.concatenate(grads_gu, axis=0)
    send_gu = product_tn(dgu_all[:, 2 * wide :], h_all)
    send_dn = product_tn(hid_all[:, wide:], e_all)
    keep_gu = product_tn(dgu_all[:, : 2 * wide], h_all)
    keep_dn = product_tn(hid_all[:, :wide], e_all)
    sum_gu = keep_gu + core_swap(send_gu)
    sum_dn = keep_dn + core_swap(send_dn)
    sent = jnp.concatenate([sum_gu[count:wide], sum_gu[wide + count :], sum_dn[count:]], axis=0)
    received = x_swap(sent)
    gate_grad = sum_gu[:count] + received[:count]
    up_grad = sum_gu[wide : wide + count] + received[count:wide]
    down_grad = sum_dn[:count] + received[wide:]

    grad_in = cotangent[0]
    grad_middle_norm, second_gain_grad = norm_back(
        grad_normed_two, middle, second_scale, gain_two
    )
    grad_middle = grad_in.astype(full) + grad_middle_norm
    grad_branch = grad_middle.astype(low)
    grad_attended = product(grad_branch, w_out).astype(low)
    grad_attended = jnp.transpose(grad_attended.reshape(TOK, CHIPS, PAIR), (1, 0, 2))
    grad_heads = lax.all_to_all(
        grad_attended,
        "blk",
        split_axis=0,
        concat_axis=0,
        axis_index_groups=SAME_CORE,
        tiled=True,
    ).reshape(CHIPS * TOK, PAIR)
    output_grad = lax.psum_scatter(
        product_tn(grad_branch, attended).astype(low),
        ("blk", "fsdp"),
        scatter_dimension=0,
        tiled=True,
    ).astype(full)

    grad_query, grad_own, grad_peer = attend_back(
        core_id, query, kv, kv_peer, begin2, grad_heads, mixed, lse, cosine, sine
    )
    grad_heads_all = collect(table, grad_query, grad_own, core_swap(grad_peer), cosine, sine)
    grad_normed_all = product(grad_heads_all, w_heads)
    parts = [grad_normed_all[j * TOK : (j + 1) * TOK] for j in range(CHIPS)]
    first_gain_grad = 0.0
    for j in range(CHIPS):
        values = x_blocks[j].astype(full)
        first_gain_grad = first_gain_grad + jnp.sum(
            parts[j] * values * rms_scale(values), axis=0
        )
    gain_grads = scattered_vector(jnp.stack([first_gain_grad, second_gain_grad]), bits)
    grad_normed = ring_scatter(parts)
    heads_grad = product_tn(grad_heads_all, normed)
    query_grad, key_grad, value_grad = head_gradient(heads_grad, core, side)
    grad_x_norm, _ = norm_back(grad_normed, x_own, rms_scale(x_own), gain_one)
    grad_tokens = grad_middle + grad_x_norm
    return (
        result[None],
        grad_tokens[None],
        gain_grads[0],
        gain_grads[1],
        query_grad,
        key_grad,
        value_grad,
        output_grad,
        gate_grad,
        up_grad,
        down_grad,
    )


def by_plane(mesh):
    return dict(mesh.shape) == {"blk": 2 * CHIPS, "fsdp": 2} and KVH == CHIPS


def solution(mesh):
    in_specs = (
        P("fsdp", "blk", None),
        P("fsdp", "blk", None),
        P("fsdp", None),
        P("fsdp", "blk"),
        P(("blk", "fsdp")),
        P(("blk", "fsdp")),
        P(("blk", "fsdp"), None),
        P(("blk", "fsdp"), None),
        P(("blk", "fsdp"), None),
        P(("blk", "fsdp"), None),
        P(("blk", "fsdp"), None),
        P(("blk", "fsdp"), None),
        P(("blk", "fsdp"), None),
    )
    out_specs = (
        P("fsdp", "blk", None),
        P("fsdp", "blk", None),
        P(("blk", "fsdp")),
        P(("blk", "fsdp")),
        P(("blk", "fsdp"), None),
        P(("blk", "fsdp"), None),
        P(("blk", "fsdp"), None),
        P(("blk", "fsdp"), None),
        P(("blk", "fsdp"), None),
        P(("blk", "fsdp"), None),
        P(("blk", "fsdp"), None),
    )
    body = plane_shards if by_plane(mesh) else shards
    return jax.shard_map(body, mesh=mesh, in_specs=in_specs, out_specs=out_specs, check_vma=False)
```

```python
import functools

import jax
import jax.numpy as jnp
from jax import lax
from jax.experimental import pallas as pl
from jax.experimental.pallas import tpu as pltpu
from jax.sharding import PartitionSpec as P

HEADS = 16
KVH = 8
HD = 96


EPS = 1e-05
ROPE_BASE = 100000.0
NEG = -1e30


def passed_along(block, axis, distance):
    devices = range(lax.axis_size(axis))
    route = [(i - distance, i) for i in devices if i - distance in devices]
    return lax.ppermute(block, axis, route)


def passed_along_2(x, axis, by):
    length = lax.axis_size(axis)
    return lax.ppermute(x, axis, [(i, (i + by) % length) for i in range(length)])


def product_t(left, right):
    return lax.dot_general(
        left, right, (((1,), (1,)), ((), ())), preferred_element_type=jnp.float32
    )


def product(left, right):
    return jnp.dot(left, right, preferred_element_type=jnp.float32)


def product_tn(left, right):
    return lax.dot_general(
        left, right, (((0,), (0,)), ((), ())), preferred_element_type=jnp.float32
    )


def rms_scale(values):
    return lax.rsqrt(jnp.mean(values * values, axis=-1, keepdims=True) + EPS)


def norm_back(grad, values, scale, gain):
    weighted = grad * gain
    inner = jnp.mean(weighted * values, axis=-1, keepdims=True)
    return (scale * weighted - values * scale**3 * inner, jnp.sum(grad * values * scale, axis=0))


def rotation(positions):
    half = HD // 2
    freqs = ROPE_BASE ** (-(jnp.arange(half, dtype=jnp.float32) * 2.0 / HD))
    angles = positions.astype(jnp.float32)[:, None] * freqs[None, :]
    return (jnp.cos(angles)[:, None, :], jnp.sin(angles)[:, None, :])


def rotate(values, cosine, sine, heads, sign):
    count = values.shape[0]
    split = values.reshape(count, heads, HD)
    half = HD // 2
    first = split[..., :half]
    second = split[..., half:]
    turned = jnp.concatenate(
        [first * cosine - sign * second * sine, second * cosine + sign * first * sine], axis=-1
    )
    return turned.reshape(count, heads * HD)


def block_mask(query_seg, query_idx, key_seg, key_idx):
    return (query_seg[:, None] == key_seg[None, :]) & (key_idx[None, :] <= query_idx[:, None])


def scores_of(queries, keys, allowed):
    raw = jnp.einsum("qhgd,khd->hgqk", queries, keys, preferred_element_type=jnp.float32) * HD ** (
        -0.5
    )
    return jnp.where(allowed[None, None], raw, NEG)


def key_blocks(keys_seen, values_seen, key_segs):
    total = keys_seen.shape[0]
    size = min(512, total)
    count = total // size
    return (
        keys_seen.reshape(count, size, KVH, HD),
        values_seen.reshape(count, size, KVH, HD),
        key_segs.reshape(count, size),
        jnp.arange(total, dtype=jnp.int32).reshape(count, size),
    )


def attend(queries, blocks, query_seg, query_idx):
    rows = queries.shape[0]
    groups = HEADS // KVH
    start = (
        jnp.full((KVH, groups, rows, 1), NEG, jnp.float32),
        jnp.zeros((KVH, groups, rows, 1), jnp.float32),
    )

    def stats_step(carry, block):
        keys, values, segs, idxs = block
        allowed = block_mask(query_seg, query_idx, segs, idxs)
        top, running = carry
        scores = scores_of(queries, keys, allowed)
        new_top = jnp.maximum(top, jnp.max(scores, axis=-1, keepdims=True))
        new_sum = running * jnp.exp(top - new_top) + jnp.sum(
            jnp.exp(scores - new_top), axis=-1, keepdims=True
        )
        return ((new_top, new_sum), None)

    (top, running), unused = lax.scan(stats_step, start, blocks)
    lse = top + jnp.log(running)

    def value_step(total_acc, block):
        keys, values, segs, idxs = block
        allowed = block_mask(query_seg, query_idx, segs, idxs)
        weights = jnp.exp(scores_of(queries, keys, allowed) - lse).astype(jnp.bfloat16)
        return (
            total_acc
            + jnp.einsum("hgqk,khd->qhgd", weights, values, preferred_element_type=jnp.float32),
            None,
        )

    mixed, unused = lax.scan(value_step, jnp.zeros((rows, KVH, groups, HD), jnp.float32), blocks)
    return (mixed, lse)


def cycle_back(queries, own_keys, own_values, key_segs, query_seg, query_idx, lse, grad_out, delta):
    rows = queries.shape[0]
    groups = HEADS // KVH
    scale = HD ** (-0.5)
    me = lax.axis_index("blk")
    count = lax.axis_size("blk")
    local = jnp.arange(rows, dtype=jnp.int32)

    def step(carry, turn):
        grad_q, key_blk, value_blk, grad_k, grad_v = carry
        anchor = (me - turn) % count
        begin = anchor * rows
        segs = lax.dynamic_slice_in_dim(key_segs, begin, rows)
        allowed = block_mask(query_seg, query_idx, segs, begin + local)
        acc_k = grad_k
        acc_v = grad_v
        probs = jnp.exp(scores_of(queries, key_blk, allowed) - lse)
        grad_probs = jnp.einsum(
            "qhgd,khd->hgqk", grad_out, value_blk, preferred_element_type=jnp.float32
        )
        grad_scores = (probs * (grad_probs - delta)).astype(jnp.bfloat16)
        new_acc = grad_q + jnp.einsum(
            "hgqk,khd->qhgd", grad_scores, key_blk, preferred_element_type=jnp.float32
        )
        new_k = (
            acc_k
            + jnp.einsum("hgqk,qhgd->khd", grad_scores, queries, preferred_element_type=jnp.float32)
            * scale
        )
        new_v = acc_v + jnp.einsum(
            "hgqk,qhgd->khd",
            probs.astype(jnp.bfloat16),
            grad_out,
            preferred_element_type=jnp.float32,
        )
        grad_k = new_k
        grad_v = new_v
        key_blk, value_blk = passed_along((key_blk, value_blk), "blk", 1)
        grad_k, grad_v = (
            passed_along_2(grad_k.astype(jnp.bfloat16), "blk", 1).astype(grad_k.dtype),
            passed_along_2(grad_v.astype(jnp.bfloat16), "blk", 1).astype(grad_v.dtype),
        )
        return ((new_acc, key_blk, value_blk, grad_k, grad_v), None)

    zero_kv = jnp.zeros((rows, KVH, HD), jnp.float32)
    start = (
        jnp.zeros((rows, KVH, groups, HD), jnp.float32),
        own_keys.reshape(rows, KVH, HD),
        own_values.reshape(rows, KVH, HD),
        zero_kv,
        zero_kv,
    )
    final, unused = lax.scan(step, start, jnp.arange(count, dtype=jnp.int32))
    grad_q, ignored_k, ignored_v, grad_k, grad_v = final
    return (grad_q * scale, grad_k.reshape(rows, KVH * HD), grad_v.reshape(rows, KVH * HD))


def fetch_attention(gain_attn, gain_ffn, w_query, w_key, w_value, w_output):
    return (
        lax.all_gather(gain_attn, ("blk", "fsdp"), axis=0, tiled=True),
        lax.all_gather(gain_ffn, ("blk", "fsdp"), axis=0, tiled=True),
        lax.all_gather(w_query, ("blk", "fsdp"), axis=0, tiled=True),
        lax.all_gather(w_key, ("blk", "fsdp"), axis=0, tiled=True),
        lax.all_gather(w_value, ("blk", "fsdp"), axis=0, tiled=True),
        lax.all_gather(w_output, ("blk", "fsdp"), axis=0, tiled=True),
    )


def fetch_ffn(w_gate, w_up, w_down):
    return (
        lax.all_gather(w_gate, ("blk", "fsdp"), axis=0, tiled=True),
        lax.all_gather(w_up, ("blk", "fsdp"), axis=0, tiled=True),
        lax.all_gather(w_down, ("blk", "fsdp"), axis=0, tiled=True),
    )


def shards(
    tokens,
    cotangent,
    segments,
    positions,
    gain_attn,
    gain_ffn,
    w_query,
    w_key,
    w_value,
    w_output,
    w_gate,
    w_up,
    w_down,
):
    rows = tokens.shape[1]
    groups = HEADS // KVH
    xin = tokens[0].astype(jnp.float32)
    offset = lax.axis_index("blk") * rows
    query_idx = offset + jnp.arange(rows, dtype=jnp.int32)
    key_segs = segments[0]
    query_seg = lax.dynamic_slice_in_dim(key_segs, offset, rows)
    cosine, sine = rotation(positions[0])
    gain_one, gain_two, query_all, key_all, value_all, output_all = fetch_attention(
        gain_attn, gain_ffn, w_query, w_key, w_value, w_output
    )
    first_gain = gain_one.astype(jnp.float32)
    second_gain = gain_two.astype(jnp.float32)
    first_scale = rms_scale(xin)
    normed = (xin * first_scale * first_gain).astype(jnp.bfloat16)
    queries = rotate(product_t(normed, query_all), cosine, sine, HEADS, 1.0).astype(jnp.bfloat16)
    keys = rotate(product_t(normed, key_all), cosine, sine, KVH, 1.0).astype(jnp.bfloat16)
    values = product_t(normed, value_all).astype(jnp.bfloat16)
    keys_seen, values_seen = (
        lax.all_gather(keys, "blk", axis=0, tiled=True),
        lax.all_gather(values, "blk", axis=0, tiled=True),
    )
    query_heads = queries.reshape(rows, KVH, groups, HD)
    mixed, lse = attend(
        query_heads, key_blocks(keys_seen, values_seen, key_segs), query_seg, query_idx
    )
    attended = mixed.reshape(rows, HEADS * HD).astype(jnp.bfloat16)
    middle = xin + product_t(attended, output_all)
    second_scale = rms_scale(middle)
    normed_two = (middle * second_scale * second_gain).astype(jnp.bfloat16)
    gate_rows, up_rows, down_rows = fetch_ffn(w_gate, w_up, w_down)
    gate = product_t(normed_two, gate_rows)
    up = product_t(normed_two, up_rows)
    sigma = jax.nn.sigmoid(gate)
    activated = gate * sigma
    hidden = (activated * up).astype(jnp.bfloat16)
    branch = product(hidden, down_rows)
    result = (middle + branch).astype(jnp.bfloat16)
    grad_in = cotangent[0]
    gate_rows, up_rows, down_rows = fetch_ffn(w_gate, w_up, w_down)
    grad_hidden = product_t(grad_in, down_rows)
    grad_gate = (grad_hidden * up * sigma * (1.0 + gate * (1.0 - sigma))).astype(jnp.bfloat16)
    grad_up = (grad_hidden * activated).astype(jnp.bfloat16)
    gate_grad = product_tn(grad_gate, normed_two)
    up_grad = product_tn(grad_up, normed_two)
    down_grad = product_tn(hidden, grad_in)
    grad_normed_two = product(grad_gate, gate_rows) + product(grad_up, up_rows)
    gate_grad, up_grad, down_grad = (
        lax.psum_scatter(gate_grad, ("blk", "fsdp"), scatter_dimension=0, tiled=True),
        lax.psum_scatter(up_grad, ("blk", "fsdp"), scatter_dimension=0, tiled=True),
        lax.psum_scatter(down_grad, ("blk", "fsdp"), scatter_dimension=0, tiled=True),
    )
    grad_middle_norm, second_gain_grad = norm_back(
        grad_normed_two, middle, second_scale, second_gain
    )
    grad_middle = grad_in.astype(jnp.float32) + grad_middle_norm
    grad_branch = grad_middle.astype(jnp.bfloat16)
    output_grad = product_tn(grad_branch, attended)
    grad_attended = product(grad_branch, output_all).astype(jnp.bfloat16)
    grad_heads = grad_attended.reshape(rows, KVH, groups, HD)
    delta = jnp.transpose(jnp.sum(grad_heads.astype(jnp.float32) * mixed, axis=-1), (1, 2, 0))[
        ..., None
    ]
    grad_q, grad_keys, grad_values = cycle_back(
        query_heads, keys, values, key_segs, query_seg, query_idx, lse, grad_heads, delta
    )
    grad_q_pre = rotate(grad_q.reshape(rows, HEADS * HD), cosine, sine, HEADS, -1.0).astype(
        jnp.bfloat16
    )
    grad_k_pre = rotate(grad_keys, cosine, sine, KVH, -1.0).astype(jnp.bfloat16)
    grad_v = grad_values.astype(jnp.bfloat16)
    query_grad = product_tn(grad_q_pre, normed)
    key_grad = product_tn(grad_k_pre, normed)
    value_grad = product_tn(grad_v, normed)
    grad_normed = (
        product(grad_q_pre, query_all) + product(grad_k_pre, key_all) + product(grad_v, value_all)
    )
    grad_x_norm, first_gain_grad = norm_back(grad_normed, xin, first_scale, first_gain)
    grad_tokens = grad_middle + grad_x_norm
    first_gain_grad, second_gain_grad, query_grad, key_grad, value_grad, output_grad = (
        lax.psum_scatter(first_gain_grad, ("blk", "fsdp"), scatter_dimension=0, tiled=True),
        lax.psum_scatter(second_gain_grad, ("blk", "fsdp"), scatter_dimension=0, tiled=True),
        lax.psum_scatter(query_grad, ("blk", "fsdp"), scatter_dimension=0, tiled=True),
        lax.psum_scatter(key_grad, ("blk", "fsdp"), scatter_dimension=0, tiled=True),
        lax.psum_scatter(value_grad, ("blk", "fsdp"), scatter_dimension=0, tiled=True),
        lax.psum_scatter(output_grad, ("blk", "fsdp"), scatter_dimension=0, tiled=True),
    )
    return (
        result[None],
        grad_tokens[None],
        first_gain_grad,
        second_gain_grad,
        query_grad,
        key_grad,
        value_grad,
        output_grad,
        gate_grad,
        up_grad,
        down_grad,
    )


CHIPS = 8
TOK = 128
PAIR = 2 * HD
LANES = 128
VMEM_LIMIT = 32 << 20
LOG2E = 1.4426950408889634
RING = (0, 2, 4, 6, 7, 5, 3, 1)
SAME_CORE = [[2 * c + core for c in range(CHIPS)] for core in range(2)]


def ring_route(step):
    return [
        (RING[k] * 2 + core, RING[(k + step) % CHIPS] * 2 + core)
        for k in range(CHIPS)
        for core in range(2)
    ]


def ring_up(value):
    return lax.ppermute(value, "blk", ring_route(1))


def ring_down(value):
    return lax.ppermute(value, "blk", ring_route(-1))


def flipped(value, bit):
    return lax.ppermute(value, "blk", [(i, i ^ bit) for i in range(2 * CHIPS)])


def core_swap(value):
    return flipped(value, 1)


def x_swap(value):
    return lax.ppermute(value, "fsdp", [(0, 1), (1, 0)])


def tie(values, deps):
    deps = [d for d in deps if d is not None]
    if not deps:
        return tuple(values)
    return lax.optimization_barrier((tuple(values), tuple(deps)))[0]


def after(value, *deps):
    return tie((value,), deps)[0]


class Gather:
    def __init__(self, block):
        self.found = [None] * CHIPS
        self.found[0] = self.up = self.down = block

    def step(self, number, *deps):
        self.up, self.down = tie((self.up, self.down), deps)
        if number < CHIPS // 2:
            self.up = ring_up(self.up)
            self.down = ring_down(self.down)
            self.found[CHIPS - number] = self.up
            self.found[number] = self.down
        else:
            half = self.up.shape[0] // 2
            self.up = ring_up(self.up[:half])
            self.down = ring_down(self.down[half:])
            self.found[number] = (self.up, self.down)
        return self.up, self.down


class Scatter:
    def __init__(self, make):
        self.make = make
        self.up = self.down = None

    def step(self, number, *deps):
        up, down = tie(self.make(number, self.up, self.down), deps)
        self.up = ring_up(up)
        self.down = ring_down(down)
        return self.up, self.down


def dot_nt(left, right):
    return lax.dot_general(
        left, right, (((1,), (1,)), ((), ())), preferred_element_type=jnp.float32
    )


def dot_nn(left, right):
    return lax.dot_general(
        left, right, (((1,), (0,)), ((), ())), preferred_element_type=jnp.float32
    )


GROUPS = ((0, 1, 7), (2, 6), (3, 5), (4,))
ARRIVAL = tuple(j for group in GROUPS for j in group)


def whole(shape):
    return pl.BlockSpec(shape, lambda i: (0,) * len(shape), pipeline_mode=pl.Buffered(1))


def window(rows, nth, width):
    return pl.BlockSpec((rows, width), lambda i: (nth, 0), pipeline_mode=pl.Buffered(1))


def call(kernel, name, outs, ins, scratch=(), far=(), far_out=(), windows={}):
    shapes = []
    for n, (shape, dtype) in enumerate(outs):
        make = pltpu.HBM if n in far_out else jax.ShapeDtypeStruct
        shapes.append(make(shape, dtype))
    ins = list(ins)
    for n in far:
        ins[n] = pltpu.with_memory_space_constraint(ins[n], pltpu.HBM)
    return pl.pallas_call(
        kernel,
        grid=(1,),
        out_shape=tuple(shapes),
        in_specs=[
            window(*windows[n], value.shape[1]) if n in windows else whole(value.shape)
            for n, value in enumerate(ins)
        ],
        out_specs=tuple(whole(shape) for shape, _ in outs),
        scratch_shapes=scratch,
        compiler_params=pltpu.CompilerParams(vmem_limit_bytes=VMEM_LIMIT),
        cost_estimate=pl.CostEstimate(flops=0, bytes_accessed=0, transcendentals=0),
        name=name,
    )(*ins)


def dot_tn(left, right):
    return lax.dot_general(
        left, right, (((0,), (0,)), ((), ())), preferred_element_type=jnp.float32
    )


def own_place():
    index = lax.axis_index("blk")
    chip = lax.div(index, 2)
    half = lax.div(chip, 2)
    spot = jnp.where(lax.rem(chip, 2) == 0, half, CHIPS - 1 - half)
    return lax.rem(index, 2), lax.axis_index("fsdp"), chip, spot


def arriving_chip(nth, spot):
    at = lax.rem(spot + ARRIVAL[nth], CHIPS)
    return jnp.where(at < CHIPS // 2, 2 * at, 2 * CHIPS - 1 - 2 * at)


def arrival_of(chip, spot):
    away = lax.rem(RING.index(chip) - spot + CHIPS, CHIPS)
    late = jnp.where(away <= CHIPS // 2, 2 * away - 1, 2 * (CHIPS - away))
    return jnp.where(away == 0, 0, late)


def heads_kernel(own, near, far, across, out):
    nq = HD // 2
    nk = HD // 4
    half = LANES // 2
    own_core, own_side, _, _ = own_place()
    out[...] = jnp.zeros_like(out)
    for core in range(2):
        for side in range(2):

            @pl.when((own_core == core) & (own_side == side))
            def _():
                for piece, c, f in (
                    (own, core, side),
                    (near, core, 1 - side),
                    (far, 1 - core, side),
                    (across, 1 - core, 1 - side),
                ):
                    at = c * LANES + f * half
                    out[at : at + nq] = piece[:nq]
                    at = 2 * LANES + c * half + f * nk
                    out[at : at + nk] = piece[nq : nq + nk]
                    at = 3 * LANES + (2 * c + f) * nk
                    out[at : at + nk] = piece[nq + nk :]


def stack_kernel(*refs):
    out = refs[-1]
    at = 0
    for piece in refs[:-1]:
        out[at : at + piece.shape[0]] = piece[...]
        at += piece.shape[0]


def out_kernel(*refs):
    own, near, out = refs[:4], refs[4:8], refs[8]
    side = own_place()[1]
    rows = own[0].shape[0] // 2
    for n, j in enumerate(ARRIVAL):
        away = min(j, CHIPS - j)
        which = 3 if away in (0, CHIPS // 2) else away - 1
        here = slice(0, rows) if j in (0, 1, 2, 3) else slice(rows, 2 * rows)
        for source, f in ((own, side), (near, 1 - side)):
            at = pl.multiple_of((2 * n + f) * rows, rows)
            out[pl.ds(at, rows), :] = source[which][here, :]


def hidden_kernel(*refs):
    gate_up, down = refs[-2:]
    count = refs[0].shape[0]
    for n in range(4):
        gate, up, out = refs[3 * n : 3 * n + 3]
        start = (n // 2) * 4 * count + (n % 2) * count
        gate_up[start : start + count] = gate[...]
        gate_up[start + 2 * count : start + 3 * count] = up[...]
        down[n * count : (n + 1) * count] = out[...]


def project_kernel(*refs):
    blocks = refs[: CHIPS + 1]
    gain, weight, cosine, sine, normed_out, query_out, kv_out = refs[CHIPS + 1 :]
    for j in range(CHIPS):
        if j < CHIPS - 1:
            values = blocks[j][-TOK:].astype(jnp.float32)
        else:
            late = blocks[CHIPS][...].astype(jnp.float32)
            values = blocks[j][-(TOK - late.shape[0]) :].astype(jnp.float32)
            values = jnp.concatenate([values, late], axis=0)
        scale = lax.rsqrt(jnp.mean(values * values, axis=-1, keepdims=True) + EPS)
        normed_out[j * TOK : (j + 1) * TOK, :] = (values * scale * gain[...]).astype(jnp.bfloat16)
    pre = dot_nt(normed_out[...], weight[...])
    for head in range(3):
        part = pre[:, head * LANES : (head + 1) * LANES]
        turned = part * cosine[...] + pltpu.roll(part, LANES // 2, 1) * sine[...]
        if head < 2:
            query_out[:, head * LANES : (head + 1) * LANES] = turned.astype(jnp.bfloat16)
        else:
            kv_out[:, :LANES] = turned.astype(jnp.bfloat16)
    kv_out[:, LANES:] = pre[:, 3 * LANES :].astype(jnp.bfloat16)


def project(blocks, *arrays):
    rows = CHIPS * TOK
    width = blocks[0].shape[1]
    low = jnp.bfloat16
    assert len(blocks) == CHIPS + 1
    return call(
        project_kernel,
        "project",
        (((rows, width), low), ((rows, 2 * LANES), low), ((rows, 2 * LANES), low)),
        (*blocks, *arrays),
        far=range(CHIPS + 1),
        far_out=(0,),
    )


def key_index(core, count):
    row = lax.broadcasted_iota(jnp.int32, (count, 1), 0)
    return (row // TOK) * (2 * TOK) + core * TOK + row % TOK


def query_index(core, chip):
    lane = lax.broadcasted_iota(jnp.int32, (1, 2 * TOK), 1)
    return lane % TOK + (2 * chip + core) * TOK


def sequence_starts(segments):
    numbers = segments[...]
    starts = []
    for number in range(1, 4):
        below = (numbers < number).astype(jnp.float32)
        total = jnp.sum(jnp.sum(below, axis=1, keepdims=True), axis=0, keepdims=True)
        starts.append(total.astype(jnp.int32))
    return starts


def first_index(starts, at):
    first = jnp.zeros_like(at)
    for start in starts:
        first = jnp.where(at >= start, start, first)
    return first


def both_heads(ref, rows):
    return jnp.concatenate([ref[rows, :LANES], ref[rows, LANES:]], axis=0)


def attend_kernel(
    segments, query_in, own_in, peer_in, attended, mixed, lse, query, own, peer
):
    core, _, _, spot = own_place()
    starts = sequence_starts(segments)
    factor = HD ** (-0.5) * LOG2E
    for source, target in ((query_in, query), (own_in, own), (peer_in, peer)):
        for chip in range(CHIPS):
            rows = pl.ds(pl.multiple_of(arrival_of(chip, spot) * TOK, TOK), TOK)
            target[chip * TOK : (chip + 1) * TOK, :] = source[rows, :]
    sides = ((own, core), (peer, 1 - core))
    values_t = [jnp.transpose(kv[:, LANES:]) for kv, _ in sides]
    for chip in range(CHIPS):
        count = (chip + 1) * TOK
        rows = slice(chip * TOK, count)
        queries = both_heads(query, rows)
        at = query_index(core, chip)
        first = first_index(starts, at)
        scores = []
        for kv, side in sides:
            raw = dot_nt(kv[:count, :LANES], queries) * factor
            keys_at = key_index(side, count)
            scores.append(jnp.where((keys_at <= at) & (keys_at >= first), raw, NEG))
        top = jnp.maximum(
            jnp.max(scores[0], axis=0, keepdims=True), jnp.max(scores[1], axis=0, keepdims=True)
        )
        weights = [jnp.exp2(part - top) for part in scores]
        total = jnp.sum(weights[0], axis=0, keepdims=True) + jnp.sum(
            weights[1], axis=0, keepdims=True
        )
        mix = dot_nn(values_t[0][:, :count], weights[0].astype(jnp.bfloat16)) + dot_nn(
            values_t[1][:, :count], weights[1].astype(jnp.bfloat16)
        )
        mix = mix / total
        mixed[chip] = mix
        lse[chip] = top + jnp.log2(total)
        attended[chip, :HD] = mix[:HD, :TOK].astype(jnp.bfloat16)
        attended[chip, HD:] = mix[:HD, TOK:].astype(jnp.bfloat16)


def attend_heads(segments, query, own, peer):
    tokens = CHIPS * TOK
    low = jnp.bfloat16
    return call(
        attend_kernel,
        "attend",
        (
            ((CHIPS, PAIR, TOK), low),
            ((CHIPS, LANES, 2 * TOK), jnp.float32),
            ((CHIPS, 1, 2 * TOK), jnp.float32),
            ((tokens, 2 * LANES), low),
            ((tokens, 2 * LANES), low),
            ((tokens, 2 * LANES), low),
        ),
        (segments, query, own, peer),
        far_out=(1, 2, 3, 4, 5),
    )


def attend_back_kernel(
    segments, query, own, peer, grad_out, mixed, lse, cosine, sine,
    grad_query, own_out, peer_out, grad_own, grad_peer,
):
    core, _, _, spot = own_place()
    starts = sequence_starts(segments)
    scale = HD ** (-0.5)
    factor = scale * LOG2E
    sides = ((own, core, grad_own), (peer, 1 - core, grad_peer))
    keys_t = [jnp.transpose(kv[:, :LANES]) for kv, _, _ in sides]
    grad_own[...] = jnp.zeros_like(grad_own)
    grad_peer[...] = jnp.zeros_like(grad_peer)
    pad = jnp.zeros((LANES - HD, 2 * TOK), jnp.bfloat16)
    for chip in range(CHIPS):
        count = (chip + 1) * TOK
        rows = slice(chip * TOK, count)
        kept = pl.ds(pl.multiple_of(arrival_of(chip, spot) * TOK, TOK), TOK)
        queries = both_heads(query, rows)
        grads = jnp.concatenate(
            [
                jnp.concatenate([grad_out[chip, :HD], grad_out[chip, HD:]], axis=1),
                pad,
            ],
            axis=0,
        )
        delta = jnp.sum(grads.astype(jnp.float32) * mixed[chip], axis=0, keepdims=True)
        at = query_index(core, chip)
        first = first_index(starts, at)
        level = lse[chip]
        grad_q = jnp.zeros((LANES, 2 * TOK), jnp.float32)
        for (kv, side, grad_kv), key_t in zip(sides, keys_t):
            raw = dot_nt(kv[:count, :LANES], queries) * factor
            keys_at = key_index(side, count)
            allowed = (keys_at <= at) & (keys_at >= first)
            probs = jnp.exp2(jnp.where(allowed, raw - level, NEG))
            grad_probs = dot_nn(kv[:count, LANES:], grads)
            grad_scores = (probs * (grad_probs - delta)).astype(jnp.bfloat16)
            grad_kv[:count, LANES:] += dot_nt(probs.astype(jnp.bfloat16), grads)
            grad_kv[:count, :LANES] += dot_nn(grad_scores, queries)
            grad_q += dot_nn(key_t[:, :count], grad_scores)
        grad_q = jnp.transpose(grad_q) * scale
        cos = cosine[kept, :]
        sin = sine[kept, :]
        for head in range(2):
            part = grad_q[head * TOK : (head + 1) * TOK]
            turned = part * cos - pltpu.roll(part, LANES // 2, 1) * sin
            grad_query[kept, head * LANES : (head + 1) * LANES] = turned.astype(jnp.bfloat16)
    for chip in range(CHIPS):
        rows = slice(chip * TOK, (chip + 1) * TOK)
        kept = pl.ds(pl.multiple_of(arrival_of(chip, spot) * TOK, TOK), TOK)
        for grad_kv, out in ((grad_own, own_out), (grad_peer, peer_out)):
            out[kept, :LANES] = grad_kv[rows, :LANES] * scale
            out[kept, LANES:] = grad_kv[rows, LANES:]


def attend_back(segments, *arrays):
    tokens = CHIPS * TOK
    full = jnp.float32
    return call(
        attend_back_kernel,
        "attend_back",
        (
            ((tokens, 2 * LANES), jnp.bfloat16),
            ((tokens, 2 * LANES), full),
            ((tokens, 2 * LANES), full),
        ),
        (segments, *arrays),
        scratch=[pltpu.VMEM((tokens, 2 * LANES), full)] * 2,
        far=(1, 2, 3, 5, 6, 7, 8),
    )


def join_kernel(heads, *refs):
    weights = refs[:2]
    block, gain, middle_out, normed_out, attended_out, weight_out, held = refs[2:]
    core, _, _, spot = own_place()
    size = weights[0].shape[0] // CHIPS
    for n in range(CHIPS):
        for piece, side in zip(weights, (core, 1 - core)):
            at = pl.multiple_of((2 * arriving_chip(n, spot) + side) * size, size)
            weight_out[pl.ds(at, size), :] = piece[n * size : (n + 1) * size, :]
    for chip in range(CHIPS):
        held[chip * PAIR : (chip + 1) * PAIR, :] = heads[chip]
    attended_out[...] = jnp.transpose(held[...])
    middle = block[...].astype(jnp.float32) + dot_nt(attended_out[...], weight_out[...])
    middle_out[...] = middle
    scale = lax.rsqrt(jnp.mean(middle * middle, axis=-1, keepdims=True) + EPS)
    normed_out[...] = (middle * scale * gain[...]).astype(jnp.bfloat16)


def ffn_kernel(number, *refs):
    blocks = refs[:number]
    outers = refs[number : 2 * number]
    gate_up, down_rows = refs[2 * number : 2 * number + 2]
    rows, outer_rows, hidden, grad_gu = refs[2 * number + 2 : 2 * number + 6]
    wide = hidden.shape[1] // 2
    size = rows.shape[0] // number
    for n in range(number):
        rows[n * size : (n + 1) * size, :] = blocks[n][...]
        outer_rows[n * size : (n + 1) * size, :] = outers[n][...]
    grads = dot_nt(outer_rows[...], down_rows[...])
    pre = dot_nt(rows[...], gate_up[...])
    for part in range(2):
        at = part * 2 * wide
        gate = pre[:, at : at + wide]
        up = pre[:, at + wide : at + 2 * wide]
        back = grads[:, part * wide : (part + 1) * wide]
        sigma = 1.0 / (1.0 + jnp.exp(-gate))
        active = gate * sigma
        hidden[:, part * wide : (part + 1) * wide] = (active * up).astype(jnp.bfloat16)
        slope = back * up * sigma * (1.0 + gate * (1.0 - sigma))
        grad_gu[:, at : at + wide] = slope.astype(jnp.bfloat16)
        grad_gu[:, at + wide : at + 2 * wide] = (back * active).astype(jnp.bfloat16)
    outs = refs[2 * number + 6 :]
    back = dot_nn(grad_gu[...], gate_up[...])
    if len(outs) == 1:
        outs[0][...] = back
    else:
        outs[0][...] = back[: TOK // 2].astype(jnp.bfloat16)
        outs[1][...] = back[TOK // 2 :].astype(jnp.bfloat16)


def ffn(blocks, outers, gate_up, down):
    number = len(blocks)
    rows = number * blocks[0].shape[0]
    width = blocks[0].shape[1]
    units = down.shape[0]
    low = jnp.bfloat16
    if rows > TOK:
        terms = [((rows, width), jnp.float32)]
    else:
        terms = [((TOK // 2, width), low)] * 2
    return call(
        functools.partial(ffn_kernel, number),
        "ffn",
        [((rows, width), low)] * 2 + [((rows, units), low), ((rows, 2 * units), low)] + terms,
        (*blocks, *outers, gate_up, down),
    )


def add_terms(up_term, down_term, up, down, up_out, down_out):
    size = up.shape[0]
    rest = up_out.shape[0] - size
    low = jnp.bfloat16
    full = jnp.float32
    up_out[:size] = (up_term[:size] + up.astype(full)).astype(low)
    down_out[rest:] = (down_term[rest:] + down.astype(full)).astype(low)
    if rest:
        up_out[size:] = up_term[size:].astype(low)
        down_out[:rest] = down_term[:rest].astype(low)


def add_kernel(up_term, down_term, up, down, up_out, down_out):
    add_terms(up_term, down_term, up[...], down[...], up_out, down_out)


def leaving(width, rows=TOK):
    return [((rows, width), jnp.bfloat16)] * 2


STEP_ROWS = {1: 7 * TOK, 2: 5 * TOK, 3: 3 * TOK, 4: TOK}


def branch_kernel(hidden, down_rows, *outs):
    found = dot_nn(hidden[...], down_rows[...])
    at = 0
    for out in outs[:-2]:
        out[...] = found[at : at + out.shape[0]]
        at += out.shape[0]
    outs[-2][...] = found[at : at + TOK // 2].astype(jnp.bfloat16)
    outs[-1][...] = found[at + TOK // 2 :].astype(jnp.bfloat16)


def result_kernel(terms, up, down, middle, out):
    full = jnp.float32
    branch = terms[...] + (up[...].astype(full) + down[...].astype(full))
    out[...] = (middle[...] + branch).astype(jnp.bfloat16)


def grads_kernel(number, *refs):
    rows_in, outer_in, hidden_in, grads_in = (refs[n * number : (n + 1) * number] for n in range(4))
    keep_gu, keep_down, send_gu, send_down, hidden, rows, grads = refs[4 * number :]
    at = 0
    for block, hid, grad in zip(rows_in, hidden_in, grads_in):
        here = slice(at, at + block.shape[0])
        rows[here, :] = block[...]
        hidden[here, :] = hid[...]
        grads[here, :] = grad[...]
        at += block.shape[0]
    half = keep_gu.shape[0]
    send_gu[...] = dot_tn(grads[:, half:], rows[...])
    keep_gu[...] = dot_tn(grads[:, :half], rows[...])
    at = 0
    for block in outer_in:
        rows[at : at + block.shape[0], :] = block[...]
        at += block.shape[0]
    half = keep_down.shape[0]
    send_down[...] = dot_tn(hidden[:, half:], rows[...])
    keep_down[...] = dot_tn(hidden[:, :half], rows[...])


def owners_kernel(keep_gu, keep_down, other_gu, other_down, *outs):
    count = outs[0].shape[0]
    for n, (value, other, at) in enumerate(
        ((keep_gu, other_gu, 0), (keep_gu, other_gu, 2 * count), (keep_down, other_down, 0))
    ):
        near = at + count
        outs[n][...] = value[at:near] + other[at:near]
        given = value[near : near + count] + other[near : near + count]
        outs[3 + n][...] = given.astype(jnp.bfloat16)


def turn_kernel(*refs):
    own, up, down, middle_ref, outer, gain, weight, middle_out, branch_out, heads, gain_out = refs
    grad = own[...] + (up[...].astype(jnp.float32) + down[...].astype(jnp.float32))
    middle = middle_ref[...]
    scale = lax.rsqrt(jnp.mean(middle * middle, axis=-1, keepdims=True) + EPS)
    weighted = grad * gain[...]
    inner = jnp.mean(weighted * middle, axis=-1, keepdims=True)
    gain_out[...] = jnp.sum(grad * middle * scale, axis=0, keepdims=True)
    total = outer[...].astype(jnp.float32) + (scale * weighted - middle * (scale**3 * inner))
    middle_out[...] = total
    branch = total.astype(jnp.bfloat16)
    branch_out[...] = branch
    back = jnp.transpose(dot_nn(branch, weight[...]).astype(jnp.bfloat16))
    for chip in range(CHIPS):
        heads[chip] = back[chip * PAIR : (chip + 1) * PAIR]


def outer_kernel(branch, attended, keep, give, held):
    held[...] = dot_tn(branch[...], attended[...])
    core = own_place()[0]
    size = keep.shape[1]
    for chip in range(CHIPS):
        at = pl.multiple_of((2 * chip + core) * size, size)
        keep[chip] = held[pl.ds(at, size), :].astype(jnp.bfloat16)
        at = pl.multiple_of((2 * chip + 1 - core) * size, size)
        give[chip] = held[pl.ds(at, size), :].astype(jnp.bfloat16)


def settle_kernel(keep, other, total):
    spot = own_place()[3]
    rows = keep.shape[1]
    for n in range(CHIPS):
        chip = arriving_chip(n, spot)
        found = keep[chip].astype(jnp.float32) + other[chip].astype(jnp.float32)
        total[n * rows : (n + 1) * rows] = found.astype(jnp.bfloat16)


def first_two(left, right, second, up_out, down_out):
    begin = STEP_ROWS[1]
    terms = dot_nn(left[begin : begin + TOK], right[...]).astype(jnp.bfloat16)
    rows = second.shape[0] // CHIPS
    begin = (CHIPS - 1) * rows
    half = TOK // 2
    up_out[:half] = terms[:half]
    down_out[:half] = terms[half:]
    up_out[half:] = second[begin : begin + rows // 2]
    down_out[half:] = second[begin + rows // 2 : begin + rows]


def both_kernel(
    up_left, down_left, right, up_second, down_second, up, down, up_out, down_out
):
    rows = up_second.shape[0]
    full = jnp.float32
    cut = up.shape[0] * TOK // (TOK + rows)
    terms = dot_nn(jnp.concatenate([up_left[...], down_left[...]], axis=0), right[...])
    add_terms(
        terms[:TOK], terms[TOK:], up[:cut], down[:cut], up_out.at[:TOK], down_out.at[:TOK]
    )
    add_terms(
        up_second[...].astype(full),
        down_second[...].astype(full),
        up[cut:],
        down[cut:],
        up_out.at[TOK:],
        down_out.at[TOK:],
    )


def spread_kernel(query, own, other, cosine, sine, weight, second, joined, up_out, down_out):
    joined[:, : 2 * LANES] = query[...]
    total = own[...] + other[...]
    part = total[:, :LANES]
    turned = part * cosine[...] - pltpu.roll(part, LANES // 2, 1) * sine[...]
    joined[:, 2 * LANES : 3 * LANES] = turned.astype(jnp.bfloat16)
    joined[:, 3 * LANES :] = total[:, LANES:].astype(jnp.bfloat16)
    first_two(joined, weight, second, up_out, down_out)


def heads_grad_kernel(*refs):
    own_core, own_side, _, _ = own_place()
    joined, weight, gain, second, normed, mine, send, gains, grad = refs
    grad[...] = dot_tn(joined[...], normed[...])
    first = jnp.sum(grad[...] * weight[...].astype(jnp.float32), axis=0, keepdims=True) / gain[...]
    nq = HD // 2
    nk = HD // 4
    half = LANES // 2
    gains[:1] = first
    gains[1:] = second[...]
    for core in range(2):
        for side in range(2):

            @pl.when((own_core == core) & (own_side == side))
            def _():
                for c in range(2):
                    for f in range(2):
                        out = mine if c == core else send
                        which = 0 if f == side else 1
                        at = c * LANES + f * half
                        out[which, :nq] = grad[at : at + nq]
                        at = 2 * LANES + c * half + f * nk
                        out[which, nq : nq + nk] = grad[at : at + nk]
                        at = 3 * LANES + (2 * c + f) * nk
                        out[which, nq + nk :] = grad[at : at + nk]


def owned_kernel(second, up, down, keep, give):
    side = own_place()[1]
    rows = keep.shape[0]
    full = jnp.float32
    total = second[...].astype(full) + (up[TOK:].astype(full) + down[TOK:].astype(full))
    keep[...] = jnp.where(side == 0, total[:rows], total[rows:])
    give[...] = jnp.where(side == 0, total[rows:], total[:rows]).astype(jnp.bfloat16)


def last_kernel(joined, weight, up, down, block, middle, gain, out):
    grad = dot_nn(joined[...], weight[...])
    grad = grad + (up[:TOK].astype(jnp.float32) + down[:TOK].astype(jnp.float32))
    values = block[...].astype(jnp.float32)
    scale = lax.rsqrt(jnp.mean(values * values, axis=-1, keepdims=True) + EPS)
    weighted = grad * gain[...]
    inner = jnp.mean(weighted * values, axis=-1, keepdims=True)
    out[...] = middle[...] + (scale * weighted - values * (scale**3 * inner))


def plane_shards(
    tokens,
    cotangent,
    segments,
    positions,
    gain_attn,
    gain_ffn,
    w_query,
    w_key,
    w_value,
    w_output,
    w_gate,
    w_up,
    w_down,
):
    full = jnp.float32
    low = jnp.bfloat16
    block = tokens[0]
    outer = cotangent[0]
    width = block.shape[1]
    index = lax.axis_index("blk")
    side = lax.axis_index("fsdp")
    core = index % 2
    chip = index // 2
    spot = jnp.where(chip % 2 == 0, chip // 2, CHIPS - 1 - chip // 2)

    segs = segments[0]
    numbers = segs.reshape(2 * CHIPS, TOK)
    starts = [jnp.sum((segs < number).astype(jnp.int32)) for number in range(1, 4)]
    row = lax.broadcasted_iota(jnp.int32, (CHIPS * TOK, LANES), 0)
    nth = row >> 7
    away = jnp.where((nth & 1) == 1, (nth + 1) >> 1, CHIPS - (nth >> 1))
    at = (spot + away) & (CHIPS - 1)
    token = jnp.where(at < CHIPS // 2, 2 * at, 2 * CHIPS - 1 - 2 * at) * (2 * TOK)
    token = token + core * TOK + (row & (TOK - 1))
    first = jnp.zeros_like(token)
    for start in starts:
        first = jnp.where(token >= start, start, first)
    half = HD // 2
    freqs = ROPE_BASE ** (-(jnp.arange(half, dtype=full) * 2.0 / HD))
    spare = jnp.zeros((LANES // 2 - half,), full)
    both = jnp.concatenate([freqs, spare, freqs, spare])
    angles = (token - first).astype(full) * both[None, :]
    sign = jnp.where(jnp.arange(LANES) < LANES // 2, -1.0, 1.0).astype(full)
    cosine = jnp.cos(angles)
    sine = jnp.sin(angles) * sign[None, :]

    ended = [()]

    def held(value):
        return after(value, *ended[-1])

    def close(*results):
        flat = []
        for result in results:
            flat += list(result) if isinstance(result, (list, tuple)) else [result]
        ended.append(tuple(flat))

    def to_chips(value):
        return lax.all_to_all(
            value, "blk", split_axis=0, concat_axis=0, axis_index_groups=SAME_CORE, tiled=True
        )

    nq = w_query.shape[0]
    nk = w_key.shape[0]
    count = w_gate.shape[0]
    units = 2 * count

    def wider(vector, bit):
        other = flipped(vector, bit) if bit else x_swap(vector)
        return jnp.where(
            ((index & bit) if bit else side) == 0,
            jnp.concatenate([vector, other], axis=1),
            jnp.concatenate([other, vector], axis=1),
        )

    both = call(
        stack_kernel, "stack_tokens", (((nq + TOK, width), low),), (w_output, block), far=(0, 1)
    )[0]
    tokens_ring = Gather(both)
    x1 = tokens_ring.step(1)
    gains = wider(wider(jnp.stack([gain_attn, gain_ffn]), 0), 1)
    close(x1, gains, cosine, sine)

    x2 = tokens_ring.step(2, *ended[-1])
    packed = call(
        stack_kernel,
        "stack_heads",
        (((nq + 2 * nk, width), low),),
        (w_query, w_key, held(w_value)),
        far=range(3),
    )[0]
    near = x_swap(packed)
    far = core_swap(packed)
    gains = wider(held(gains), 2)
    close(x2, near, far, gains)

    def out_pair(first, second):
        return call(
            stack_kernel,
            "stack_pair",
            (((2 * nq, width), low),),
            (first, second),
            far=(0, 1),
            windows={0: (nq, 0), 1: (nq, 0)},
        )[0]

    found = tokens_ring.found
    x3 = tokens_ring.step(3, *ended[-1])
    across = core_swap(held(near))
    gains = wider(held(gains), 4)
    own_outs = [out_pair(held(found[1]), found[7])]
    near_outs = [x_swap(own_outs[0])]
    close(x3, across, gains, near_outs)

    x4 = tokens_ring.step(4, *ended[-1])
    w_heads = call(
        heads_kernel,
        "head_rows",
        (((4 * LANES, width), low),),
        (packed, near, far, held(across)),
        far=range(4),
    )[0]
    own_outs.append(out_pair(held(found[2]), found[6]))
    near_outs.append(x_swap(own_outs[1]))
    gains = wider(held(gains), 8).astype(full)
    gain_one = gains[:1]
    gain_two = gains[1:]
    close(x4, gains, w_heads, near_outs[1])

    outer_ring = Gather(held(outer))
    e1 = outer_ring.step(1)
    blocks = [found[j] for j in ARRIVAL[:-1]] + list(found[4])
    normed, query, kv = project(
        [held(blocks[0])] + blocks[1:], gain_one, w_heads, cosine, sine
    )
    own_outs.append(out_pair(held(found[3]), found[5]))
    near_outs.append(x_swap(own_outs[2]))
    own_outs.append(out_pair(held(found[0]), found[4][0]))
    close(e1, near_outs[2], kv, own_outs[3])

    kv_peer = core_swap(held(kv))
    close(kv_peer)

    e2 = outer_ring.step(2, *ended[-1])
    near_outs.append(x_swap(held(own_outs[3])))
    heads, mixed, lse, query_all, kv_all, kv_peer_all = attend_heads(
        numbers, query, kv, held(kv_peer)
    )
    close(e2, near_outs[3], heads)

    swapped = to_chips(held(heads))
    near_gate = x_swap(held(w_gate))
    out_rows = call(
        out_kernel,
        "stack_out",
        (((CHIPS * 2 * nq, width), low),),
        own_outs + near_outs[:3] + [held(near_outs[3])],
        far=range(8),
    )[0]
    far_ffn = [core_swap(held(w_gate)), core_swap(held(w_up)), core_swap(held(w_down))]
    close(swapped, near_gate, out_rows, far_ffn)

    e3 = outer_ring.step(3, *ended[-1])
    out_rows_peer = core_swap(held(out_rows))
    across_ffn = [core_swap(held(near_gate))]
    near_up = x_swap(held(w_up))
    middle, normed_two, attended, w_out = call(
        join_kernel,
        "join",
        (
            ((TOK, width), full),
            ((TOK, width), low),
            ((TOK, width), low),
            ((width, width), low),
        ),
        (held(swapped), out_rows, out_rows_peer, block, gain_two),
        scratch=[pltpu.VMEM((width, TOK), low)],
        far=(3,),
        far_out=(0, 2, 3),
    )
    close(e3, normed_two, across_ffn, near_up)

    normed_ring = Gather(held(normed_two))
    fed = []

    def ffn_group(n):
        group = GROUPS[n]
        if len(group) > 1:
            blocks, outers = ([ring.found[j] for j in group] for ring in (normed_ring, outer_ring))
        else:
            blocks, outers = (list(ring.found[group[0]]) for ring in (normed_ring, outer_ring))
        blocks[0] = held(blocks[0])
        fed.append(ffn(blocks, outers, w_gu, w_dn))
        return fed[-1][3]

    h1 = normed_ring.step(1)
    e4 = outer_ring.step(4, *ended[-1])
    near_down = x_swap(held(w_down))
    close(h1, e4, near_down)

    h2 = normed_ring.step(2, *ended[-1])
    across_ffn += [core_swap(held(near_up)), core_swap(held(near_down))]
    w_gu, w_dn = call(
        hidden_kernel,
        "hidden_rows",
        (((4 * units, width), low), ((2 * units, width), low)),
        (w_gate, w_up, w_down, near_gate, near_up, near_down, *far_ffn, *across_ffn),
        far=range(12),
    )
    close(h2, w_gu)

    h3 = normed_ring.step(3, *ended[-1])
    close(h3, ffn_group(0), ffn_group(1))

    h4 = normed_ring.step(4, *ended[-1])
    close(h4, ffn_group(2))

    ffn_group(3)

    def stored(terms, name, far=()):
        def make(number, up, down):
            if number == 1:
                return terms[3:]
            begin = 1 if number == 4 else 0
            part = terms[4 - number]
            return call(
                add_kernel,
                name,
                leaving(width),
                (part, part, up, down),
                far=far,
                windows={0: (TOK, begin), 1: (TOK, begin + 1)},
            )

        return make

    back_ring = Scatter(stored([part[4] for part in fed[:3]] + list(fed[3][4:]), "back_add"))
    close(back_ring.step(1))

    d2 = back_ring.step(2, *ended[-1])
    arrays = [part[n] for n in range(4) for part in fed]
    arrays[0] = held(arrays[0])
    sums = call(
        functools.partial(grads_kernel, len(GROUPS)),
        "ffn_grads",
        [((2 * units, width), full), ((units, width), full)] * 2 + [((CHIPS * TOK, 2 * units), low)],
        arrays,
        scratch=[
            pltpu.VMEM((CHIPS * TOK, width), low),
            pltpu.VMEM((CHIPS * TOK, 4 * units), low),
        ],
        far_out=(4,),
    )
    close(d2, sums[2])

    d3 = back_ring.step(3, *ended[-1])
    others = [core_swap(held(value)) for value in sums[2:4]]
    branch = call(
        branch_kernel,
        "branch",
        [((len(group) * TOK, width), full) for group in GROUPS[:3]] + leaving(width, TOK // 2),
        (held(sums[4]), w_dn),
        far_out=(0, 1, 2),
    )
    close(d3, others, branch[-1])

    d4 = back_ring.step(4, *ended[-1])
    kept = call(
        owners_kernel,
        "ffn_owners",
        [((count, width), full)] * 3 + [((count, width), low)] * 3,
        (*sums[:2], held(others[0]), others[1]),
        far_out=(0, 1, 2),
    )
    near_grads = [x_swap(kept[3])]
    close(d4, near_grads)

    branch_ring = Scatter(stored(branch, "branch_add", (0, 1)))
    z1 = branch_ring.step(1, *ended[-1])
    grad_middle, grad_branch, grad_heads, second_gain_grad = call(
        turn_kernel,
        "turn",
        (
            ((TOK, width), full),
            ((TOK, width), low),
            ((CHIPS, PAIR, TOK), low),
            ((1, width), full),
        ),
        (fed[0][4], *d4, middle, outer, gain_two, w_out),
        far=(3, 4, 6),
        far_out=(0,),
        windows={0: (TOK, 0)},
    )
    close(z1, grad_heads)

    grad_heads = to_chips(held(grad_heads))
    z2 = branch_ring.step(2, *ended[-1])
    near_grads.append(x_swap(held(kept[4])))
    keep, give = call(
        outer_kernel,
        "outer",
        (((CHIPS, 2 * nq, width), low), ((CHIPS, 2 * nq, width), low)),
        (held(grad_branch), attended),
        far=(1,),
        far_out=(0,),
        scratch=[pltpu.VMEM((width, width), full)],
    )
    close(grad_heads, z2, near_grads[1], give)

    z3 = branch_ring.step(3, *ended[-1])
    other = core_swap(held(give))
    grad_query, grad_own, grad_peer = attend_back(
        numbers, query_all, kv_all, kv_peer_all, held(grad_heads), mixed, lse, cosine, sine
    )
    close(z3, other, grad_query)

    z4 = branch_ring.step(4, *ended[-1])
    second = call(
        settle_kernel,
        "settle",
        (((CHIPS * 2 * nq, width), low),),
        (keep, held(other)),
        far=(0,),
    )[0]
    joined, *leave = call(
        spread_kernel,
        "spread",
        [((CHIPS * TOK, 4 * LANES), low)] + leaving(width, TOK // 2 + nq),
        (grad_query, grad_own, core_swap(held(grad_peer)), cosine, sine, w_heads, second),
        far=(3, 4, 5),
    )
    close(z4, leave)

    def last_terms(number, up, down):
        if number == 1:
            return leave
        begin = STEP_ROWS[number] // TOK
        return call(
            both_kernel,
            "last_terms",
            leaving(width, TOK + 2 * nq),
            (joined, joined, w_heads, second, second, up, down),
            far=(0, 1, 2, 3, 4),
            windows={
                0: (TOK, begin),
                1: (TOK, begin + 1),
                3: (2 * nq, begin),
                4: (2 * nq, begin + 1),
            },
        )

    last_ring = Scatter(last_terms)
    t1 = last_ring.step(1, *ended[-1])
    mine, send, gain_grads = call(
        heads_grad_kernel,
        "heads_grad",
        (((2, HD, width), full), ((2, HD, width), full), ((2, width), full)),
        (held(joined), w_heads, gain_one, second_gain_grad, normed),
        scratch=[pltpu.VMEM((4 * LANES, width), full)],
        far=range(1, 5),
    )
    near_grads.append(x_swap(held(kept[5])))
    close(t1, send, gain_grads, near_grads[2])

    t2 = last_ring.step(2, *ended[-1])
    other = core_swap(held(send))
    result = call(
        result_kernel,
        "result",
        (((TOK, width), low),),
        (branch[0], held(z4[0]), z4[1], middle),
        far=(0, 3),
        far_out=(0,),
        windows={0: (TOK, 0)},
    )[0]
    gain_grads = gain_grads + flipped(held(gain_grads), 2)
    close(t2, other, result, gain_grads)

    t3 = last_ring.step(3, *ended[-1])
    mine = mine + held(other)
    heads_grad = mine[0] + x_swap(mine[1].astype(low)).astype(full)
    gain_grads = gain_grads + flipped(held(gain_grads), 4)
    close(t3, heads_grad, gain_grads)

    t4 = last_ring.step(4, *ended[-1])
    gain_grads = gain_grads + flipped(held(gain_grads), 8)
    ffn_grad = [own + held(other).astype(full) for own, other in zip(kept[:3], near_grads)]
    close(t4, gain_grads, ffn_grad)

    keep, give = call(
        owned_kernel,
        "owned",
        (((nq, width), full), ((nq, width), low)),
        (second, held(t4[0]), t4[1]),
        far=(0,),
        windows={0: (2 * nq, 0)},
    )
    output_grad = keep + x_swap(give).astype(full)
    gain_grads = gain_grads + core_swap(held(gain_grads))
    gain_grads = gain_grads + x_swap(gain_grads)
    gain_grads = lax.dynamic_slice_in_dim(gain_grads, (2 * index + side) * nq, nq, 1)
    grad_tokens = call(
        last_kernel,
        "last",
        (((TOK, width), full),),
        (joined, w_heads, held(t4[0]), t4[1], block, grad_middle, gain_one),
        far=(0, 1, 4, 5),
        far_out=(0,),
        windows={0: (TOK, 0)},
    )[0]
    return (
        result[None],
        grad_tokens[None],
        gain_grads[0],
        gain_grads[1],
        heads_grad[:nq],
        heads_grad[nq : nq + nk],
        heads_grad[nq + nk :],
        output_grad,
        ffn_grad[0],
        ffn_grad[1],
        ffn_grad[2],
    )


def by_plane(mesh):
    return dict(mesh.shape) == {"blk": 2 * CHIPS, "fsdp": 2} and KVH == CHIPS


def solution(mesh):
    in_specs = (
        P("fsdp", "blk", None),
        P("fsdp", "blk", None),
        P("fsdp", None),
        P("fsdp", "blk"),
        P(("blk", "fsdp")),
        P(("blk", "fsdp")),
        P(("blk", "fsdp"), None),
        P(("blk", "fsdp"), None),
        P(("blk", "fsdp"), None),
        P(("blk", "fsdp"), None),
        P(("blk", "fsdp"), None),
        P(("blk", "fsdp"), None),
        P(("blk", "fsdp"), None),
    )
    out_specs = (
        P("fsdp", "blk", None),
        P("fsdp", "blk", None),
        P(("blk", "fsdp")),
        P(("blk", "fsdp")),
        P(("blk", "fsdp"), None),
        P(("blk", "fsdp"), None),
        P(("blk", "fsdp"), None),
        P(("blk", "fsdp"), None),
        P(("blk", "fsdp"), None),
        P(("blk", "fsdp"), None),
        P(("blk", "fsdp"), None),
    )
    body = plane_shards if by_plane(mesh) else shards
    return jax.shard_map(body, mesh=mesh, in_specs=in_specs, out_specs=out_specs, check_vma=False)
```

```python
import functools

import jax
import jax.numpy as jnp
from jax import lax
from jax.experimental import pallas as pl
from jax.experimental.pallas import tpu as pltpu
from jax.sharding import PartitionSpec as P

HEADS = 16
KVH = 8
HD = 96


EPS = 1e-05
ROPE_BASE = 100000.0
NEG = -1e30


def passed_along(block, axis, distance):
    devices = range(lax.axis_size(axis))
    route = [(i - distance, i) for i in devices if i - distance in devices]
    return lax.ppermute(block, axis, route)


def passed_along_2(x, axis, by):
    length = lax.axis_size(axis)
    return lax.ppermute(x, axis, [(i, (i + by) % length) for i in range(length)])


def product_t(left, right):
    return lax.dot_general(
        left, right, (((1,), (1,)), ((), ())), preferred_element_type=jnp.float32
    )


def product(left, right):
    return jnp.dot(left, right, preferred_element_type=jnp.float32)


def product_tn(left, right):
    return lax.dot_general(
        left, right, (((0,), (0,)), ((), ())), preferred_element_type=jnp.float32
    )


def rms_scale(values):
    return lax.rsqrt(jnp.mean(values * values, axis=-1, keepdims=True) + EPS)


def norm_back(grad, values, scale, gain):
    weighted = grad * gain
    inner = jnp.mean(weighted * values, axis=-1, keepdims=True)
    return (scale * weighted - values * scale**3 * inner, jnp.sum(grad * values * scale, axis=0))


def rotation(positions):
    half = HD // 2
    freqs = ROPE_BASE ** (-(jnp.arange(half, dtype=jnp.float32) * 2.0 / HD))
    angles = positions.astype(jnp.float32)[:, None] * freqs[None, :]
    return (jnp.cos(angles)[:, None, :], jnp.sin(angles)[:, None, :])


def rotate(values, cosine, sine, heads, sign):
    count = values.shape[0]
    split = values.reshape(count, heads, HD)
    half = HD // 2
    first = split[..., :half]
    second = split[..., half:]
    turned = jnp.concatenate(
        [first * cosine - sign * second * sine, second * cosine + sign * first * sine], axis=-1
    )
    return turned.reshape(count, heads * HD)


def block_mask(query_seg, query_idx, key_seg, key_idx):
    return (query_seg[:, None] == key_seg[None, :]) & (key_idx[None, :] <= query_idx[:, None])


def scores_of(queries, keys, allowed):
    raw = jnp.einsum("qhgd,khd->hgqk", queries, keys, preferred_element_type=jnp.float32) * HD ** (
        -0.5
    )
    return jnp.where(allowed[None, None], raw, NEG)


def key_blocks(keys_seen, values_seen, key_segs):
    total = keys_seen.shape[0]
    size = min(512, total)
    count = total // size
    return (
        keys_seen.reshape(count, size, KVH, HD),
        values_seen.reshape(count, size, KVH, HD),
        key_segs.reshape(count, size),
        jnp.arange(total, dtype=jnp.int32).reshape(count, size),
    )


def attend(queries, blocks, query_seg, query_idx):
    rows = queries.shape[0]
    groups = HEADS // KVH
    start = (
        jnp.full((KVH, groups, rows, 1), NEG, jnp.float32),
        jnp.zeros((KVH, groups, rows, 1), jnp.float32),
    )

    def stats_step(carry, block):
        keys, values, segs, idxs = block
        allowed = block_mask(query_seg, query_idx, segs, idxs)
        top, running = carry
        scores = scores_of(queries, keys, allowed)
        new_top = jnp.maximum(top, jnp.max(scores, axis=-1, keepdims=True))
        new_sum = running * jnp.exp(top - new_top) + jnp.sum(
            jnp.exp(scores - new_top), axis=-1, keepdims=True
        )
        return ((new_top, new_sum), None)

    (top, running), unused = lax.scan(stats_step, start, blocks)
    lse = top + jnp.log(running)

    def value_step(total_acc, block):
        keys, values, segs, idxs = block
        allowed = block_mask(query_seg, query_idx, segs, idxs)
        weights = jnp.exp(scores_of(queries, keys, allowed) - lse).astype(jnp.bfloat16)
        return (
            total_acc
            + jnp.einsum("hgqk,khd->qhgd", weights, values, preferred_element_type=jnp.float32),
            None,
        )

    mixed, unused = lax.scan(value_step, jnp.zeros((rows, KVH, groups, HD), jnp.float32), blocks)
    return (mixed, lse)


def cycle_back(queries, own_keys, own_values, key_segs, query_seg, query_idx, lse, grad_out, delta):
    rows = queries.shape[0]
    groups = HEADS // KVH
    scale = HD ** (-0.5)
    me = lax.axis_index("blk")
    count = lax.axis_size("blk")
    local = jnp.arange(rows, dtype=jnp.int32)

    def step(carry, turn):
        grad_q, key_blk, value_blk, grad_k, grad_v = carry
        anchor = (me - turn) % count
        begin = anchor * rows
        segs = lax.dynamic_slice_in_dim(key_segs, begin, rows)
        allowed = block_mask(query_seg, query_idx, segs, begin + local)
        acc_k = grad_k
        acc_v = grad_v
        probs = jnp.exp(scores_of(queries, key_blk, allowed) - lse)
        grad_probs = jnp.einsum(
            "qhgd,khd->hgqk", grad_out, value_blk, preferred_element_type=jnp.float32
        )
        grad_scores = (probs * (grad_probs - delta)).astype(jnp.bfloat16)
        new_acc = grad_q + jnp.einsum(
            "hgqk,khd->qhgd", grad_scores, key_blk, preferred_element_type=jnp.float32
        )
        new_k = (
            acc_k
            + jnp.einsum("hgqk,qhgd->khd", grad_scores, queries, preferred_element_type=jnp.float32)
            * scale
        )
        new_v = acc_v + jnp.einsum(
            "hgqk,qhgd->khd",
            probs.astype(jnp.bfloat16),
            grad_out,
            preferred_element_type=jnp.float32,
        )
        grad_k = new_k
        grad_v = new_v
        key_blk, value_blk = passed_along((key_blk, value_blk), "blk", 1)
        grad_k, grad_v = (
            passed_along_2(grad_k.astype(jnp.bfloat16), "blk", 1).astype(grad_k.dtype),
            passed_along_2(grad_v.astype(jnp.bfloat16), "blk", 1).astype(grad_v.dtype),
        )
        return ((new_acc, key_blk, value_blk, grad_k, grad_v), None)

    zero_kv = jnp.zeros((rows, KVH, HD), jnp.float32)
    start = (
        jnp.zeros((rows, KVH, groups, HD), jnp.float32),
        own_keys.reshape(rows, KVH, HD),
        own_values.reshape(rows, KVH, HD),
        zero_kv,
        zero_kv,
    )
    final, unused = lax.scan(step, start, jnp.arange(count, dtype=jnp.int32))
    grad_q, ignored_k, ignored_v, grad_k, grad_v = final
    return (grad_q * scale, grad_k.reshape(rows, KVH * HD), grad_v.reshape(rows, KVH * HD))


def fetch_attention(gain_attn, gain_ffn, w_query, w_key, w_value, w_output):
    return (
        lax.all_gather(gain_attn, ("blk", "fsdp"), axis=0, tiled=True),
        lax.all_gather(gain_ffn, ("blk", "fsdp"), axis=0, tiled=True),
        lax.all_gather(w_query, ("blk", "fsdp"), axis=0, tiled=True),
        lax.all_gather(w_key, ("blk", "fsdp"), axis=0, tiled=True),
        lax.all_gather(w_value, ("blk", "fsdp"), axis=0, tiled=True),
        lax.all_gather(w_output, ("blk", "fsdp"), axis=0, tiled=True),
    )


def fetch_ffn(w_gate, w_up, w_down):
    return (
        lax.all_gather(w_gate, ("blk", "fsdp"), axis=0, tiled=True),
        lax.all_gather(w_up, ("blk", "fsdp"), axis=0, tiled=True),
        lax.all_gather(w_down, ("blk", "fsdp"), axis=0, tiled=True),
    )


def shards(
    tokens,
    cotangent,
    segments,
    positions,
    gain_attn,
    gain_ffn,
    w_query,
    w_key,
    w_value,
    w_output,
    w_gate,
    w_up,
    w_down,
):
    rows = tokens.shape[1]
    groups = HEADS // KVH
    xin = tokens[0].astype(jnp.float32)
    offset = lax.axis_index("blk") * rows
    query_idx = offset + jnp.arange(rows, dtype=jnp.int32)
    key_segs = segments[0]
    query_seg = lax.dynamic_slice_in_dim(key_segs, offset, rows)
    cosine, sine = rotation(positions[0])
    gain_one, gain_two, query_all, key_all, value_all, output_all = fetch_attention(
        gain_attn, gain_ffn, w_query, w_key, w_value, w_output
    )
    first_gain = gain_one.astype(jnp.float32)
    second_gain = gain_two.astype(jnp.float32)
    first_scale = rms_scale(xin)
    normed = (xin * first_scale * first_gain).astype(jnp.bfloat16)
    queries = rotate(product_t(normed, query_all), cosine, sine, HEADS, 1.0).astype(jnp.bfloat16)
    keys = rotate(product_t(normed, key_all), cosine, sine, KVH, 1.0).astype(jnp.bfloat16)
    values = product_t(normed, value_all).astype(jnp.bfloat16)
    keys_seen, values_seen = (
        lax.all_gather(keys, "blk", axis=0, tiled=True),
        lax.all_gather(values, "blk", axis=0, tiled=True),
    )
    query_heads = queries.reshape(rows, KVH, groups, HD)
    mixed, lse = attend(
        query_heads, key_blocks(keys_seen, values_seen, key_segs), query_seg, query_idx
    )
    attended = mixed.reshape(rows, HEADS * HD).astype(jnp.bfloat16)
    middle = xin + product_t(attended, output_all)
    second_scale = rms_scale(middle)
    normed_two = (middle * second_scale * second_gain).astype(jnp.bfloat16)
    gate_rows, up_rows, down_rows = fetch_ffn(w_gate, w_up, w_down)
    gate = product_t(normed_two, gate_rows)
    up = product_t(normed_two, up_rows)
    sigma = jax.nn.sigmoid(gate)
    activated = gate * sigma
    hidden = (activated * up).astype(jnp.bfloat16)
    branch = product(hidden, down_rows)
    result = (middle + branch).astype(jnp.bfloat16)
    grad_in = cotangent[0]
    gate_rows, up_rows, down_rows = fetch_ffn(w_gate, w_up, w_down)
    grad_hidden = product_t(grad_in, down_rows)
    grad_gate = (grad_hidden * up * sigma * (1.0 + gate * (1.0 - sigma))).astype(jnp.bfloat16)
    grad_up = (grad_hidden * activated).astype(jnp.bfloat16)
    gate_grad = product_tn(grad_gate, normed_two)
    up_grad = product_tn(grad_up, normed_two)
    down_grad = product_tn(hidden, grad_in)
    grad_normed_two = product(grad_gate, gate_rows) + product(grad_up, up_rows)
    gate_grad, up_grad, down_grad = (
        lax.psum_scatter(gate_grad, ("blk", "fsdp"), scatter_dimension=0, tiled=True),
        lax.psum_scatter(up_grad, ("blk", "fsdp"), scatter_dimension=0, tiled=True),
        lax.psum_scatter(down_grad, ("blk", "fsdp"), scatter_dimension=0, tiled=True),
    )
    grad_middle_norm, second_gain_grad = norm_back(
        grad_normed_two, middle, second_scale, second_gain
    )
    grad_middle = grad_in.astype(jnp.float32) + grad_middle_norm
    grad_branch = grad_middle.astype(jnp.bfloat16)
    output_grad = product_tn(grad_branch, attended)
    grad_attended = product(grad_branch, output_all).astype(jnp.bfloat16)
    grad_heads = grad_attended.reshape(rows, KVH, groups, HD)
    delta = jnp.transpose(jnp.sum(grad_heads.astype(jnp.float32) * mixed, axis=-1), (1, 2, 0))[
        ..., None
    ]
    grad_q, grad_keys, grad_values = cycle_back(
        query_heads, keys, values, key_segs, query_seg, query_idx, lse, grad_heads, delta
    )
    grad_q_pre = rotate(grad_q.reshape(rows, HEADS * HD), cosine, sine, HEADS, -1.0).astype(
        jnp.bfloat16
    )
    grad_k_pre = rotate(grad_keys, cosine, sine, KVH, -1.0).astype(jnp.bfloat16)
    grad_v = grad_values.astype(jnp.bfloat16)
    query_grad = product_tn(grad_q_pre, normed)
    key_grad = product_tn(grad_k_pre, normed)
    value_grad = product_tn(grad_v, normed)
    grad_normed = (
        product(grad_q_pre, query_all) + product(grad_k_pre, key_all) + product(grad_v, value_all)
    )
    grad_x_norm, first_gain_grad = norm_back(grad_normed, xin, first_scale, first_gain)
    grad_tokens = grad_middle + grad_x_norm
    first_gain_grad, second_gain_grad, query_grad, key_grad, value_grad, output_grad = (
        lax.psum_scatter(first_gain_grad, ("blk", "fsdp"), scatter_dimension=0, tiled=True),
        lax.psum_scatter(second_gain_grad, ("blk", "fsdp"), scatter_dimension=0, tiled=True),
        lax.psum_scatter(query_grad, ("blk", "fsdp"), scatter_dimension=0, tiled=True),
        lax.psum_scatter(key_grad, ("blk", "fsdp"), scatter_dimension=0, tiled=True),
        lax.psum_scatter(value_grad, ("blk", "fsdp"), scatter_dimension=0, tiled=True),
        lax.psum_scatter(output_grad, ("blk", "fsdp"), scatter_dimension=0, tiled=True),
    )
    return (
        result[None],
        grad_tokens[None],
        first_gain_grad,
        second_gain_grad,
        query_grad,
        key_grad,
        value_grad,
        output_grad,
        gate_grad,
        up_grad,
        down_grad,
    )


CHIPS = 8
TOK = 128
PAIR = 2 * HD
LANES = 128
VMEM_LIMIT = 32 << 20
LOG2E = 1.4426950408889634
RING = (0, 2, 4, 6, 7, 5, 3, 1)
SAME_CORE = [[2 * c + core for c in range(CHIPS)] for core in range(2)]


def ring_route(step):
    return [
        (RING[k] * 2 + core, RING[(k + step) % CHIPS] * 2 + core)
        for k in range(CHIPS)
        for core in range(2)
    ]


def ring_up(value):
    return lax.ppermute(value, "blk", ring_route(1))


def ring_down(value):
    return lax.ppermute(value, "blk", ring_route(-1))


def flipped(value, bit):
    return lax.ppermute(value, "blk", [(i, i ^ bit) for i in range(2 * CHIPS)])


def core_swap(value):
    return flipped(value, 1)


def x_swap(value):
    return lax.ppermute(value, "fsdp", [(0, 1), (1, 0)])


def tie(values, deps):
    deps = [d for d in deps if d is not None]
    if not deps:
        return tuple(values)
    return lax.optimization_barrier((tuple(values), tuple(deps)))[0]


def after(value, *deps):
    return tie((value,), deps)[0]


class Gather:
    def __init__(self, block):
        self.found = [None] * CHIPS
        self.found[0] = self.up = self.down = block

    def step(self, number, *deps):
        self.up, self.down = tie((self.up, self.down), deps)
        if number < CHIPS // 2:
            self.up = ring_up(self.up)
            self.down = ring_down(self.down)
            self.found[CHIPS - number] = self.up
            self.found[number] = self.down
        else:
            half = self.up.shape[0] // 2
            self.up = ring_up(self.up[:half])
            self.down = ring_down(self.down[half:])
            self.found[number] = (self.up, self.down)
        return self.up, self.down


class Scatter:
    def __init__(self, make):
        self.make = make
        self.up = self.down = None

    def step(self, number, *deps):
        up, down = tie(self.make(number, self.up, self.down), deps)
        self.up = ring_up(up)
        self.down = ring_down(down)
        return self.up, self.down


def dot_nt(left, right):
    return lax.dot_general(
        left, right, (((1,), (1,)), ((), ())), preferred_element_type=jnp.float32
    )


def dot_nn(left, right):
    return lax.dot_general(
        left, right, (((1,), (0,)), ((), ())), preferred_element_type=jnp.float32
    )


GROUPS = ((0, 1, 7), (2, 6), (3, 5), (4,))
ARRIVAL = tuple(j for group in GROUPS for j in group)


def whole(shape):
    return pl.BlockSpec(shape, lambda i: (0,) * len(shape), pipeline_mode=pl.Buffered(1))


def window(rows, nth, width):
    return pl.BlockSpec((rows, width), lambda i: (nth, 0), pipeline_mode=pl.Buffered(1))


def call(kernel, name, outs, ins, scratch=(), far=(), far_out=(), windows={}):
    shapes = []
    for n, (shape, dtype) in enumerate(outs):
        make = pltpu.HBM if n in far_out else jax.ShapeDtypeStruct
        shapes.append(make(shape, dtype))
    ins = list(ins)
    for n in far:
        ins[n] = pltpu.with_memory_space_constraint(ins[n], pltpu.HBM)
    return pl.pallas_call(
        kernel,
        grid=(1,),
        out_shape=tuple(shapes),
        in_specs=[
            window(*windows[n], value.shape[1]) if n in windows else whole(value.shape)
            for n, value in enumerate(ins)
        ],
        out_specs=tuple(whole(shape) for shape, _ in outs),
        scratch_shapes=scratch,
        compiler_params=pltpu.CompilerParams(vmem_limit_bytes=VMEM_LIMIT),
        cost_estimate=pl.CostEstimate(flops=0, bytes_accessed=0, transcendentals=0),
        name=name,
    )(*ins)


def dot_tn(left, right):
    return lax.dot_general(
        left, right, (((0,), (0,)), ((), ())), preferred_element_type=jnp.float32
    )


def own_place():
    index = lax.axis_index("blk")
    chip = lax.div(index, 2)
    half = lax.div(chip, 2)
    spot = jnp.where(lax.rem(chip, 2) == 0, half, CHIPS - 1 - half)
    return lax.rem(index, 2), lax.axis_index("fsdp"), chip, spot


def arriving_chip(nth, spot):
    at = lax.rem(spot + ARRIVAL[nth], CHIPS)
    return jnp.where(at < CHIPS // 2, 2 * at, 2 * CHIPS - 1 - 2 * at)


def arrival_of(chip, spot):
    away = lax.rem(RING.index(chip) - spot + CHIPS, CHIPS)
    late = jnp.where(away <= CHIPS // 2, 2 * away - 1, 2 * (CHIPS - away))
    return jnp.where(away == 0, 0, late)


def heads_kernel(own, near, far, across, out):
    nq = HD // 2
    nk = HD // 4
    half = LANES // 2
    own_core, own_side, _, _ = own_place()
    out[...] = jnp.zeros_like(out)
    for core in range(2):
        for side in range(2):

            @pl.when((own_core == core) & (own_side == side))
            def _():
                for piece, c, f in (
                    (own, core, side),
                    (near, core, 1 - side),
                    (far, 1 - core, side),
                    (across, 1 - core, 1 - side),
                ):
                    at = c * LANES + f * half
                    out[at : at + nq] = piece[:nq]
                    at = 2 * LANES + c * half + f * nk
                    out[at : at + nk] = piece[nq : nq + nk]
                    at = 3 * LANES + (2 * c + f) * nk
                    out[at : at + nk] = piece[nq + nk :]


def stack_kernel(*refs):
    out = refs[-1]
    at = 0
    for piece in refs[:-1]:
        out[at : at + piece.shape[0]] = piece[...]
        at += piece.shape[0]


def out_kernel(*refs):
    own, near, out = refs[:4], refs[4:8], refs[8]
    side = own_place()[1]
    rows = own[0].shape[0] // 2
    for n, j in enumerate(ARRIVAL):
        away = min(j, CHIPS - j)
        which = 3 if away in (0, CHIPS // 2) else away - 1
        here = slice(0, rows) if j in (0, 1, 2, 3) else slice(rows, 2 * rows)
        for source, f in ((own, side), (near, 1 - side)):
            at = pl.multiple_of((2 * n + f) * rows, rows)
            out[pl.ds(at, rows), :] = source[which][here, :]


def hidden_kernel(*refs):
    gate_up, down = refs[-2:]
    count = refs[0].shape[0]
    for n in range(4):
        gate, up, out = refs[3 * n : 3 * n + 3]
        start = (n // 2) * 4 * count + (n % 2) * count
        gate_up[start : start + count] = gate[...]
        gate_up[start + 2 * count : start + 3 * count] = up[...]
        down[n * count : (n + 1) * count] = out[...]


def project_kernel(*refs):
    blocks = refs[: CHIPS + 1]
    gain, weight, cosine, sine, normed_out, query_out, kv_out = refs[CHIPS + 1 :]
    for j in range(CHIPS):
        if j < CHIPS - 1:
            values = blocks[j][-TOK:].astype(jnp.float32)
        else:
            late = blocks[CHIPS][...].astype(jnp.float32)
            values = blocks[j][-(TOK - late.shape[0]) :].astype(jnp.float32)
            values = jnp.concatenate([values, late], axis=0)
        scale = lax.rsqrt(jnp.mean(values * values, axis=-1, keepdims=True) + EPS)
        normed_out[j * TOK : (j + 1) * TOK, :] = (values * scale * gain[...]).astype(jnp.bfloat16)
    pre = dot_nt(normed_out[...], weight[...])
    for head in range(3):
        part = pre[:, head * LANES : (head + 1) * LANES]
        turned = part * cosine[...] + pltpu.roll(part, LANES // 2, 1) * sine[...]
        if head < 2:
            query_out[:, head * LANES : (head + 1) * LANES] = turned.astype(jnp.bfloat16)
        else:
            kv_out[:, :LANES] = turned.astype(jnp.bfloat16)
    kv_out[:, LANES:] = pre[:, 3 * LANES :].astype(jnp.bfloat16)


def project(blocks, *arrays):
    rows = CHIPS * TOK
    width = blocks[0].shape[1]
    low = jnp.bfloat16
    assert len(blocks) == CHIPS + 1
    return call(
        project_kernel,
        "project",
        (((rows, width), low), ((rows, 2 * LANES), low), ((rows, 2 * LANES), low)),
        (*blocks, *arrays),
        far=range(CHIPS + 1),
        far_out=(0,),
    )


def key_index(core, count):
    row = lax.broadcasted_iota(jnp.int32, (count, 1), 0)
    return (row // TOK) * (2 * TOK) + core * TOK + row % TOK


def query_index(core, chip):
    lane = lax.broadcasted_iota(jnp.int32, (1, 2 * TOK), 1)
    return lane % TOK + (2 * chip + core) * TOK


def sequence_starts(segments):
    numbers = segments[...]
    starts = []
    for number in range(1, 4):
        below = (numbers < number).astype(jnp.float32)
        total = jnp.sum(jnp.sum(below, axis=1, keepdims=True), axis=0, keepdims=True)
        starts.append(total.astype(jnp.int32))
    return starts


def first_index(starts, at):
    first = jnp.zeros_like(at)
    for start in starts:
        first = jnp.where(at >= start, start, first)
    return first


def only_allowed(values, keys_at, at, first, chip):
    if chip in (0, CHIPS - 1):
        return jnp.where((keys_at <= at) & (keys_at >= first), values, NEG)
    low = jnp.where(keys_at[:TOK] >= first, values[:TOK], NEG)
    high = jnp.where(keys_at[chip * TOK :] <= at, values[chip * TOK :], NEG)
    parts = [low, values[TOK : chip * TOK], high] if chip > 1 else [low, high]
    return jnp.concatenate(parts, axis=0)


def both_heads(ref, rows):
    return jnp.concatenate([ref[rows, :LANES], ref[rows, LANES:]], axis=0)


def attend_kernel(
    segments, query_in, own_in, peer_in, attended, mixed, lse, query, own, peer
):
    core, _, _, spot = own_place()
    starts = sequence_starts(segments)
    factor = HD ** (-0.5) * LOG2E
    for source, target in ((query_in, query), (own_in, own), (peer_in, peer)):
        for chip in range(CHIPS):
            rows = pl.ds(pl.multiple_of(arrival_of(chip, spot) * TOK, TOK), TOK)
            target[chip * TOK : (chip + 1) * TOK, :] = source[rows, :]
    sides = ((own, core), (peer, 1 - core))
    values_t = [jnp.transpose(kv[:, LANES:]) for kv, _ in sides]
    for chip in range(CHIPS):
        count = (chip + 1) * TOK
        rows = slice(chip * TOK, count)
        queries = both_heads(query, rows)
        at = query_index(core, chip)
        first = first_index(starts, at)
        scores = []
        for kv, side in sides:
            raw = dot_nt(kv[:count, :LANES], queries) * factor
            scores.append(only_allowed(raw, key_index(side, count), at, first, chip))
        top = jnp.maximum(
            jnp.max(scores[0], axis=0, keepdims=True), jnp.max(scores[1], axis=0, keepdims=True)
        )
        weights = [jnp.exp2(part - top) for part in scores]
        total = jnp.sum(weights[0], axis=0, keepdims=True) + jnp.sum(
            weights[1], axis=0, keepdims=True
        )
        mix = dot_nn(values_t[0][:, :count], weights[0].astype(jnp.bfloat16)) + dot_nn(
            values_t[1][:, :count], weights[1].astype(jnp.bfloat16)
        )
        mix = mix / total
        mixed[chip] = mix
        lse[chip] = top + jnp.log2(total)
        attended[chip, :HD] = mix[:HD, :TOK].astype(jnp.bfloat16)
        attended[chip, HD:] = mix[:HD, TOK:].astype(jnp.bfloat16)


def attend_heads(segments, query, own, peer):
    tokens = CHIPS * TOK
    low = jnp.bfloat16
    return call(
        attend_kernel,
        "attend",
        (
            ((CHIPS, PAIR, TOK), low),
            ((CHIPS, LANES, 2 * TOK), jnp.float32),
            ((CHIPS, 1, 2 * TOK), jnp.float32),
            ((tokens, 2 * LANES), low),
            ((tokens, 2 * LANES), low),
            ((tokens, 2 * LANES), low),
        ),
        (segments, query, own, peer),
        far_out=(1, 2, 3, 4, 5),
    )


def attend_back_kernel(
    segments, query, own, peer, grad_out, mixed, lse, cosine, sine,
    grad_query, own_out, peer_out, grad_own, grad_peer,
):
    core, _, _, spot = own_place()
    starts = sequence_starts(segments)
    scale = HD ** (-0.5)
    factor = scale * LOG2E
    sides = ((own, core, grad_own), (peer, 1 - core, grad_peer))
    keys_t = [jnp.transpose(kv[:, :LANES]) for kv, _, _ in sides]
    grad_own[...] = jnp.zeros_like(grad_own)
    grad_peer[...] = jnp.zeros_like(grad_peer)
    pad = jnp.zeros((LANES - HD, 2 * TOK), jnp.bfloat16)
    for chip in range(CHIPS):
        count = (chip + 1) * TOK
        rows = slice(chip * TOK, count)
        kept = pl.ds(pl.multiple_of(arrival_of(chip, spot) * TOK, TOK), TOK)
        queries = both_heads(query, rows)
        grads = jnp.concatenate(
            [
                jnp.concatenate([grad_out[chip, :HD], grad_out[chip, HD:]], axis=1),
                pad,
            ],
            axis=0,
        )
        delta = jnp.sum(grads.astype(jnp.float32) * mixed[chip], axis=0, keepdims=True)
        at = query_index(core, chip)
        first = first_index(starts, at)
        level = lse[chip]
        grad_q = jnp.zeros((LANES, 2 * TOK), jnp.float32)
        for (kv, side, grad_kv), key_t in zip(sides, keys_t):
            raw = dot_nt(kv[:count, :LANES], queries) * factor
            keys_at = key_index(side, count)
            probs = jnp.exp2(only_allowed(raw - level, keys_at, at, first, chip))
            grad_probs = dot_nn(kv[:count, LANES:], grads)
            grad_scores = (probs * (grad_probs - delta)).astype(jnp.bfloat16)
            grad_kv[:count, LANES:] += dot_nt(probs.astype(jnp.bfloat16), grads)
            grad_kv[:count, :LANES] += dot_nn(grad_scores, queries)
            grad_q += dot_nn(key_t[:, :count], grad_scores)
        grad_q = jnp.transpose(grad_q) * scale
        cos = cosine[kept, :]
        sin = sine[kept, :]
        for head in range(2):
            part = grad_q[head * TOK : (head + 1) * TOK]
            turned = part * cos - pltpu.roll(part, LANES // 2, 1) * sin
            grad_query[kept, head * LANES : (head + 1) * LANES] = turned.astype(jnp.bfloat16)
    for chip in range(CHIPS):
        rows = slice(chip * TOK, (chip + 1) * TOK)
        kept = pl.ds(pl.multiple_of(arrival_of(chip, spot) * TOK, TOK), TOK)
        for grad_kv, out in ((grad_own, own_out), (grad_peer, peer_out)):
            out[kept, :LANES] = grad_kv[rows, :LANES] * scale
            out[kept, LANES:] = grad_kv[rows, LANES:]


def attend_back(segments, *arrays):
    tokens = CHIPS * TOK
    full = jnp.float32
    return call(
        attend_back_kernel,
        "attend_back",
        (
            ((tokens, 2 * LANES), jnp.bfloat16),
            ((tokens, 2 * LANES), full),
            ((tokens, 2 * LANES), full),
        ),
        (segments, *arrays),
        scratch=[pltpu.VMEM((tokens, 2 * LANES), full)] * 2,
        far=(1, 2, 3, 5, 6, 7, 8),
    )


def join_kernel(heads, *refs):
    weights = refs[:2]
    block, gain, middle_out, normed_out, attended_out, weight_out, held = refs[2:]
    core, _, _, spot = own_place()
    size = weights[0].shape[0] // CHIPS
    for n in range(CHIPS):
        for piece, side in zip(weights, (core, 1 - core)):
            at = pl.multiple_of((2 * arriving_chip(n, spot) + side) * size, size)
            weight_out[pl.ds(at, size), :] = piece[n * size : (n + 1) * size, :]
    for chip in range(CHIPS):
        held[chip * PAIR : (chip + 1) * PAIR, :] = heads[chip]
    attended_out[...] = jnp.transpose(held[...])
    middle = block[...].astype(jnp.float32) + dot_nt(attended_out[...], weight_out[...])
    middle_out[...] = middle
    scale = lax.rsqrt(jnp.mean(middle * middle, axis=-1, keepdims=True) + EPS)
    normed_out[...] = (middle * scale * gain[...]).astype(jnp.bfloat16)


def ffn_kernel(number, *refs):
    blocks = refs[:number]
    outers = refs[number : 2 * number]
    gate_up, down_rows = refs[2 * number : 2 * number + 2]
    rows, outer_rows, hidden, grad_gu = refs[2 * number + 2 : 2 * number + 6]
    wide = hidden.shape[1] // 2
    size = rows.shape[0] // number
    for n in range(number):
        rows[n * size : (n + 1) * size, :] = blocks[n][...]
        outer_rows[n * size : (n + 1) * size, :] = outers[n][...]
    grads = dot_nt(outer_rows[...], down_rows[...])
    pre = dot_nt(rows[...], gate_up[...])
    for part in range(2):
        at = part * 2 * wide
        gate = pre[:, at : at + wide]
        up = pre[:, at + wide : at + 2 * wide]
        back = grads[:, part * wide : (part + 1) * wide]
        sigma = 1.0 / (1.0 + jnp.exp(-gate))
        active = gate * sigma
        hidden[:, part * wide : (part + 1) * wide] = (active * up).astype(jnp.bfloat16)
        slope = back * up * sigma * (1.0 + gate * (1.0 - sigma))
        grad_gu[:, at : at + wide] = slope.astype(jnp.bfloat16)
        grad_gu[:, at + wide : at + 2 * wide] = (back * active).astype(jnp.bfloat16)
    outs = refs[2 * number + 6 :]
    back = dot_nn(grad_gu[...], gate_up[...])
    if len(outs) == 1:
        outs[0][...] = back
    else:
        outs[0][...] = back[: TOK // 2].astype(jnp.bfloat16)
        outs[1][...] = back[TOK // 2 :].astype(jnp.bfloat16)


def ffn(blocks, outers, gate_up, down):
    number = len(blocks)
    rows = number * blocks[0].shape[0]
    width = blocks[0].shape[1]
    units = down.shape[0]
    low = jnp.bfloat16
    if rows > TOK:
        terms = [((rows, width), jnp.float32)]
    else:
        terms = [((TOK // 2, width), low)] * 2
    return call(
        functools.partial(ffn_kernel, number),
        "ffn",
        [((rows, width), low)] * 2 + [((rows, units), low), ((rows, 2 * units), low)] + terms,
        (*blocks, *outers, gate_up, down),
    )


def add_terms(up_term, down_term, up, down, up_out, down_out):
    size = up.shape[0]
    rest = up_out.shape[0] - size
    low = jnp.bfloat16
    full = jnp.float32
    up_out[:size] = (up_term[:size] + up.astype(full)).astype(low)
    down_out[rest:] = (down_term[rest:] + down.astype(full)).astype(low)
    if rest:
        up_out[size:] = up_term[size:].astype(low)
        down_out[:rest] = down_term[:rest].astype(low)


def add_kernel(up_term, down_term, up, down, up_out, down_out):
    add_terms(up_term, down_term, up[...], down[...], up_out, down_out)


def leaving(width, rows=TOK):
    return [((rows, width), jnp.bfloat16)] * 2


STEP_ROWS = {1: 7 * TOK, 2: 5 * TOK, 3: 3 * TOK, 4: TOK}


def branch_kernel(hidden, down_rows, *outs):
    found = dot_nn(hidden[...], down_rows[...])
    at = 0
    for out in outs[:-2]:
        out[...] = found[at : at + out.shape[0]]
        at += out.shape[0]
    outs[-2][...] = found[at : at + TOK // 2].astype(jnp.bfloat16)
    outs[-1][...] = found[at + TOK // 2 :].astype(jnp.bfloat16)


def result_kernel(terms, up, down, middle, out):
    full = jnp.float32
    branch = terms[...] + (up[...].astype(full) + down[...].astype(full))
    out[...] = (middle[...] + branch).astype(jnp.bfloat16)


def grads_kernel(number, *refs):
    rows_in, outer_in, hidden_in, grads_in = (refs[n * number : (n + 1) * number] for n in range(4))
    keep_gu, keep_down, send_gu, send_down, hidden, rows, grads = refs[4 * number :]
    at = 0
    for block, hid, grad in zip(rows_in, hidden_in, grads_in):
        here = slice(at, at + block.shape[0])
        rows[here, :] = block[...]
        hidden[here, :] = hid[...]
        grads[here, :] = grad[...]
        at += block.shape[0]
    half = keep_gu.shape[0]
    send_gu[...] = dot_tn(grads[:, half:], rows[...])
    keep_gu[...] = dot_tn(grads[:, :half], rows[...])
    at = 0
    for block in outer_in:
        rows[at : at + block.shape[0], :] = block[...]
        at += block.shape[0]
    half = keep_down.shape[0]
    send_down[...] = dot_tn(hidden[:, half:], rows[...])
    keep_down[...] = dot_tn(hidden[:, :half], rows[...])


def owners_kernel(keep_gu, keep_down, other_gu, other_down, *outs):
    count = outs[0].shape[0]
    for n, (value, other, at) in enumerate(
        ((keep_gu, other_gu, 0), (keep_gu, other_gu, 2 * count), (keep_down, other_down, 0))
    ):
        near = at + count
        outs[n][...] = value[at:near] + other[at:near]
        given = value[near : near + count] + other[near : near + count]
        outs[3 + n][...] = given.astype(jnp.bfloat16)


def turn_kernel(*refs):
    own, up, down, middle_ref, outer, gain, weight, middle_out, branch_out, heads, gain_out = refs
    grad = own[...] + (up[...].astype(jnp.float32) + down[...].astype(jnp.float32))
    middle = middle_ref[...]
    scale = lax.rsqrt(jnp.mean(middle * middle, axis=-1, keepdims=True) + EPS)
    weighted = grad * gain[...]
    inner = jnp.mean(weighted * middle, axis=-1, keepdims=True)
    gain_out[...] = jnp.sum(grad * middle * scale, axis=0, keepdims=True)
    total = outer[...].astype(jnp.float32) + (scale * weighted - middle * (scale**3 * inner))
    middle_out[...] = total
    branch = total.astype(jnp.bfloat16)
    branch_out[...] = branch
    back = jnp.transpose(dot_nn(branch, weight[...]).astype(jnp.bfloat16))
    for chip in range(CHIPS):
        heads[chip] = back[chip * PAIR : (chip + 1) * PAIR]


def outer_kernel(branch, attended, keep, give, held):
    held[...] = dot_tn(branch[...], attended[...])
    core = own_place()[0]
    size = keep.shape[1]
    for chip in range(CHIPS):
        at = pl.multiple_of((2 * chip + core) * size, size)
        keep[chip] = held[pl.ds(at, size), :].astype(jnp.bfloat16)
        at = pl.multiple_of((2 * chip + 1 - core) * size, size)
        give[chip] = held[pl.ds(at, size), :].astype(jnp.bfloat16)


def settle_kernel(keep, other, total):
    spot = own_place()[3]
    rows = keep.shape[1]
    for n in range(CHIPS):
        chip = arriving_chip(n, spot)
        found = keep[chip].astype(jnp.float32) + other[chip].astype(jnp.float32)
        total[n * rows : (n + 1) * rows] = found.astype(jnp.bfloat16)


def product_kernel(up_left, down_left, right, up, down, up_out, down_out):
    terms = dot_nn(jnp.concatenate([up_left[...], down_left[...]], axis=0), right[...])
    add_terms(terms[:TOK], terms[TOK:], up[...], down[...], up_out, down_out)


def rows_kernel(up_term, down_term, up, down, up_out, down_out):
    full = jnp.float32
    add_terms(
        up_term[...].astype(full), down_term[...].astype(full), up[...], down[...], up_out, down_out
    )


def spread_kernel(
    query, own, other, cosine, sine, weight, second, joined, up_out, down_out, up_rows, down_rows
):
    joined[:, : 2 * LANES] = query[...]
    total = own[...] + other[...]
    part = total[:, :LANES]
    turned = part * cosine[...] - pltpu.roll(part, LANES // 2, 1) * sine[...]
    joined[:, 2 * LANES : 3 * LANES] = turned.astype(jnp.bfloat16)
    joined[:, 3 * LANES :] = total[:, LANES:].astype(jnp.bfloat16)
    begin = STEP_ROWS[1]
    terms = dot_nn(joined[begin : begin + TOK], weight[...]).astype(jnp.bfloat16)
    up_out[...] = terms[: TOK // 2]
    down_out[...] = terms[TOK // 2 :]
    rows = second.shape[0] // CHIPS
    up_rows[...] = second[(CHIPS - 1) * rows : (CHIPS - 1) * rows + rows // 2]
    down_rows[...] = second[(CHIPS - 1) * rows + rows // 2 :]


def heads_grad_kernel(*refs):
    own_core, own_side, _, _ = own_place()
    joined, weight, gain, second, normed, mine, send, gains, grad = refs
    grad[...] = dot_tn(joined[...], normed[...])
    first = jnp.sum(grad[...] * weight[...].astype(jnp.float32), axis=0, keepdims=True) / gain[...]
    nq = HD // 2
    nk = HD // 4
    half = LANES // 2
    gains[:1] = first
    gains[1:] = second[...]
    for core in range(2):
        for side in range(2):

            @pl.when((own_core == core) & (own_side == side))
            def _():
                for c in range(2):
                    for f in range(2):
                        out = mine if c == core else send
                        which = 0 if f == side else 1
                        at = c * LANES + f * half
                        out[which, :nq] = grad[at : at + nq]
                        at = 2 * LANES + c * half + f * nk
                        out[which, nq : nq + nk] = grad[at : at + nk]
                        at = 3 * LANES + (2 * c + f) * nk
                        out[which, nq + nk :] = grad[at : at + nk]


def owned_kernel(second, up, down, keep, give):
    side = own_place()[1]
    rows = keep.shape[0]
    full = jnp.float32
    total = second[...].astype(full) + (up[...].astype(full) + down[...].astype(full))
    keep[...] = jnp.where(side == 0, total[:rows], total[rows:])
    give[...] = jnp.where(side == 0, total[rows:], total[:rows]).astype(jnp.bfloat16)


def last_kernel(joined, weight, up, down, block, middle, gain, out):
    grad = dot_nn(joined[...], weight[...])
    grad = grad + (up[...].astype(jnp.float32) + down[...].astype(jnp.float32))
    values = block[...].astype(jnp.float32)
    scale = lax.rsqrt(jnp.mean(values * values, axis=-1, keepdims=True) + EPS)
    weighted = grad * gain[...]
    inner = jnp.mean(weighted * values, axis=-1, keepdims=True)
    out[...] = middle[...] + (scale * weighted - values * (scale**3 * inner))


def plane_shards(
    tokens,
    cotangent,
    segments,
    positions,
    gain_attn,
    gain_ffn,
    w_query,
    w_key,
    w_value,
    w_output,
    w_gate,
    w_up,
    w_down,
):
    full = jnp.float32
    low = jnp.bfloat16
    block = tokens[0]
    outer = cotangent[0]
    width = block.shape[1]
    index = lax.axis_index("blk")
    side = lax.axis_index("fsdp")
    core = index % 2
    chip = index // 2
    spot = jnp.where(chip % 2 == 0, chip // 2, CHIPS - 1 - chip // 2)

    segs = segments[0]
    numbers = segs.reshape(2 * CHIPS, TOK)
    starts = [jnp.sum((segs < number).astype(jnp.int32)) for number in range(1, 4)]
    row = lax.broadcasted_iota(jnp.int32, (CHIPS * TOK, LANES), 0)
    nth = row >> 7
    away = jnp.where((nth & 1) == 1, (nth + 1) >> 1, CHIPS - (nth >> 1))
    at = (spot + away) & (CHIPS - 1)
    token = jnp.where(at < CHIPS // 2, 2 * at, 2 * CHIPS - 1 - 2 * at) * (2 * TOK)
    token = token + core * TOK + (row & (TOK - 1))
    first = jnp.zeros_like(token)
    for start in starts:
        first = jnp.where(token >= start, start, first)
    half = HD // 2
    freqs = ROPE_BASE ** (-(jnp.arange(half, dtype=full) * 2.0 / HD))
    spare = jnp.zeros((LANES // 2 - half,), full)
    both = jnp.concatenate([freqs, spare, freqs, spare])
    angles = (token - first).astype(full) * both[None, :]
    sign = jnp.where(jnp.arange(LANES) < LANES // 2, -1.0, 1.0).astype(full)
    cosine = jnp.cos(angles)
    sine = jnp.sin(angles) * sign[None, :]

    ended = [()]

    def held(value):
        return after(value, *ended[-1])

    def close(*results):
        flat = []
        for result in results:
            flat += list(result) if isinstance(result, (list, tuple)) else [result]
        ended.append(tuple(flat))

    def to_chips(value):
        return lax.all_to_all(
            value, "blk", split_axis=0, concat_axis=0, axis_index_groups=SAME_CORE, tiled=True
        )

    nq = w_query.shape[0]
    nk = w_key.shape[0]
    count = w_gate.shape[0]
    units = 2 * count

    def wider(vector, bit):
        other = flipped(vector, bit) if bit else x_swap(vector)
        return jnp.where(
            ((index & bit) if bit else side) == 0,
            jnp.concatenate([vector, other], axis=1),
            jnp.concatenate([other, vector], axis=1),
        )

    both = call(
        stack_kernel, "stack_tokens", (((nq + TOK, width), low),), (w_output, block), far=(0, 1)
    )[0]
    tokens_ring = Gather(both)
    x1 = tokens_ring.step(1)
    gains = wider(wider(jnp.stack([gain_attn, gain_ffn]), 0), 1)
    close(x1, gains, cosine, sine)

    x2 = tokens_ring.step(2, *ended[-1])
    packed = call(
        stack_kernel,
        "stack_heads",
        (((nq + 2 * nk, width), low),),
        (w_query, w_key, held(w_value)),
        far=range(3),
    )[0]
    near = x_swap(packed)
    far = core_swap(packed)
    gains = wider(held(gains), 2)
    close(x2, near, far, gains)

    def out_pair(first, second):
        return call(
            stack_kernel,
            "stack_pair",
            (((2 * nq, width), low),),
            (first, second),
            far=(0, 1),
            windows={0: (nq, 0), 1: (nq, 0)},
        )[0]

    found = tokens_ring.found
    x3 = tokens_ring.step(3, *ended[-1])
    across = core_swap(held(near))
    gains = wider(held(gains), 4)
    own_outs = [out_pair(held(found[1]), found[7])]
    near_outs = [x_swap(own_outs[0])]
    close(x3, across, gains, near_outs)

    x4 = tokens_ring.step(4, *ended[-1])
    w_heads = call(
        heads_kernel,
        "head_rows",
        (((4 * LANES, width), low),),
        (packed, near, far, held(across)),
        far=range(4),
    )[0]
    own_outs.append(out_pair(held(found[2]), found[6]))
    near_outs.append(x_swap(own_outs[1]))
    gains = wider(held(gains), 8).astype(full)
    gain_one = gains[:1]
    gain_two = gains[1:]
    close(x4, gains, w_heads, near_outs[1])

    outer_ring = Gather(held(outer))
    e1 = outer_ring.step(1)
    blocks = [found[j] for j in ARRIVAL[:-1]] + list(found[4])
    normed, query, kv = project(
        [held(blocks[0])] + blocks[1:], gain_one, w_heads, cosine, sine
    )
    own_outs.append(out_pair(held(found[3]), found[5]))
    near_outs.append(x_swap(own_outs[2]))
    own_outs.append(out_pair(held(found[0]), found[4][0]))
    close(e1, near_outs[2], kv, own_outs[3])

    kv_peer = core_swap(held(kv))
    close(kv_peer)

    e2 = outer_ring.step(2, *ended[-1])
    near_outs.append(x_swap(held(own_outs[3])))
    heads, mixed, lse, query_all, kv_all, kv_peer_all = attend_heads(
        numbers, query, kv, held(kv_peer)
    )
    close(e2, near_outs[3], heads)

    swapped = to_chips(held(heads))
    near_gate = x_swap(held(w_gate))
    out_rows = call(
        out_kernel,
        "stack_out",
        (((CHIPS * 2 * nq, width), low),),
        own_outs + near_outs[:3] + [held(near_outs[3])],
        far=range(8),
    )[0]
    far_ffn = [core_swap(held(w_gate)), core_swap(held(w_up)), core_swap(held(w_down))]
    close(swapped, near_gate, out_rows, far_ffn)

    e3 = outer_ring.step(3, *ended[-1])
    out_rows_peer = core_swap(held(out_rows))
    across_ffn = [core_swap(held(near_gate))]
    near_up = x_swap(held(w_up))
    middle, normed_two, attended, w_out = call(
        join_kernel,
        "join",
        (
            ((TOK, width), full),
            ((TOK, width), low),
            ((TOK, width), low),
            ((width, width), low),
        ),
        (held(swapped), out_rows, out_rows_peer, block, gain_two),
        scratch=[pltpu.VMEM((width, TOK), low)],
        far=(3,),
        far_out=(0, 2, 3),
    )
    close(e3, normed_two, across_ffn, near_up)

    normed_ring = Gather(held(normed_two))
    fed = []

    def ffn_group(n):
        group = GROUPS[n]
        if len(group) > 1:
            blocks, outers = ([ring.found[j] for j in group] for ring in (normed_ring, outer_ring))
        else:
            blocks, outers = (list(ring.found[group[0]]) for ring in (normed_ring, outer_ring))
        blocks[0] = held(blocks[0])
        fed.append(ffn(blocks, outers, w_gu, w_dn))
        return fed[-1][3]

    h1 = normed_ring.step(1)
    e4 = outer_ring.step(4, *ended[-1])
    near_down = x_swap(held(w_down))
    close(h1, e4, near_down)

    h2 = normed_ring.step(2, *ended[-1])
    across_ffn += [core_swap(held(near_up)), core_swap(held(near_down))]
    w_gu, w_dn = call(
        hidden_kernel,
        "hidden_rows",
        (((4 * units, width), low), ((2 * units, width), low)),
        (w_gate, w_up, w_down, near_gate, near_up, near_down, *far_ffn, *across_ffn),
        far=range(12),
    )
    close(h2, w_gu)

    h3 = normed_ring.step(3, *ended[-1])
    close(h3, ffn_group(0), ffn_group(1))

    h4 = normed_ring.step(4, *ended[-1])
    close(h4, ffn_group(2))

    ffn_group(3)

    def stored(terms, name, far=()):
        def make(number, up, down):
            if number == 1:
                return terms[3:]
            begin = 1 if number == 4 else 0
            part = terms[4 - number]
            return call(
                add_kernel,
                name,
                leaving(width),
                (part, part, up, down),
                far=far,
                windows={0: (TOK, begin), 1: (TOK, begin + 1)},
            )

        return make

    back_ring = Scatter(stored([part[4] for part in fed[:3]] + list(fed[3][4:]), "back_add"))
    close(back_ring.step(1))

    d2 = back_ring.step(2, *ended[-1])
    arrays = [part[n] for n in range(4) for part in fed]
    arrays[0] = held(arrays[0])
    sums = call(
        functools.partial(grads_kernel, len(GROUPS)),
        "ffn_grads",
        [((2 * units, width), full), ((units, width), full)] * 2 + [((CHIPS * TOK, 2 * units), low)],
        arrays,
        scratch=[
            pltpu.VMEM((CHIPS * TOK, width), low),
            pltpu.VMEM((CHIPS * TOK, 4 * units), low),
        ],
        far_out=(4,),
    )
    close(d2, sums[2])

    d3 = back_ring.step(3, *ended[-1])
    others = [core_swap(held(value)) for value in sums[2:4]]
    branch = call(
        branch_kernel,
        "branch",
        [((len(group) * TOK, width), full) for group in GROUPS[:3]] + leaving(width, TOK // 2),
        (held(sums[4]), w_dn),
        far_out=(0, 1, 2),
    )
    close(d3, others, branch[-1])

    d4 = back_ring.step(4, *ended[-1])
    kept = call(
        owners_kernel,
        "ffn_owners",
        [((count, width), full)] * 3 + [((count, width), low)] * 3,
        (*sums[:2], held(others[0]), others[1]),
        far_out=(0, 1, 2),
    )
    near_grads = [x_swap(kept[3])]
    close(d4, near_grads)

    branch_ring = Scatter(stored(branch, "branch_add", (0, 1)))
    z1 = branch_ring.step(1, *ended[-1])
    grad_middle, grad_branch, grad_heads, second_gain_grad = call(
        turn_kernel,
        "turn",
        (
            ((TOK, width), full),
            ((TOK, width), low),
            ((CHIPS, PAIR, TOK), low),
            ((1, width), full),
        ),
        (fed[0][4], *d4, middle, outer, gain_two, w_out),
        far=(3, 4, 6),
        far_out=(0,),
        windows={0: (TOK, 0)},
    )
    close(z1, grad_heads)

    grad_heads = to_chips(held(grad_heads))
    z2 = branch_ring.step(2, *ended[-1])
    near_grads.append(x_swap(held(kept[4])))
    keep, give = call(
        outer_kernel,
        "outer",
        (((CHIPS, 2 * nq, width), low), ((CHIPS, 2 * nq, width), low)),
        (held(grad_branch), attended),
        far=(1,),
        far_out=(0,),
        scratch=[pltpu.VMEM((width, width), full)],
    )
    close(grad_heads, z2, near_grads[1], give)

    z3 = branch_ring.step(3, *ended[-1])
    other = core_swap(held(give))
    grad_query, grad_own, grad_peer = attend_back(
        numbers, query_all, kv_all, kv_peer_all, held(grad_heads), mixed, lse, cosine, sine
    )
    close(z3, other, grad_query)

    z4 = branch_ring.step(4, *ended[-1])
    second = call(
        settle_kernel,
        "settle",
        (((CHIPS * 2 * nq, width), low),),
        (keep, held(other)),
        far=(0,),
    )[0]
    joined, *leave = call(
        spread_kernel,
        "spread",
        [((CHIPS * TOK, 4 * LANES), low)] + leaving(width, TOK // 2) + leaving(width, nq),
        (grad_query, grad_own, core_swap(held(grad_peer)), cosine, sine, w_heads, second),
        far=(3, 4, 5),
    )
    near_grads.append(x_swap(held(kept[5])))
    close(z4, leave, near_grads[2])

    def last_terms(number, up, down):
        if number == 1:
            return leave[:2]
        begin = STEP_ROWS[number] // TOK
        return call(
            product_kernel,
            "last_terms",
            leaving(width),
            (joined, joined, w_heads, up, down),
            far=(0, 1, 2),
            windows={0: (TOK, begin), 1: (TOK, begin + 1)},
        )

    def out_terms(number, up, down):
        if number == 1:
            return leave[2:]
        begin = STEP_ROWS[number] // TOK
        return call(
            rows_kernel,
            "out_terms",
            leaving(width, 2 * nq),
            (second, second, up, down),
            far=(0, 1),
            windows={0: (2 * nq, begin), 1: (2 * nq, begin + 1)},
        )

    grad_ring = Scatter(out_terms)
    last_ring = Scatter(last_terms)
    t1 = last_ring.step(1, *ended[-1])
    g1 = grad_ring.step(1, *ended[-1])
    mine, send, gain_grads = call(
        heads_grad_kernel,
        "heads_grad",
        (((2, HD, width), full), ((2, HD, width), full), ((2, width), full)),
        (held(joined), w_heads, gain_one, second_gain_grad, normed),
        scratch=[pltpu.VMEM((4 * LANES, width), full)],
        far=range(1, 5),
    )
    t2 = last_ring.step(2)
    g2 = grad_ring.step(2)
    other = core_swap(send)
    result = call(
        result_kernel,
        "result",
        (((TOK, width), low),),
        (branch[0], after(z4[0], *t1), z4[1], middle),
        far=(0, 3),
        far_out=(0,),
        windows={0: (TOK, 0)},
    )[0]
    t3 = last_ring.step(3)
    g3 = grad_ring.step(3)
    mine = mine + other
    heads_grad = mine[0] + x_swap(mine[1].astype(low)).astype(full)
    t4 = last_ring.step(4)
    g4 = grad_ring.step(4)
    gain_grads = after(gain_grads, *t2).reshape(2, CHIPS, 4 * nq)
    gain_grads = jnp.sum(to_chips(jnp.transpose(gain_grads, (1, 0, 2))), axis=0)
    ffn_grad = [own + after(other, *t2).astype(full) for own, other in zip(kept[:3], near_grads)]
    keep, give = call(
        owned_kernel,
        "owned",
        (((nq, width), full), ((nq, width), low)),
        (second, *g4),
        far=(0,),
        windows={0: (2 * nq, 0)},
    )
    output_grad = keep + x_swap(give).astype(full)
    gain_grads = gain_grads + core_swap(gain_grads)
    gain_grads = gain_grads + x_swap(gain_grads)
    gain_grads = lax.dynamic_slice_in_dim(gain_grads, (2 * core + side) * nq, nq, 1)
    grad_tokens = call(
        last_kernel,
        "last",
        (((TOK, width), full),),
        (joined, w_heads, *t4, block, grad_middle, gain_one),
        far=(0, 1, 4, 5),
        far_out=(0,),
        windows={0: (TOK, 0)},
    )[0]
    return (
        result[None],
        grad_tokens[None],
        gain_grads[0],
        gain_grads[1],
        heads_grad[:nq],
        heads_grad[nq : nq + nk],
        heads_grad[nq + nk :],
        output_grad,
        ffn_grad[0],
        ffn_grad[1],
        ffn_grad[2],
    )


def by_plane(mesh):
    return dict(mesh.shape) == {"blk": 2 * CHIPS, "fsdp": 2} and KVH == CHIPS


def solution(mesh):
    in_specs = (
        P("fsdp", "blk", None),
        P("fsdp", "blk", None),
        P("fsdp", None),
        P("fsdp", "blk"),
        P(("blk", "fsdp")),
        P(("blk", "fsdp")),
        P(("blk", "fsdp"), None),
        P(("blk", "fsdp"), None),
        P(("blk", "fsdp"), None),
        P(("blk", "fsdp"), None),
        P(("blk", "fsdp"), None),
        P(("blk", "fsdp"), None),
        P(("blk", "fsdp"), None),
    )
    out_specs = (
        P("fsdp", "blk", None),
        P("fsdp", "blk", None),
        P(("blk", "fsdp")),
        P(("blk", "fsdp")),
        P(("blk", "fsdp"), None),
        P(("blk", "fsdp"), None),
        P(("blk", "fsdp"), None),
        P(("blk", "fsdp"), None),
        P(("blk", "fsdp"), None),
        P(("blk", "fsdp"), None),
        P(("blk", "fsdp"), None),
    )
    body = plane_shards if by_plane(mesh) else shards
    return jax.shard_map(body, mesh=mesh, in_specs=in_specs, out_specs=out_specs, check_vma=False)
```

```python
import functools

import jax
import jax.numpy as jnp
from jax import lax
from jax.experimental import pallas as pl
from jax.experimental.pallas import tpu as pltpu
from jax.sharding import PartitionSpec as P

HEADS = 16
KVH = 8
HD = 96


EPS = 1e-05
ROPE_BASE = 100000.0
NEG = -1e30


def passed_along(block, axis, distance):
    devices = range(lax.axis_size(axis))
    route = [(i - distance, i) for i in devices if i - distance in devices]
    return lax.ppermute(block, axis, route)


def passed_along_2(x, axis, by):
    length = lax.axis_size(axis)
    return lax.ppermute(x, axis, [(i, (i + by) % length) for i in range(length)])


def product_t(left, right):
    return lax.dot_general(
        left, right, (((1,), (1,)), ((), ())), preferred_element_type=jnp.float32
    )


def product(left, right):
    return jnp.dot(left, right, preferred_element_type=jnp.float32)


def product_tn(left, right):
    return lax.dot_general(
        left, right, (((0,), (0,)), ((), ())), preferred_element_type=jnp.float32
    )


def rms_scale(values):
    return lax.rsqrt(jnp.mean(values * values, axis=-1, keepdims=True) + EPS)


def norm_back(grad, values, scale, gain):
    weighted = grad * gain
    inner = jnp.mean(weighted * values, axis=-1, keepdims=True)
    return (scale * weighted - values * scale**3 * inner, jnp.sum(grad * values * scale, axis=0))


def rotation(positions):
    half = HD // 2
    freqs = ROPE_BASE ** (-(jnp.arange(half, dtype=jnp.float32) * 2.0 / HD))
    angles = positions.astype(jnp.float32)[:, None] * freqs[None, :]
    return (jnp.cos(angles)[:, None, :], jnp.sin(angles)[:, None, :])


def rotate(values, cosine, sine, heads, sign):
    count = values.shape[0]
    split = values.reshape(count, heads, HD)
    half = HD // 2
    first = split[..., :half]
    second = split[..., half:]
    turned = jnp.concatenate(
        [first * cosine - sign * second * sine, second * cosine + sign * first * sine], axis=-1
    )
    return turned.reshape(count, heads * HD)


def block_mask(query_seg, query_idx, key_seg, key_idx):
    return (query_seg[:, None] == key_seg[None, :]) & (key_idx[None, :] <= query_idx[:, None])


def scores_of(queries, keys, allowed):
    raw = jnp.einsum("qhgd,khd->hgqk", queries, keys, preferred_element_type=jnp.float32) * HD ** (
        -0.5
    )
    return jnp.where(allowed[None, None], raw, NEG)


def key_blocks(keys_seen, values_seen, key_segs):
    total = keys_seen.shape[0]
    size = min(512, total)
    count = total // size
    return (
        keys_seen.reshape(count, size, KVH, HD),
        values_seen.reshape(count, size, KVH, HD),
        key_segs.reshape(count, size),
        jnp.arange(total, dtype=jnp.int32).reshape(count, size),
    )


def attend(queries, blocks, query_seg, query_idx):
    rows = queries.shape[0]
    groups = HEADS // KVH
    start = (
        jnp.full((KVH, groups, rows, 1), NEG, jnp.float32),
        jnp.zeros((KVH, groups, rows, 1), jnp.float32),
    )

    def stats_step(carry, block):
        keys, values, segs, idxs = block
        allowed = block_mask(query_seg, query_idx, segs, idxs)
        top, running = carry
        scores = scores_of(queries, keys, allowed)
        new_top = jnp.maximum(top, jnp.max(scores, axis=-1, keepdims=True))
        new_sum = running * jnp.exp(top - new_top) + jnp.sum(
            jnp.exp(scores - new_top), axis=-1, keepdims=True
        )
        return ((new_top, new_sum), None)

    (top, running), unused = lax.scan(stats_step, start, blocks)
    lse = top + jnp.log(running)

    def value_step(total_acc, block):
        keys, values, segs, idxs = block
        allowed = block_mask(query_seg, query_idx, segs, idxs)
        weights = jnp.exp(scores_of(queries, keys, allowed) - lse).astype(jnp.bfloat16)
        return (
            total_acc
            + jnp.einsum("hgqk,khd->qhgd", weights, values, preferred_element_type=jnp.float32),
            None,
        )

    mixed, unused = lax.scan(value_step, jnp.zeros((rows, KVH, groups, HD), jnp.float32), blocks)
    return (mixed, lse)


def cycle_back(queries, own_keys, own_values, key_segs, query_seg, query_idx, lse, grad_out, delta):
    rows = queries.shape[0]
    groups = HEADS // KVH
    scale = HD ** (-0.5)
    me = lax.axis_index("blk")
    count = lax.axis_size("blk")
    local = jnp.arange(rows, dtype=jnp.int32)

    def step(carry, turn):
        grad_q, key_blk, value_blk, grad_k, grad_v = carry
        anchor = (me - turn) % count
        begin = anchor * rows
        segs = lax.dynamic_slice_in_dim(key_segs, begin, rows)
        allowed = block_mask(query_seg, query_idx, segs, begin + local)
        acc_k = grad_k
        acc_v = grad_v
        probs = jnp.exp(scores_of(queries, key_blk, allowed) - lse)
        grad_probs = jnp.einsum(
            "qhgd,khd->hgqk", grad_out, value_blk, preferred_element_type=jnp.float32
        )
        grad_scores = (probs * (grad_probs - delta)).astype(jnp.bfloat16)
        new_acc = grad_q + jnp.einsum(
            "hgqk,khd->qhgd", grad_scores, key_blk, preferred_element_type=jnp.float32
        )
        new_k = (
            acc_k
            + jnp.einsum("hgqk,qhgd->khd", grad_scores, queries, preferred_element_type=jnp.float32)
            * scale
        )
        new_v = acc_v + jnp.einsum(
            "hgqk,qhgd->khd",
            probs.astype(jnp.bfloat16),
            grad_out,
            preferred_element_type=jnp.float32,
        )
        grad_k = new_k
        grad_v = new_v
        key_blk, value_blk = passed_along((key_blk, value_blk), "blk", 1)
        grad_k, grad_v = (
            passed_along_2(grad_k.astype(jnp.bfloat16), "blk", 1).astype(grad_k.dtype),
            passed_along_2(grad_v.astype(jnp.bfloat16), "blk", 1).astype(grad_v.dtype),
        )
        return ((new_acc, key_blk, value_blk, grad_k, grad_v), None)

    zero_kv = jnp.zeros((rows, KVH, HD), jnp.float32)
    start = (
        jnp.zeros((rows, KVH, groups, HD), jnp.float32),
        own_keys.reshape(rows, KVH, HD),
        own_values.reshape(rows, KVH, HD),
        zero_kv,
        zero_kv,
    )
    final, unused = lax.scan(step, start, jnp.arange(count, dtype=jnp.int32))
    grad_q, ignored_k, ignored_v, grad_k, grad_v = final
    return (grad_q * scale, grad_k.reshape(rows, KVH * HD), grad_v.reshape(rows, KVH * HD))


def fetch_attention(gain_attn, gain_ffn, w_query, w_key, w_value, w_output):
    return (
        lax.all_gather(gain_attn, ("blk", "fsdp"), axis=0, tiled=True),
        lax.all_gather(gain_ffn, ("blk", "fsdp"), axis=0, tiled=True),
        lax.all_gather(w_query, ("blk", "fsdp"), axis=0, tiled=True),
        lax.all_gather(w_key, ("blk", "fsdp"), axis=0, tiled=True),
        lax.all_gather(w_value, ("blk", "fsdp"), axis=0, tiled=True),
        lax.all_gather(w_output, ("blk", "fsdp"), axis=0, tiled=True),
    )


def fetch_ffn(w_gate, w_up, w_down):
    return (
        lax.all_gather(w_gate, ("blk", "fsdp"), axis=0, tiled=True),
        lax.all_gather(w_up, ("blk", "fsdp"), axis=0, tiled=True),
        lax.all_gather(w_down, ("blk", "fsdp"), axis=0, tiled=True),
    )


def shards(
    tokens,
    cotangent,
    segments,
    positions,
    gain_attn,
    gain_ffn,
    w_query,
    w_key,
    w_value,
    w_output,
    w_gate,
    w_up,
    w_down,
):
    rows = tokens.shape[1]
    groups = HEADS // KVH
    xin = tokens[0].astype(jnp.float32)
    offset = lax.axis_index("blk") * rows
    query_idx = offset + jnp.arange(rows, dtype=jnp.int32)
    key_segs = segments[0]
    query_seg = lax.dynamic_slice_in_dim(key_segs, offset, rows)
    cosine, sine = rotation(positions[0])
    gain_one, gain_two, query_all, key_all, value_all, output_all = fetch_attention(
        gain_attn, gain_ffn, w_query, w_key, w_value, w_output
    )
    first_gain = gain_one.astype(jnp.float32)
    second_gain = gain_two.astype(jnp.float32)
    first_scale = rms_scale(xin)
    normed = (xin * first_scale * first_gain).astype(jnp.bfloat16)
    queries = rotate(product_t(normed, query_all), cosine, sine, HEADS, 1.0).astype(jnp.bfloat16)
    keys = rotate(product_t(normed, key_all), cosine, sine, KVH, 1.0).astype(jnp.bfloat16)
    values = product_t(normed, value_all).astype(jnp.bfloat16)
    keys_seen, values_seen = (
        lax.all_gather(keys, "blk", axis=0, tiled=True),
        lax.all_gather(values, "blk", axis=0, tiled=True),
    )
    query_heads = queries.reshape(rows, KVH, groups, HD)
    mixed, lse = attend(
        query_heads, key_blocks(keys_seen, values_seen, key_segs), query_seg, query_idx
    )
    attended = mixed.reshape(rows, HEADS * HD).astype(jnp.bfloat16)
    middle = xin + product_t(attended, output_all)
    second_scale = rms_scale(middle)
    normed_two = (middle * second_scale * second_gain).astype(jnp.bfloat16)
    gate_rows, up_rows, down_rows = fetch_ffn(w_gate, w_up, w_down)
    gate = product_t(normed_two, gate_rows)
    up = product_t(normed_two, up_rows)
    sigma = jax.nn.sigmoid(gate)
    activated = gate * sigma
    hidden = (activated * up).astype(jnp.bfloat16)
    branch = product(hidden, down_rows)
    result = (middle + branch).astype(jnp.bfloat16)
    grad_in = cotangent[0]
    gate_rows, up_rows, down_rows = fetch_ffn(w_gate, w_up, w_down)
    grad_hidden = product_t(grad_in, down_rows)
    grad_gate = (grad_hidden * up * sigma * (1.0 + gate * (1.0 - sigma))).astype(jnp.bfloat16)
    grad_up = (grad_hidden * activated).astype(jnp.bfloat16)
    gate_grad = product_tn(grad_gate, normed_two)
    up_grad = product_tn(grad_up, normed_two)
    down_grad = product_tn(hidden, grad_in)
    grad_normed_two = product(grad_gate, gate_rows) + product(grad_up, up_rows)
    gate_grad, up_grad, down_grad = (
        lax.psum_scatter(gate_grad, ("blk", "fsdp"), scatter_dimension=0, tiled=True),
        lax.psum_scatter(up_grad, ("blk", "fsdp"), scatter_dimension=0, tiled=True),
        lax.psum_scatter(down_grad, ("blk", "fsdp"), scatter_dimension=0, tiled=True),
    )
    grad_middle_norm, second_gain_grad = norm_back(
        grad_normed_two, middle, second_scale, second_gain
    )
    grad_middle = grad_in.astype(jnp.float32) + grad_middle_norm
    grad_branch = grad_middle.astype(jnp.bfloat16)
    output_grad = product_tn(grad_branch, attended)
    grad_attended = product(grad_branch, output_all).astype(jnp.bfloat16)
    grad_heads = grad_attended.reshape(rows, KVH, groups, HD)
    delta = jnp.transpose(jnp.sum(grad_heads.astype(jnp.float32) * mixed, axis=-1), (1, 2, 0))[
        ..., None
    ]
    grad_q, grad_keys, grad_values = cycle_back(
        query_heads, keys, values, key_segs, query_seg, query_idx, lse, grad_heads, delta
    )
    grad_q_pre = rotate(grad_q.reshape(rows, HEADS * HD), cosine, sine, HEADS, -1.0).astype(
        jnp.bfloat16
    )
    grad_k_pre = rotate(grad_keys, cosine, sine, KVH, -1.0).astype(jnp.bfloat16)
    grad_v = grad_values.astype(jnp.bfloat16)
    query_grad = product_tn(grad_q_pre, normed)
    key_grad = product_tn(grad_k_pre, normed)
    value_grad = product_tn(grad_v, normed)
    grad_normed = (
        product(grad_q_pre, query_all) + product(grad_k_pre, key_all) + product(grad_v, value_all)
    )
    grad_x_norm, first_gain_grad = norm_back(grad_normed, xin, first_scale, first_gain)
    grad_tokens = grad_middle + grad_x_norm
    first_gain_grad, second_gain_grad, query_grad, key_grad, value_grad, output_grad = (
        lax.psum_scatter(first_gain_grad, ("blk", "fsdp"), scatter_dimension=0, tiled=True),
        lax.psum_scatter(second_gain_grad, ("blk", "fsdp"), scatter_dimension=0, tiled=True),
        lax.psum_scatter(query_grad, ("blk", "fsdp"), scatter_dimension=0, tiled=True),
        lax.psum_scatter(key_grad, ("blk", "fsdp"), scatter_dimension=0, tiled=True),
        lax.psum_scatter(value_grad, ("blk", "fsdp"), scatter_dimension=0, tiled=True),
        lax.psum_scatter(output_grad, ("blk", "fsdp"), scatter_dimension=0, tiled=True),
    )
    return (
        result[None],
        grad_tokens[None],
        first_gain_grad,
        second_gain_grad,
        query_grad,
        key_grad,
        value_grad,
        output_grad,
        gate_grad,
        up_grad,
        down_grad,
    )


CHIPS = 8
TOK = 128
PAIR = 2 * HD
LANES = 128
VMEM_LIMIT = 32 << 20
LOG2E = 1.4426950408889634
RING = (0, 2, 4, 6, 7, 5, 3, 1)
SAME_CORE = [[2 * c + core for c in range(CHIPS)] for core in range(2)]


def ring_route(step):
    return [
        (RING[k] * 2 + core, RING[(k + step) % CHIPS] * 2 + core)
        for k in range(CHIPS)
        for core in range(2)
    ]


def ring_up(value):
    return lax.ppermute(value, "blk", ring_route(1))


def ring_down(value):
    return lax.ppermute(value, "blk", ring_route(-1))


def flipped(value, bit):
    return lax.ppermute(value, "blk", [(i, i ^ bit) for i in range(2 * CHIPS)])


def core_swap(value):
    return flipped(value, 1)


def x_swap(value):
    return lax.ppermute(value, "fsdp", [(0, 1), (1, 0)])


def tie(values, deps):
    deps = [d for d in deps if d is not None]
    if not deps:
        return tuple(values)
    return lax.optimization_barrier((tuple(values), tuple(deps)))[0]


def after(value, *deps):
    return tie((value,), deps)[0]


class Gather:
    def __init__(self, block):
        self.found = [None] * CHIPS
        self.found[0] = self.up = self.down = block

    def step(self, number, *deps):
        self.up, self.down = tie((self.up, self.down), deps)
        if number < CHIPS // 2:
            self.up = ring_up(self.up)
            self.down = ring_down(self.down)
            self.found[CHIPS - number] = self.up
            self.found[number] = self.down
        else:
            half = self.up.shape[0] // 2
            self.up = ring_up(self.up[:half])
            self.down = ring_down(self.down[half:])
            self.found[number] = (self.up, self.down)
        return self.up, self.down


class Scatter:
    def __init__(self, make):
        self.make = make
        self.up = self.down = None

    def step(self, number, *deps):
        up, down = tie(self.make(number, self.up, self.down), deps)
        self.up = ring_up(up)
        self.down = ring_down(down)
        return self.up, self.down


def dot_nt(left, right):
    return lax.dot_general(
        left, right, (((1,), (1,)), ((), ())), preferred_element_type=jnp.float32
    )


def dot_nn(left, right):
    return lax.dot_general(
        left, right, (((1,), (0,)), ((), ())), preferred_element_type=jnp.float32
    )


GROUPS = ((0, 1, 7), (2, 6), (3, 5), (4,))
ARRIVAL = tuple(j for group in GROUPS for j in group)


def whole(shape):
    return pl.BlockSpec(shape, lambda i: (0,) * len(shape), pipeline_mode=pl.Buffered(1))


def window(rows, nth, width):
    return pl.BlockSpec((rows, width), lambda i: (nth, 0), pipeline_mode=pl.Buffered(1))


def call(kernel, name, outs, ins, scratch=(), far=(), far_out=(), windows={}):
    shapes = []
    for n, (shape, dtype) in enumerate(outs):
        make = pltpu.HBM if n in far_out else jax.ShapeDtypeStruct
        shapes.append(make(shape, dtype))
    ins = list(ins)
    for n in far:
        ins[n] = pltpu.with_memory_space_constraint(ins[n], pltpu.HBM)
    return pl.pallas_call(
        kernel,
        grid=(1,),
        out_shape=tuple(shapes),
        in_specs=[
            window(*windows[n], value.shape[1]) if n in windows else whole(value.shape)
            for n, value in enumerate(ins)
        ],
        out_specs=tuple(whole(shape) for shape, _ in outs),
        scratch_shapes=scratch,
        compiler_params=pltpu.CompilerParams(vmem_limit_bytes=VMEM_LIMIT),
        cost_estimate=pl.CostEstimate(flops=0, bytes_accessed=0, transcendentals=0),
        name=name,
    )(*ins)


def dot_tn(left, right):
    return lax.dot_general(
        left, right, (((0,), (0,)), ((), ())), preferred_element_type=jnp.float32
    )


def own_place():
    index = lax.axis_index("blk")
    chip = lax.div(index, 2)
    half = lax.div(chip, 2)
    spot = jnp.where(lax.rem(chip, 2) == 0, half, CHIPS - 1 - half)
    return lax.rem(index, 2), lax.axis_index("fsdp"), chip, spot


def arriving_chip(nth, spot):
    at = lax.rem(spot + ARRIVAL[nth], CHIPS)
    return jnp.where(at < CHIPS // 2, 2 * at, 2 * CHIPS - 1 - 2 * at)


def arrival_of(chip, spot):
    away = lax.rem(RING.index(chip) - spot + CHIPS, CHIPS)
    late = jnp.where(away <= CHIPS // 2, 2 * away - 1, 2 * (CHIPS - away))
    return jnp.where(away == 0, 0, late)


def heads_kernel(own, near, far, across, out):
    nq = HD // 2
    nk = HD // 4
    half = LANES // 2
    own_core, own_side, _, _ = own_place()
    out[...] = jnp.zeros_like(out)
    for core in range(2):
        for side in range(2):

            @pl.when((own_core == core) & (own_side == side))
            def _():
                for piece, c, f in (
                    (own, core, side),
                    (near, core, 1 - side),
                    (far, 1 - core, side),
                    (across, 1 - core, 1 - side),
                ):
                    at = c * LANES + f * half
                    out[at : at + nq] = piece[:nq]
                    at = 2 * LANES + c * half + f * nk
                    out[at : at + nk] = piece[nq : nq + nk]
                    at = 3 * LANES + (2 * c + f) * nk
                    out[at : at + nk] = piece[nq + nk :]


def stack_kernel(*refs):
    out = refs[-1]
    at = 0
    for piece in refs[:-1]:
        out[at : at + piece.shape[0]] = piece[...]
        at += piece.shape[0]


def out_kernel(*refs):
    own, near, out = refs[:4], refs[4:8], refs[8]
    side = own_place()[1]
    rows = own[0].shape[0] // 2
    for n, j in enumerate(ARRIVAL):
        away = min(j, CHIPS - j)
        which = 3 if away in (0, CHIPS // 2) else away - 1
        here = slice(0, rows) if j in (0, 1, 2, 3) else slice(rows, 2 * rows)
        for source, f in ((own, side), (near, 1 - side)):
            at = pl.multiple_of((2 * n + f) * rows, rows)
            out[pl.ds(at, rows), :] = source[which][here, :]


def hidden_kernel(*refs):
    gate_up, down = refs[-2:]
    count = refs[0].shape[0]
    for n in range(4):
        gate, up, out = refs[3 * n : 3 * n + 3]
        start = (n // 2) * 4 * count + (n % 2) * count
        gate_up[start : start + count] = gate[...]
        gate_up[start + 2 * count : start + 3 * count] = up[...]
        down[n * count : (n + 1) * count] = out[...]


def project_kernel(*refs):
    blocks = refs[: CHIPS + 1]
    gain, weight, cosine, sine, normed_out, query_out, kv_out = refs[CHIPS + 1 :]
    for j in range(CHIPS):
        if j < CHIPS - 1:
            values = blocks[j][-TOK:].astype(jnp.float32)
        else:
            late = blocks[CHIPS][...].astype(jnp.float32)
            values = blocks[j][-(TOK - late.shape[0]) :].astype(jnp.float32)
            values = jnp.concatenate([values, late], axis=0)
        scale = lax.rsqrt(jnp.mean(values * values, axis=-1, keepdims=True) + EPS)
        normed_out[j * TOK : (j + 1) * TOK, :] = (values * scale * gain[...]).astype(jnp.bfloat16)
    pre = dot_nt(normed_out[...], weight[...])
    for head in range(3):
        part = pre[:, head * LANES : (head + 1) * LANES]
        turned = part * cosine[...] + pltpu.roll(part, LANES // 2, 1) * sine[...]
        if head < 2:
            query_out[:, head * LANES : (head + 1) * LANES] = turned.astype(jnp.bfloat16)
        else:
            kv_out[:, :LANES] = turned.astype(jnp.bfloat16)
    kv_out[:, LANES:] = pre[:, 3 * LANES :].astype(jnp.bfloat16)


def project(blocks, *arrays):
    rows = CHIPS * TOK
    width = blocks[0].shape[1]
    low = jnp.bfloat16
    assert len(blocks) == CHIPS + 1
    return call(
        project_kernel,
        "project",
        (((rows, width), low), ((rows, 2 * LANES), low), ((rows, 2 * LANES), low)),
        (*blocks, *arrays),
        far=range(CHIPS + 1),
        far_out=(0,),
    )


def key_index(core, count):
    row = lax.broadcasted_iota(jnp.int32, (count, 1), 0)
    return (row // TOK) * (2 * TOK) + core * TOK + row % TOK


def query_index(core, chip):
    lane = lax.broadcasted_iota(jnp.int32, (1, 2 * TOK), 1)
    return lane % TOK + (2 * chip + core) * TOK


def sequence_starts(segments):
    numbers = segments[...]
    starts = []
    for number in range(1, 4):
        below = (numbers < number).astype(jnp.float32)
        total = jnp.sum(jnp.sum(below, axis=1, keepdims=True), axis=0, keepdims=True)
        starts.append(total.astype(jnp.int32))
    return starts


def first_index(starts, at):
    first = jnp.zeros_like(at)
    for start in starts:
        first = jnp.where(at >= start, start, first)
    return first


def only_allowed(values, keys_at, at, first, chip):
    if chip in (0, CHIPS - 1):
        return jnp.where((keys_at <= at) & (keys_at >= first), values, NEG)
    low = jnp.where(keys_at[:TOK] >= first, values[:TOK], NEG)
    high = jnp.where(keys_at[chip * TOK :] <= at, values[chip * TOK :], NEG)
    parts = [low, values[TOK : chip * TOK], high] if chip > 1 else [low, high]
    return jnp.concatenate(parts, axis=0)


def both_heads(ref, rows):
    return jnp.concatenate([ref[rows, :LANES], ref[rows, LANES:]], axis=0)


def attend_kernel(
    segments, query_in, own_in, peer_in, attended, mixed, lse, query, own, peer
):
    core, _, _, spot = own_place()
    starts = sequence_starts(segments)
    factor = HD ** (-0.5) * LOG2E
    for source, target in ((query_in, query), (own_in, own), (peer_in, peer)):
        for chip in range(CHIPS):
            rows = pl.ds(pl.multiple_of(arrival_of(chip, spot) * TOK, TOK), TOK)
            target[chip * TOK : (chip + 1) * TOK, :] = source[rows, :]
    sides = ((own, core), (peer, 1 - core))
    values_t = [jnp.transpose(kv[:, LANES:]) for kv, _ in sides]
    for chip in range(CHIPS):
        count = (chip + 1) * TOK
        rows = slice(chip * TOK, count)
        queries = both_heads(query, rows)
        at = query_index(core, chip)
        first = first_index(starts, at)
        scores = []
        for kv, side in sides:
            raw = dot_nt(kv[:count, :LANES], queries) * factor
            scores.append(only_allowed(raw, key_index(side, count), at, first, chip))
        top = jnp.maximum(
            jnp.max(scores[0], axis=0, keepdims=True), jnp.max(scores[1], axis=0, keepdims=True)
        )
        weights = [jnp.exp2(part - top) for part in scores]
        total = jnp.sum(weights[0], axis=0, keepdims=True) + jnp.sum(
            weights[1], axis=0, keepdims=True
        )
        mix = dot_nn(values_t[0][:, :count], weights[0].astype(jnp.bfloat16)) + dot_nn(
            values_t[1][:, :count], weights[1].astype(jnp.bfloat16)
        )
        mix = mix / total
        mixed[chip] = mix
        lse[chip] = top + jnp.log2(total)
        attended[chip, :HD] = mix[:HD, :TOK].astype(jnp.bfloat16)
        attended[chip, HD:] = mix[:HD, TOK:].astype(jnp.bfloat16)


def attend_heads(segments, query, own, peer):
    tokens = CHIPS * TOK
    low = jnp.bfloat16
    return call(
        attend_kernel,
        "attend",
        (
            ((CHIPS, PAIR, TOK), low),
            ((CHIPS, LANES, 2 * TOK), jnp.float32),
            ((CHIPS, 1, 2 * TOK), jnp.float32),
            ((tokens, 2 * LANES), low),
            ((tokens, 2 * LANES), low),
            ((tokens, 2 * LANES), low),
        ),
        (segments, query, own, peer),
        far_out=(1, 2, 3, 4, 5),
    )


def attend_back_kernel(
    segments, query, own, peer, grad_out, mixed, lse, cosine, sine,
    grad_query, own_out, peer_out, grad_own, grad_peer,
):
    core, _, _, spot = own_place()
    starts = sequence_starts(segments)
    scale = HD ** (-0.5)
    factor = scale * LOG2E
    sides = ((own, core, grad_own), (peer, 1 - core, grad_peer))
    keys_t = [jnp.transpose(kv[:, :LANES]) for kv, _, _ in sides]
    grad_own[...] = jnp.zeros_like(grad_own)
    grad_peer[...] = jnp.zeros_like(grad_peer)
    pad = jnp.zeros((LANES - HD, 2 * TOK), jnp.bfloat16)
    for chip in range(CHIPS):
        count = (chip + 1) * TOK
        rows = slice(chip * TOK, count)
        kept = pl.ds(pl.multiple_of(arrival_of(chip, spot) * TOK, TOK), TOK)
        queries = both_heads(query, rows)
        grads = jnp.concatenate(
            [
                jnp.concatenate([grad_out[chip, :HD], grad_out[chip, HD:]], axis=1),
                pad,
            ],
            axis=0,
        )
        delta = jnp.sum(grads.astype(jnp.float32) * mixed[chip], axis=0, keepdims=True)
        at = query_index(core, chip)
        first = first_index(starts, at)
        level = lse[chip]
        grad_q = jnp.zeros((LANES, 2 * TOK), jnp.float32)
        for (kv, side, grad_kv), key_t in zip(sides, keys_t):
            raw = dot_nt(kv[:count, :LANES], queries) * factor
            keys_at = key_index(side, count)
            probs = jnp.exp2(only_allowed(raw - level, keys_at, at, first, chip))
            grad_probs = dot_nn(kv[:count, LANES:], grads)
            grad_scores = (probs * (grad_probs - delta)).astype(jnp.bfloat16)
            grad_kv[:count, LANES:] += dot_nt(probs.astype(jnp.bfloat16), grads)
            grad_kv[:count, :LANES] += dot_nn(grad_scores, queries)
            grad_q += dot_nn(key_t[:, :count], grad_scores)
        grad_q = jnp.transpose(grad_q) * scale
        cos = cosine[kept, :]
        sin = sine[kept, :]
        for head in range(2):
            part = grad_q[head * TOK : (head + 1) * TOK]
            turned = part * cos - pltpu.roll(part, LANES // 2, 1) * sin
            grad_query[kept, head * LANES : (head + 1) * LANES] = turned.astype(jnp.bfloat16)
    for chip in range(CHIPS):
        rows = slice(chip * TOK, (chip + 1) * TOK)
        kept = pl.ds(pl.multiple_of(arrival_of(chip, spot) * TOK, TOK), TOK)
        for grad_kv, out in ((grad_own, own_out), (grad_peer, peer_out)):
            out[kept, :LANES] = grad_kv[rows, :LANES] * scale
            out[kept, LANES:] = grad_kv[rows, LANES:]


def attend_back(segments, *arrays):
    tokens = CHIPS * TOK
    full = jnp.float32
    return call(
        attend_back_kernel,
        "attend_back",
        (
            ((tokens, 2 * LANES), jnp.bfloat16),
            ((tokens, 2 * LANES), full),
            ((tokens, 2 * LANES), full),
        ),
        (segments, *arrays),
        scratch=[pltpu.VMEM((tokens, 2 * LANES), full)] * 2,
        far=(1, 2, 3, 5, 6, 7, 8),
    )


def join_kernel(heads, *refs):
    weights = refs[:2]
    block, gain, middle_out, normed_out, attended_out, weight_out, held = refs[2:]
    core, _, _, spot = own_place()
    size = weights[0].shape[0] // CHIPS
    for n in range(CHIPS):
        for piece, side in zip(weights, (core, 1 - core)):
            at = pl.multiple_of((2 * arriving_chip(n, spot) + side) * size, size)
            weight_out[pl.ds(at, size), :] = piece[n * size : (n + 1) * size, :]
    for chip in range(CHIPS):
        held[chip * PAIR : (chip + 1) * PAIR, :] = heads[chip]
    attended_out[...] = jnp.transpose(held[...])
    middle = block[...].astype(jnp.float32) + dot_nt(attended_out[...], weight_out[...])
    middle_out[...] = middle
    scale = lax.rsqrt(jnp.mean(middle * middle, axis=-1, keepdims=True) + EPS)
    normed_out[...] = (middle * scale * gain[...]).astype(jnp.bfloat16)


def ffn_kernel(number, *refs):
    blocks = refs[:number]
    outers = refs[number : 2 * number]
    gate_up, down_rows = refs[2 * number : 2 * number + 2]
    rows, outer_rows, hidden, grad_gu = refs[2 * number + 2 : 2 * number + 6]
    wide = hidden.shape[1] // 2
    size = rows.shape[0] // number
    for n in range(number):
        rows[n * size : (n + 1) * size, :] = blocks[n][...]
        outer_rows[n * size : (n + 1) * size, :] = outers[n][...]
    grads = dot_nt(outer_rows[...], down_rows[...])
    pre = dot_nt(rows[...], gate_up[...])
    for part in range(2):
        at = part * 2 * wide
        gate = pre[:, at : at + wide]
        up = pre[:, at + wide : at + 2 * wide]
        back = grads[:, part * wide : (part + 1) * wide]
        sigma = 1.0 / (1.0 + jnp.exp(-gate))
        active = gate * sigma
        hidden[:, part * wide : (part + 1) * wide] = (active * up).astype(jnp.bfloat16)
        slope = back * up * sigma * (1.0 + gate * (1.0 - sigma))
        grad_gu[:, at : at + wide] = slope.astype(jnp.bfloat16)
        grad_gu[:, at + wide : at + 2 * wide] = (back * active).astype(jnp.bfloat16)
    outs = refs[2 * number + 6 :]
    back = dot_nn(grad_gu[...], gate_up[...])
    if len(outs) == 1:
        outs[0][...] = back
    else:
        outs[0][...] = back[: TOK // 2].astype(jnp.bfloat16)
        outs[1][...] = back[TOK // 2 :].astype(jnp.bfloat16)


def ffn(blocks, outers, gate_up, down):
    number = len(blocks)
    rows = number * blocks[0].shape[0]
    width = blocks[0].shape[1]
    units = down.shape[0]
    low = jnp.bfloat16
    if rows > TOK:
        terms = [((rows, width), jnp.float32)]
    else:
        terms = [((TOK // 2, width), low)] * 2
    return call(
        functools.partial(ffn_kernel, number),
        "ffn",
        [((rows, width), low)] * 2 + [((rows, units), low), ((rows, 2 * units), low)] + terms,
        (*blocks, *outers, gate_up, down),
    )


def add_terms(up_term, down_term, up, down, up_out, down_out):
    size = up.shape[0]
    rest = up_out.shape[0] - size
    low = jnp.bfloat16
    full = jnp.float32
    up_out[:size] = (up_term[:size] + up.astype(full)).astype(low)
    down_out[rest:] = (down_term[rest:] + down.astype(full)).astype(low)
    if rest:
        up_out[size:] = up_term[size:].astype(low)
        down_out[:rest] = down_term[:rest].astype(low)


def add_kernel(up_term, down_term, up, down, up_out, down_out):
    add_terms(up_term, down_term, up[...], down[...], up_out, down_out)


def leaving(width, rows=TOK):
    return [((rows, width), jnp.bfloat16)] * 2


STEP_ROWS = {1: 7 * TOK, 2: 5 * TOK, 3: 3 * TOK, 4: TOK}


def branch_kernel(hidden, down_rows, *outs):
    found = dot_nn(hidden[...], down_rows[...])
    at = 0
    for out in outs[:-2]:
        out[...] = found[at : at + out.shape[0]]
        at += out.shape[0]
    outs[-2][...] = found[at : at + TOK // 2].astype(jnp.bfloat16)
    outs[-1][...] = found[at + TOK // 2 :].astype(jnp.bfloat16)


def result_kernel(terms, up, down, middle, out):
    full = jnp.float32
    branch = terms[...] + (up[...].astype(full) + down[...].astype(full))
    out[...] = (middle[...] + branch).astype(jnp.bfloat16)


def grads_kernel(number, *refs):
    rows_in, outer_in, hidden_in, grads_in = (refs[n * number : (n + 1) * number] for n in range(4))
    keep_gu, keep_down, send_gu, send_down, hidden, rows, grads = refs[4 * number :]
    at = 0
    for block, hid, grad in zip(rows_in, hidden_in, grads_in):
        here = slice(at, at + block.shape[0])
        rows[here, :] = block[...]
        hidden[here, :] = hid[...]
        grads[here, :] = grad[...]
        at += block.shape[0]
    half = keep_gu.shape[0]
    send_gu[...] = dot_tn(grads[:, half:], rows[...])
    keep_gu[...] = dot_tn(grads[:, :half], rows[...])
    at = 0
    for block in outer_in:
        rows[at : at + block.shape[0], :] = block[...]
        at += block.shape[0]
    half = keep_down.shape[0]
    send_down[...] = dot_tn(hidden[:, half:], rows[...])
    keep_down[...] = dot_tn(hidden[:, :half], rows[...])


def owners_kernel(keep_gu, keep_down, other_gu, other_down, *outs):
    count = outs[0].shape[0]
    for n, (value, other, at) in enumerate(
        ((keep_gu, other_gu, 0), (keep_gu, other_gu, 2 * count), (keep_down, other_down, 0))
    ):
        near = at + count
        outs[n][...] = value[at:near] + other[at:near]
        given = value[near : near + count] + other[near : near + count]
        outs[3 + n][...] = given.astype(jnp.bfloat16)


def turn_kernel(*refs):
    own, up, down, middle_ref, outer, gain, weight, middle_out, branch_out, heads, gain_out = refs
    grad = own[...] + (up[...].astype(jnp.float32) + down[...].astype(jnp.float32))
    middle = middle_ref[...]
    scale = lax.rsqrt(jnp.mean(middle * middle, axis=-1, keepdims=True) + EPS)
    weighted = grad * gain[...]
    inner = jnp.mean(weighted * middle, axis=-1, keepdims=True)
    gain_out[...] = jnp.sum(grad * middle * scale, axis=0, keepdims=True)
    total = outer[...].astype(jnp.float32) + (scale * weighted - middle * (scale**3 * inner))
    middle_out[...] = total
    branch = total.astype(jnp.bfloat16)
    branch_out[...] = branch
    back = jnp.transpose(dot_nn(branch, weight[...]).astype(jnp.bfloat16))
    for chip in range(CHIPS):
        heads[chip] = back[chip * PAIR : (chip + 1) * PAIR]


def outer_kernel(branch, attended, keep, give, held):
    held[...] = dot_tn(branch[...], attended[...])
    core = own_place()[0]
    size = keep.shape[1]
    for chip in range(CHIPS):
        at = pl.multiple_of((2 * chip + core) * size, size)
        keep[chip] = held[pl.ds(at, size), :].astype(jnp.bfloat16)
        at = pl.multiple_of((2 * chip + 1 - core) * size, size)
        give[chip] = held[pl.ds(at, size), :].astype(jnp.bfloat16)


def settle_kernel(keep, other, total):
    spot = own_place()[3]
    rows = keep.shape[1]
    for n in range(CHIPS):
        chip = arriving_chip(n, spot)
        found = keep[chip].astype(jnp.float32) + other[chip].astype(jnp.float32)
        total[n * rows : (n + 1) * rows] = found.astype(jnp.bfloat16)


def product_kernel(up_left, down_left, right, up, down, up_out, down_out):
    terms = dot_nn(jnp.concatenate([up_left[...], down_left[...]], axis=0), right[...])
    add_terms(terms[:TOK], terms[TOK:], up[...], down[...], up_out, down_out)


def rows_kernel(up_term, down_term, up, down, up_out, down_out):
    full = jnp.float32
    add_terms(
        up_term[...].astype(full), down_term[...].astype(full), up[...], down[...], up_out, down_out
    )


def spread_kernel(
    query, own, other, cosine, sine, weight, second, joined, up_out, down_out, up_rows, down_rows
):
    joined[:, : 2 * LANES] = query[...]
    total = own[...] + other[...]
    part = total[:, :LANES]
    turned = part * cosine[...] - pltpu.roll(part, LANES // 2, 1) * sine[...]
    joined[:, 2 * LANES : 3 * LANES] = turned.astype(jnp.bfloat16)
    joined[:, 3 * LANES :] = total[:, LANES:].astype(jnp.bfloat16)
    begin = STEP_ROWS[1]
    terms = dot_nn(joined[begin : begin + TOK], weight[...]).astype(jnp.bfloat16)
    up_out[...] = terms[: TOK // 2]
    down_out[...] = terms[TOK // 2 :]
    rows = second.shape[0] // CHIPS
    up_rows[...] = second[(CHIPS - 1) * rows : (CHIPS - 1) * rows + rows // 2]
    down_rows[...] = second[(CHIPS - 1) * rows + rows // 2 :]


def heads_grad_kernel(*refs):
    own_core, own_side, _, _ = own_place()
    joined, weight, gain, second, normed, mine, send, gains, grad = refs
    grad[...] = dot_tn(joined[...], normed[...])
    first = jnp.sum(grad[...] * weight[...].astype(jnp.float32), axis=0, keepdims=True) / gain[...]
    nq = HD // 2
    nk = HD // 4
    half = LANES // 2
    gains[:1] = first
    gains[1:] = second[...]
    for core in range(2):
        for side in range(2):

            @pl.when((own_core == core) & (own_side == side))
            def _():
                for c in range(2):
                    for f in range(2):
                        out = mine if c == core else send
                        which = 0 if f == side else 1
                        at = c * LANES + f * half
                        out[which, :nq] = grad[at : at + nq]
                        at = 2 * LANES + c * half + f * nk
                        out[which, nq : nq + nk] = grad[at : at + nk]
                        at = 3 * LANES + (2 * c + f) * nk
                        out[which, nq + nk :] = grad[at : at + nk]


def owned_kernel(second, up, down, keep, give):
    side = own_place()[1]
    rows = keep.shape[0]
    full = jnp.float32
    total = second[...].astype(full) + (up[...].astype(full) + down[...].astype(full))
    keep[...] = jnp.where(side == 0, total[:rows], total[rows:])
    give[...] = jnp.where(side == 0, total[rows:], total[:rows]).astype(jnp.bfloat16)


def last_kernel(joined, weight, up, down, block, middle, gain, out):
    grad = dot_nn(joined[...], weight[...])
    grad = grad + (up[...].astype(jnp.float32) + down[...].astype(jnp.float32))
    values = block[...].astype(jnp.float32)
    scale = lax.rsqrt(jnp.mean(values * values, axis=-1, keepdims=True) + EPS)
    weighted = grad * gain[...]
    inner = jnp.mean(weighted * values, axis=-1, keepdims=True)
    out[...] = middle[...] + (scale * weighted - values * (scale**3 * inner))


def plane_shards(
    tokens,
    cotangent,
    segments,
    positions,
    gain_attn,
    gain_ffn,
    w_query,
    w_key,
    w_value,
    w_output,
    w_gate,
    w_up,
    w_down,
):
    full = jnp.float32
    low = jnp.bfloat16
    block = tokens[0]
    outer = cotangent[0]
    width = block.shape[1]
    index = lax.axis_index("blk")
    side = lax.axis_index("fsdp")
    core = index % 2
    chip = index // 2
    spot = jnp.where(chip % 2 == 0, chip // 2, CHIPS - 1 - chip // 2)

    segs = segments[0]
    numbers = segs.reshape(2 * CHIPS, TOK)
    starts = [jnp.sum((segs < number).astype(jnp.int32)) for number in range(1, 4)]
    row = lax.broadcasted_iota(jnp.int32, (CHIPS * TOK, LANES), 0)
    nth = row >> 7
    away = jnp.where((nth & 1) == 1, (nth + 1) >> 1, CHIPS - (nth >> 1))
    at = (spot + away) & (CHIPS - 1)
    token = jnp.where(at < CHIPS // 2, 2 * at, 2 * CHIPS - 1 - 2 * at) * (2 * TOK)
    token = token + core * TOK + (row & (TOK - 1))
    first = jnp.zeros_like(token)
    for start in starts:
        first = jnp.where(token >= start, start, first)
    half = HD // 2
    freqs = ROPE_BASE ** (-(jnp.arange(half, dtype=full) * 2.0 / HD))
    spare = jnp.zeros((LANES // 2 - half,), full)
    both = jnp.concatenate([freqs, spare, freqs, spare])
    angles = (token - first).astype(full) * both[None, :]
    sign = jnp.where(jnp.arange(LANES) < LANES // 2, -1.0, 1.0).astype(full)
    cosine = jnp.cos(angles)
    sine = jnp.sin(angles) * sign[None, :]

    ended = [()]

    def held(value):
        return after(value, *ended[-1])

    def close(*results):
        flat = []
        for result in results:
            flat += list(result) if isinstance(result, (list, tuple)) else [result]
        ended.append(tuple(flat))

    def to_chips(value):
        return lax.all_to_all(
            value, "blk", split_axis=0, concat_axis=0, axis_index_groups=SAME_CORE, tiled=True
        )

    nq = w_query.shape[0]
    nk = w_key.shape[0]
    count = w_gate.shape[0]
    units = 2 * count

    def wider(vector, bit):
        other = flipped(vector, bit) if bit else x_swap(vector)
        return jnp.where(
            ((index & bit) if bit else side) == 0,
            jnp.concatenate([vector, other], axis=1),
            jnp.concatenate([other, vector], axis=1),
        )

    both = call(
        stack_kernel, "stack_tokens", (((nq + TOK, width), low),), (w_output, block), far=(0, 1)
    )[0]
    tokens_ring = Gather(both)
    x1 = tokens_ring.step(1)
    gains = wider(wider(jnp.stack([gain_attn, gain_ffn]), 0), 1)
    close(x1, gains, cosine, sine)

    x2 = tokens_ring.step(2, *ended[-1])
    packed = call(
        stack_kernel,
        "stack_heads",
        (((nq + 2 * nk, width), low),),
        (w_query, w_key, held(w_value)),
        far=range(3),
    )[0]
    near = x_swap(packed)
    far = core_swap(packed)
    gains = wider(held(gains), 2)
    close(x2, near, far, gains)

    def out_pair(first, second):
        return call(
            stack_kernel,
            "stack_pair",
            (((2 * nq, width), low),),
            (first, second),
            far=(0, 1),
            windows={0: (nq, 0), 1: (nq, 0)},
        )[0]

    found = tokens_ring.found
    x3 = tokens_ring.step(3, *ended[-1])
    across = core_swap(held(near))
    gains = wider(held(gains), 4)
    own_outs = [out_pair(held(found[1]), found[7])]
    near_outs = [x_swap(own_outs[0])]
    close(x3, across, gains, near_outs)

    x4 = tokens_ring.step(4, *ended[-1])
    w_heads = call(
        heads_kernel,
        "head_rows",
        (((4 * LANES, width), low),),
        (packed, near, far, held(across)),
        far=range(4),
    )[0]
    own_outs.append(out_pair(held(found[2]), found[6]))
    near_outs.append(x_swap(own_outs[1]))
    gains = wider(held(gains), 8).astype(full)
    gain_one = gains[:1]
    gain_two = gains[1:]
    close(x4, gains, w_heads, near_outs[1])

    outer_ring = Gather(held(outer))
    e1 = outer_ring.step(1)
    blocks = [found[j] for j in ARRIVAL[:-1]] + list(found[4])
    normed, query, kv = project(
        [held(blocks[0])] + blocks[1:], gain_one, w_heads, cosine, sine
    )
    own_outs.append(out_pair(held(found[3]), found[5]))
    near_outs.append(x_swap(own_outs[2]))
    own_outs.append(out_pair(held(found[0]), found[4][0]))
    close(e1, near_outs[2], kv, own_outs[3])

    kv_peer = core_swap(held(kv))
    close(kv_peer)

    e2 = outer_ring.step(2, *ended[-1])
    near_outs.append(x_swap(held(own_outs[3])))
    heads, mixed, lse, query_all, kv_all, kv_peer_all = attend_heads(
        numbers, query, kv, held(kv_peer)
    )
    close(e2, near_outs[3], heads)

    swapped = to_chips(held(heads))
    near_gate = x_swap(held(w_gate))
    out_rows = call(
        out_kernel,
        "stack_out",
        (((CHIPS * 2 * nq, width), low),),
        own_outs + near_outs[:3] + [held(near_outs[3])],
        far=range(8),
    )[0]
    far_ffn = [core_swap(held(w_gate)), core_swap(held(w_up)), core_swap(held(w_down))]
    close(swapped, near_gate, out_rows, far_ffn)

    e3 = outer_ring.step(3, *ended[-1])
    out_rows_peer = core_swap(held(out_rows))
    across_ffn = [core_swap(held(near_gate))]
    near_up = x_swap(held(w_up))
    middle, normed_two, attended, w_out = call(
        join_kernel,
        "join",
        (
            ((TOK, width), full),
            ((TOK, width), low),
            ((TOK, width), low),
            ((width, width), low),
        ),
        (held(swapped), out_rows, out_rows_peer, block, gain_two),
        scratch=[pltpu.VMEM((width, TOK), low)],
        far=(3,),
        far_out=(0, 2, 3),
    )
    close(e3, normed_two, across_ffn, near_up)

    normed_ring = Gather(held(normed_two))
    fed = []

    def ffn_group(n):
        group = GROUPS[n]
        if len(group) > 1:
            blocks, outers = ([ring.found[j] for j in group] for ring in (normed_ring, outer_ring))
        else:
            blocks, outers = (list(ring.found[group[0]]) for ring in (normed_ring, outer_ring))
        blocks[0] = held(blocks[0])
        fed.append(ffn(blocks, outers, w_gu, w_dn))
        return fed[-1][3]

    h1 = normed_ring.step(1)
    e4 = outer_ring.step(4, *ended[-1])
    near_down = x_swap(held(w_down))
    close(h1, e4, near_down)

    h2 = normed_ring.step(2, *ended[-1])
    across_ffn += [core_swap(held(near_up)), core_swap(held(near_down))]
    w_gu, w_dn = call(
        hidden_kernel,
        "hidden_rows",
        (((4 * units, width), low), ((2 * units, width), low)),
        (w_gate, w_up, w_down, near_gate, near_up, near_down, *far_ffn, *across_ffn),
        far=range(12),
    )
    close(h2, w_gu)

    h3 = normed_ring.step(3, *ended[-1])
    close(h3, ffn_group(0), ffn_group(1))

    h4 = normed_ring.step(4, *ended[-1])
    close(h4, ffn_group(2))

    ffn_group(3)

    def stored(terms, name, far=()):
        def make(number, up, down):
            if number == 1:
                return terms[3:]
            begin = 1 if number == 4 else 0
            part = terms[4 - number]
            return call(
                add_kernel,
                name,
                leaving(width),
                (part, part, up, down),
                far=far,
                windows={0: (TOK, begin), 1: (TOK, begin + 1)},
            )

        return make

    back_ring = Scatter(stored([part[4] for part in fed[:3]] + list(fed[3][4:]), "back_add"))
    close(back_ring.step(1))

    d2 = back_ring.step(2, *ended[-1])
    arrays = [part[n] for n in range(4) for part in fed]
    arrays[0] = held(arrays[0])
    sums = call(
        functools.partial(grads_kernel, len(GROUPS)),
        "ffn_grads",
        [((2 * units, width), full), ((units, width), full)] * 2 + [((CHIPS * TOK, 2 * units), low)],
        arrays,
        scratch=[
            pltpu.VMEM((CHIPS * TOK, width), low),
            pltpu.VMEM((CHIPS * TOK, 4 * units), low),
        ],
        far_out=(4,),
    )
    close(d2, sums[2])

    d3 = back_ring.step(3, *ended[-1])
    others = [core_swap(held(value)) for value in sums[2:4]]
    branch = call(
        branch_kernel,
        "branch",
        [((len(group) * TOK, width), full) for group in GROUPS[:3]] + leaving(width, TOK // 2),
        (held(sums[4]), w_dn),
        far_out=(0, 1, 2),
    )
    close(d3, others, branch[-1])

    d4 = back_ring.step(4, *ended[-1])
    kept = call(
        owners_kernel,
        "ffn_owners",
        [((count, width), full)] * 3 + [((count, width), low)] * 3,
        (*sums[:2], held(others[0]), others[1]),
        far_out=(0, 1, 2),
    )
    near_grads = [x_swap(kept[3])]
    close(d4, near_grads)

    branch_ring = Scatter(stored(branch, "branch_add", (0, 1)))
    z1 = branch_ring.step(1, *ended[-1])
    grad_middle, grad_branch, grad_heads, second_gain_grad = call(
        turn_kernel,
        "turn",
        (
            ((TOK, width), full),
            ((TOK, width), low),
            ((CHIPS, PAIR, TOK), low),
            ((1, width), full),
        ),
        (fed[0][4], *d4, middle, outer, gain_two, w_out),
        far=(3, 4, 6),
        far_out=(0,),
        windows={0: (TOK, 0)},
    )
    close(z1, grad_heads)

    grad_heads = to_chips(held(grad_heads))
    z2 = branch_ring.step(2, *ended[-1])
    near_grads.append(x_swap(held(kept[4])))
    keep, give = call(
        outer_kernel,
        "outer",
        (((CHIPS, 2 * nq, width), low), ((CHIPS, 2 * nq, width), low)),
        (held(grad_branch), attended),
        far=(1,),
        far_out=(0,),
        scratch=[pltpu.VMEM((width, width), full)],
    )
    close(grad_heads, z2, near_grads[1], give)

    z3 = branch_ring.step(3, *ended[-1])
    other = core_swap(held(give))
    grad_query, grad_own, grad_peer = attend_back(
        numbers, query_all, kv_all, kv_peer_all, held(grad_heads), mixed, lse, cosine, sine
    )
    close(z3, other, grad_query)

    z4 = branch_ring.step(4, *ended[-1])
    second = call(
        settle_kernel,
        "settle",
        (((CHIPS * 2 * nq, width), low),),
        (keep, held(other)),
        far=(0,),
    )[0]
    joined, *leave = call(
        spread_kernel,
        "spread",
        [((CHIPS * TOK, 4 * LANES), low)] + leaving(width, TOK // 2) + leaving(width, nq),
        (grad_query, grad_own, core_swap(held(grad_peer)), cosine, sine, w_heads, second),
        far=(3, 4, 5),
    )
    near_grads.append(x_swap(held(kept[5])))
    close(z4, leave, near_grads[2])

    def last_terms(number, up, down):
        if number == 1:
            return leave[:2]
        begin = STEP_ROWS[number] // TOK
        return call(
            product_kernel,
            "last_terms",
            leaving(width),
            (joined, joined, w_heads, up, down),
            far=(0, 1),
            windows={0: (TOK, begin), 1: (TOK, begin + 1)},
        )

    def out_terms(number, up, down):
        if number == 1:
            return leave[2:]
        begin = STEP_ROWS[number] // TOK
        return call(
            rows_kernel,
            "out_terms",
            leaving(width, 2 * nq),
            (second, second, up, down),
            far=(0, 1),
            windows={0: (2 * nq, begin), 1: (2 * nq, begin + 1)},
        )

    grad_ring = Scatter(out_terms)
    last_ring = Scatter(last_terms)
    t1 = last_ring.step(1, *ended[-1])
    g1 = grad_ring.step(1, *ended[-1])
    mine, send, gain_grads = call(
        heads_grad_kernel,
        "heads_grad",
        (((2, HD, width), full), ((2, HD, width), full), ((2, width), full)),
        (held(joined), w_heads, gain_one, second_gain_grad, normed),
        scratch=[pltpu.VMEM((4 * LANES, width), full)],
        far=range(1, 5),
    )
    t2 = last_ring.step(2)
    g2 = grad_ring.step(2)
    other = core_swap(send)
    result = call(
        result_kernel,
        "result",
        (((TOK, width), low),),
        (branch[0], after(z4[0], *t1), z4[1], middle),
        far=(0, 3),
        far_out=(0,),
        windows={0: (TOK, 0)},
    )[0]
    t3 = last_ring.step(3)
    g3 = grad_ring.step(3)
    mine = mine + other
    heads_grad = mine[0] + x_swap(mine[1].astype(low)).astype(full)
    t4 = last_ring.step(4)
    g4 = grad_ring.step(4)
    gain_grads = after(gain_grads, *t2).reshape(2, CHIPS, 4 * nq)
    gain_grads = jnp.sum(to_chips(jnp.transpose(gain_grads, (1, 0, 2))), axis=0)
    ffn_grad = [own + after(other, *t2).astype(full) for own, other in zip(kept[:3], near_grads)]
    keep, give = call(
        owned_kernel,
        "owned",
        (((nq, width), full), ((nq, width), low)),
        (second, *g4),
        far=(0,),
        windows={0: (2 * nq, 0)},
    )
    output_grad = keep + x_swap(give).astype(full)
    gain_grads = gain_grads + core_swap(gain_grads)
    gain_grads = gain_grads + x_swap(gain_grads)
    gain_grads = lax.dynamic_slice_in_dim(gain_grads, (2 * core + side) * nq, nq, 1)
    grad_tokens = call(
        last_kernel,
        "last",
        (((TOK, width), full),),
        (joined, w_heads, *t4, block, grad_middle, gain_one),
        far=(0, 1, 4, 5),
        far_out=(0,),
        windows={0: (TOK, 0)},
    )[0]
    return (
        result[None],
        grad_tokens[None],
        gain_grads[0],
        gain_grads[1],
        heads_grad[:nq],
        heads_grad[nq : nq + nk],
        heads_grad[nq + nk :],
        output_grad,
        ffn_grad[0],
        ffn_grad[1],
        ffn_grad[2],
    )


def by_plane(mesh):
    return dict(mesh.shape) == {"blk": 2 * CHIPS, "fsdp": 2} and KVH == CHIPS


def solution(mesh):
    in_specs = (
        P("fsdp", "blk", None),
        P("fsdp", "blk", None),
        P("fsdp", None),
        P("fsdp", "blk"),
        P(("blk", "fsdp")),
        P(("blk", "fsdp")),
        P(("blk", "fsdp"), None),
        P(("blk", "fsdp"), None),
        P(("blk", "fsdp"), None),
        P(("blk", "fsdp"), None),
        P(("blk", "fsdp"), None),
        P(("blk", "fsdp"), None),
        P(("blk", "fsdp"), None),
    )
    out_specs = (
        P("fsdp", "blk", None),
        P("fsdp", "blk", None),
        P(("blk", "fsdp")),
        P(("blk", "fsdp")),
        P(("blk", "fsdp"), None),
        P(("blk", "fsdp"), None),
        P(("blk", "fsdp"), None),
        P(("blk", "fsdp"), None),
        P(("blk", "fsdp"), None),
        P(("blk", "fsdp"), None),
        P(("blk", "fsdp"), None),
    )
    body = plane_shards if by_plane(mesh) else shards
    return jax.shard_map(body, mesh=mesh, in_specs=in_specs, out_specs=out_specs, check_vma=False)
```

```python
import functools

import jax
import jax.numpy as jnp
from jax import lax
from jax.experimental import pallas as pl
from jax.experimental.pallas import tpu as pltpu
from jax.sharding import PartitionSpec as P

HEADS = 16
KVH = 8
HD = 96


EPS = 1e-05
ROPE_BASE = 100000.0
NEG = -1e30


def passed_along(block, axis, distance):
    devices = range(lax.axis_size(axis))
    route = [(i - distance, i) for i in devices if i - distance in devices]
    return lax.ppermute(block, axis, route)


def passed_along_2(x, axis, by):
    length = lax.axis_size(axis)
    return lax.ppermute(x, axis, [(i, (i + by) % length) for i in range(length)])


def product_t(left, right):
    return lax.dot_general(
        left, right, (((1,), (1,)), ((), ())), preferred_element_type=jnp.float32
    )


def product(left, right):
    return jnp.dot(left, right, preferred_element_type=jnp.float32)


def product_tn(left, right):
    return lax.dot_general(
        left, right, (((0,), (0,)), ((), ())), preferred_element_type=jnp.float32
    )


def rms_scale(values):
    return lax.rsqrt(jnp.mean(values * values, axis=-1, keepdims=True) + EPS)


def norm_back(grad, values, scale, gain):
    weighted = grad * gain
    inner = jnp.mean(weighted * values, axis=-1, keepdims=True)
    return (scale * weighted - values * scale**3 * inner, jnp.sum(grad * values * scale, axis=0))


def rotation(positions):
    half = HD // 2
    freqs = ROPE_BASE ** (-(jnp.arange(half, dtype=jnp.float32) * 2.0 / HD))
    angles = positions.astype(jnp.float32)[:, None] * freqs[None, :]
    return (jnp.cos(angles)[:, None, :], jnp.sin(angles)[:, None, :])


def rotate(values, cosine, sine, heads, sign):
    count = values.shape[0]
    split = values.reshape(count, heads, HD)
    half = HD // 2
    first = split[..., :half]
    second = split[..., half:]
    turned = jnp.concatenate(
        [first * cosine - sign * second * sine, second * cosine + sign * first * sine], axis=-1
    )
    return turned.reshape(count, heads * HD)


def block_mask(query_seg, query_idx, key_seg, key_idx):
    return (query_seg[:, None] == key_seg[None, :]) & (key_idx[None, :] <= query_idx[:, None])


def scores_of(queries, keys, allowed):
    raw = jnp.einsum("qhgd,khd->hgqk", queries, keys, preferred_element_type=jnp.float32) * HD ** (
        -0.5
    )
    return jnp.where(allowed[None, None], raw, NEG)


def key_blocks(keys_seen, values_seen, key_segs):
    total = keys_seen.shape[0]
    size = min(512, total)
    count = total // size
    return (
        keys_seen.reshape(count, size, KVH, HD),
        values_seen.reshape(count, size, KVH, HD),
        key_segs.reshape(count, size),
        jnp.arange(total, dtype=jnp.int32).reshape(count, size),
    )


def attend(queries, blocks, query_seg, query_idx):
    rows = queries.shape[0]
    groups = HEADS // KVH
    start = (
        jnp.full((KVH, groups, rows, 1), NEG, jnp.float32),
        jnp.zeros((KVH, groups, rows, 1), jnp.float32),
    )

    def stats_step(carry, block):
        keys, values, segs, idxs = block
        allowed = block_mask(query_seg, query_idx, segs, idxs)
        top, running = carry
        scores = scores_of(queries, keys, allowed)
        new_top = jnp.maximum(top, jnp.max(scores, axis=-1, keepdims=True))
        new_sum = running * jnp.exp(top - new_top) + jnp.sum(
            jnp.exp(scores - new_top), axis=-1, keepdims=True
        )
        return ((new_top, new_sum), None)

    (top, running), unused = lax.scan(stats_step, start, blocks)
    lse = top + jnp.log(running)

    def value_step(total_acc, block):
        keys, values, segs, idxs = block
        allowed = block_mask(query_seg, query_idx, segs, idxs)
        weights = jnp.exp(scores_of(queries, keys, allowed) - lse).astype(jnp.bfloat16)
        return (
            total_acc
            + jnp.einsum("hgqk,khd->qhgd", weights, values, preferred_element_type=jnp.float32),
            None,
        )

    mixed, unused = lax.scan(value_step, jnp.zeros((rows, KVH, groups, HD), jnp.float32), blocks)
    return (mixed, lse)


def cycle_back(queries, own_keys, own_values, key_segs, query_seg, query_idx, lse, grad_out, delta):
    rows = queries.shape[0]
    groups = HEADS // KVH
    scale = HD ** (-0.5)
    me = lax.axis_index("blk")
    count = lax.axis_size("blk")
    local = jnp.arange(rows, dtype=jnp.int32)

    def step(carry, turn):
        grad_q, key_blk, value_blk, grad_k, grad_v = carry
        anchor = (me - turn) % count
        begin = anchor * rows
        segs = lax.dynamic_slice_in_dim(key_segs, begin, rows)
        allowed = block_mask(query_seg, query_idx, segs, begin + local)
        acc_k = grad_k
        acc_v = grad_v
        probs = jnp.exp(scores_of(queries, key_blk, allowed) - lse)
        grad_probs = jnp.einsum(
            "qhgd,khd->hgqk", grad_out, value_blk, preferred_element_type=jnp.float32
        )
        grad_scores = (probs * (grad_probs - delta)).astype(jnp.bfloat16)
        new_acc = grad_q + jnp.einsum(
            "hgqk,khd->qhgd", grad_scores, key_blk, preferred_element_type=jnp.float32
        )
        new_k = (
            acc_k
            + jnp.einsum("hgqk,qhgd->khd", grad_scores, queries, preferred_element_type=jnp.float32)
            * scale
        )
        new_v = acc_v + jnp.einsum(
            "hgqk,qhgd->khd",
            probs.astype(jnp.bfloat16),
            grad_out,
            preferred_element_type=jnp.float32,
        )
        grad_k = new_k
        grad_v = new_v
        key_blk, value_blk = passed_along((key_blk, value_blk), "blk", 1)
        grad_k, grad_v = (
            passed_along_2(grad_k.astype(jnp.bfloat16), "blk", 1).astype(grad_k.dtype),
            passed_along_2(grad_v.astype(jnp.bfloat16), "blk", 1).astype(grad_v.dtype),
        )
        return ((new_acc, key_blk, value_blk, grad_k, grad_v), None)

    zero_kv = jnp.zeros((rows, KVH, HD), jnp.float32)
    start = (
        jnp.zeros((rows, KVH, groups, HD), jnp.float32),
        own_keys.reshape(rows, KVH, HD),
        own_values.reshape(rows, KVH, HD),
        zero_kv,
        zero_kv,
    )
    final, unused = lax.scan(step, start, jnp.arange(count, dtype=jnp.int32))
    grad_q, ignored_k, ignored_v, grad_k, grad_v = final
    return (grad_q * scale, grad_k.reshape(rows, KVH * HD), grad_v.reshape(rows, KVH * HD))


def fetch_attention(gain_attn, gain_ffn, w_query, w_key, w_value, w_output):
    return (
        lax.all_gather(gain_attn, ("blk", "fsdp"), axis=0, tiled=True),
        lax.all_gather(gain_ffn, ("blk", "fsdp"), axis=0, tiled=True),
        lax.all_gather(w_query, ("blk", "fsdp"), axis=0, tiled=True),
        lax.all_gather(w_key, ("blk", "fsdp"), axis=0, tiled=True),
        lax.all_gather(w_value, ("blk", "fsdp"), axis=0, tiled=True),
        lax.all_gather(w_output, ("blk", "fsdp"), axis=0, tiled=True),
    )


def fetch_ffn(w_gate, w_up, w_down):
    return (
        lax.all_gather(w_gate, ("blk", "fsdp"), axis=0, tiled=True),
        lax.all_gather(w_up, ("blk", "fsdp"), axis=0, tiled=True),
        lax.all_gather(w_down, ("blk", "fsdp"), axis=0, tiled=True),
    )


def shards(
    tokens,
    cotangent,
    segments,
    positions,
    gain_attn,
    gain_ffn,
    w_query,
    w_key,
    w_value,
    w_output,
    w_gate,
    w_up,
    w_down,
):
    rows = tokens.shape[1]
    groups = HEADS // KVH
    xin = tokens[0].astype(jnp.float32)
    offset = lax.axis_index("blk") * rows
    query_idx = offset + jnp.arange(rows, dtype=jnp.int32)
    key_segs = segments[0]
    query_seg = lax.dynamic_slice_in_dim(key_segs, offset, rows)
    cosine, sine = rotation(positions[0])
    gain_one, gain_two, query_all, key_all, value_all, output_all = fetch_attention(
        gain_attn, gain_ffn, w_query, w_key, w_value, w_output
    )
    first_gain = gain_one.astype(jnp.float32)
    second_gain = gain_two.astype(jnp.float32)
    first_scale = rms_scale(xin)
    normed = (xin * first_scale * first_gain).astype(jnp.bfloat16)
    queries = rotate(product_t(normed, query_all), cosine, sine, HEADS, 1.0).astype(jnp.bfloat16)
    keys = rotate(product_t(normed, key_all), cosine, sine, KVH, 1.0).astype(jnp.bfloat16)
    values = product_t(normed, value_all).astype(jnp.bfloat16)
    keys_seen, values_seen = (
        lax.all_gather(keys, "blk", axis=0, tiled=True),
        lax.all_gather(values, "blk", axis=0, tiled=True),
    )
    query_heads = queries.reshape(rows, KVH, groups, HD)
    mixed, lse = attend(
        query_heads, key_blocks(keys_seen, values_seen, key_segs), query_seg, query_idx
    )
    attended = mixed.reshape(rows, HEADS * HD).astype(jnp.bfloat16)
    middle = xin + product_t(attended, output_all)
    second_scale = rms_scale(middle)
    normed_two = (middle * second_scale * second_gain).astype(jnp.bfloat16)
    gate_rows, up_rows, down_rows = fetch_ffn(w_gate, w_up, w_down)
    gate = product_t(normed_two, gate_rows)
    up = product_t(normed_two, up_rows)
    sigma = jax.nn.sigmoid(gate)
    activated = gate * sigma
    hidden = (activated * up).astype(jnp.bfloat16)
    branch = product(hidden, down_rows)
    result = (middle + branch).astype(jnp.bfloat16)
    grad_in = cotangent[0]
    gate_rows, up_rows, down_rows = fetch_ffn(w_gate, w_up, w_down)
    grad_hidden = product_t(grad_in, down_rows)
    grad_gate = (grad_hidden * up * sigma * (1.0 + gate * (1.0 - sigma))).astype(jnp.bfloat16)
    grad_up = (grad_hidden * activated).astype(jnp.bfloat16)
    gate_grad = product_tn(grad_gate, normed_two)
    up_grad = product_tn(grad_up, normed_two)
    down_grad = product_tn(hidden, grad_in)
    grad_normed_two = product(grad_gate, gate_rows) + product(grad_up, up_rows)
    gate_grad, up_grad, down_grad = (
        lax.psum_scatter(gate_grad, ("blk", "fsdp"), scatter_dimension=0, tiled=True),
        lax.psum_scatter(up_grad, ("blk", "fsdp"), scatter_dimension=0, tiled=True),
        lax.psum_scatter(down_grad, ("blk", "fsdp"), scatter_dimension=0, tiled=True),
    )
    grad_middle_norm, second_gain_grad = norm_back(
        grad_normed_two, middle, second_scale, second_gain
    )
    grad_middle = grad_in.astype(jnp.float32) + grad_middle_norm
    grad_branch = grad_middle.astype(jnp.bfloat16)
    output_grad = product_tn(grad_branch, attended)
    grad_attended = product(grad_branch, output_all).astype(jnp.bfloat16)
    grad_heads = grad_attended.reshape(rows, KVH, groups, HD)
    delta = jnp.transpose(jnp.sum(grad_heads.astype(jnp.float32) * mixed, axis=-1), (1, 2, 0))[
        ..., None
    ]
    grad_q, grad_keys, grad_values = cycle_back(
        query_heads, keys, values, key_segs, query_seg, query_idx, lse, grad_heads, delta
    )
    grad_q_pre = rotate(grad_q.reshape(rows, HEADS * HD), cosine, sine, HEADS, -1.0).astype(
        jnp.bfloat16
    )
    grad_k_pre = rotate(grad_keys, cosine, sine, KVH, -1.0).astype(jnp.bfloat16)
    grad_v = grad_values.astype(jnp.bfloat16)
    query_grad = product_tn(grad_q_pre, normed)
    key_grad = product_tn(grad_k_pre, normed)
    value_grad = product_tn(grad_v, normed)
    grad_normed = (
        product(grad_q_pre, query_all) + product(grad_k_pre, key_all) + product(grad_v, value_all)
    )
    grad_x_norm, first_gain_grad = norm_back(grad_normed, xin, first_scale, first_gain)
    grad_tokens = grad_middle + grad_x_norm
    first_gain_grad, second_gain_grad, query_grad, key_grad, value_grad, output_grad = (
        lax.psum_scatter(first_gain_grad, ("blk", "fsdp"), scatter_dimension=0, tiled=True),
        lax.psum_scatter(second_gain_grad, ("blk", "fsdp"), scatter_dimension=0, tiled=True),
        lax.psum_scatter(query_grad, ("blk", "fsdp"), scatter_dimension=0, tiled=True),
        lax.psum_scatter(key_grad, ("blk", "fsdp"), scatter_dimension=0, tiled=True),
        lax.psum_scatter(value_grad, ("blk", "fsdp"), scatter_dimension=0, tiled=True),
        lax.psum_scatter(output_grad, ("blk", "fsdp"), scatter_dimension=0, tiled=True),
    )
    return (
        result[None],
        grad_tokens[None],
        first_gain_grad,
        second_gain_grad,
        query_grad,
        key_grad,
        value_grad,
        output_grad,
        gate_grad,
        up_grad,
        down_grad,
    )


CHIPS = 8
TOK = 128
PAIR = 2 * HD
LANES = 128
VMEM_LIMIT = 32 << 20
LOG2E = 1.4426950408889634
RING = (0, 2, 4, 6, 7, 5, 3, 1)
SAME_CORE = [[2 * c + core for c in range(CHIPS)] for core in range(2)]


def ring_route(step):
    return [
        (RING[k] * 2 + core, RING[(k + step) % CHIPS] * 2 + core)
        for k in range(CHIPS)
        for core in range(2)
    ]


def ring_up(value):
    return lax.ppermute(value, "blk", ring_route(1))


def ring_down(value):
    return lax.ppermute(value, "blk", ring_route(-1))


def flipped(value, bit):
    return lax.ppermute(value, "blk", [(i, i ^ bit) for i in range(2 * CHIPS)])


def core_swap(value):
    return flipped(value, 1)


def x_swap(value):
    return lax.ppermute(value, "fsdp", [(0, 1), (1, 0)])


def tie(values, deps):
    deps = [d for d in deps if d is not None]
    if not deps:
        return tuple(values)
    return lax.optimization_barrier((tuple(values), tuple(deps)))[0]


def after(value, *deps):
    return tie((value,), deps)[0]


class Gather:
    def __init__(self, block):
        self.found = [None] * CHIPS
        self.found[0] = self.up = self.down = block

    def step(self, number, *deps):
        self.up, self.down = tie((self.up, self.down), deps)
        if number < CHIPS // 2:
            self.up = ring_up(self.up)
            self.down = ring_down(self.down)
            self.found[CHIPS - number] = self.up
            self.found[number] = self.down
        else:
            half = self.up.shape[0] // 2
            self.up = ring_up(self.up[:half])
            self.down = ring_down(self.down[half:])
            self.found[number] = (self.up, self.down)
        return self.up, self.down


class Scatter:
    def __init__(self, make):
        self.make = make
        self.up = self.down = None

    def step(self, number, *deps):
        up, down = tie(self.make(number, self.up, self.down), deps)
        self.up = ring_up(up)
        self.down = ring_down(down)
        return self.up, self.down


def dot_nt(left, right):
    return lax.dot_general(
        left, right, (((1,), (1,)), ((), ())), preferred_element_type=jnp.float32
    )


def dot_nn(left, right):
    return lax.dot_general(
        left, right, (((1,), (0,)), ((), ())), preferred_element_type=jnp.float32
    )


GROUPS = ((0, 1, 7), (2, 6), (3, 5), (4,))
ARRIVAL = tuple(j for group in GROUPS for j in group)


def whole(shape):
    return pl.BlockSpec(shape, lambda i: (0,) * len(shape), pipeline_mode=pl.Buffered(1))


def window(rows, nth, width):
    return pl.BlockSpec((rows, width), lambda i: (nth, 0), pipeline_mode=pl.Buffered(1))


def call(kernel, name, outs, ins, scratch=(), far=(), far_out=(), windows={}):
    shapes = []
    for n, (shape, dtype) in enumerate(outs):
        make = pltpu.HBM if n in far_out else jax.ShapeDtypeStruct
        shapes.append(make(shape, dtype))
    ins = list(ins)
    for n in far:
        ins[n] = pltpu.with_memory_space_constraint(ins[n], pltpu.HBM)
    return pl.pallas_call(
        kernel,
        grid=(1,),
        out_shape=tuple(shapes),
        in_specs=[
            window(*windows[n], value.shape[1]) if n in windows else whole(value.shape)
            for n, value in enumerate(ins)
        ],
        out_specs=tuple(whole(shape) for shape, _ in outs),
        scratch_shapes=scratch,
        compiler_params=pltpu.CompilerParams(vmem_limit_bytes=VMEM_LIMIT),
        cost_estimate=pl.CostEstimate(flops=0, bytes_accessed=0, transcendentals=0),
        name=name,
    )(*ins)


def dot_tn(left, right):
    return lax.dot_general(
        left, right, (((0,), (0,)), ((), ())), preferred_element_type=jnp.float32
    )


def own_place():
    index = lax.axis_index("blk")
    chip = lax.div(index, 2)
    half = lax.div(chip, 2)
    spot = jnp.where(lax.rem(chip, 2) == 0, half, CHIPS - 1 - half)
    return lax.rem(index, 2), lax.axis_index("fsdp"), chip, spot


def arriving_chip(nth, spot):
    at = lax.rem(spot + ARRIVAL[nth], CHIPS)
    return jnp.where(at < CHIPS // 2, 2 * at, 2 * CHIPS - 1 - 2 * at)


def arrival_of(chip, spot):
    away = lax.rem(RING.index(chip) - spot + CHIPS, CHIPS)
    late = jnp.where(away <= CHIPS // 2, 2 * away - 1, 2 * (CHIPS - away))
    return jnp.where(away == 0, 0, late)


def heads_kernel(own, near, far, across, out):
    nq = HD // 2
    nk = HD // 4
    half = LANES // 2
    own_core, own_side, _, _ = own_place()
    out[...] = jnp.zeros_like(out)
    for core in range(2):
        for side in range(2):

            @pl.when((own_core == core) & (own_side == side))
            def _():
                for piece, c, f in (
                    (own, core, side),
                    (near, core, 1 - side),
                    (far, 1 - core, side),
                    (across, 1 - core, 1 - side),
                ):
                    at = c * LANES + f * half
                    out[at : at + nq] = piece[:nq]
                    at = 2 * LANES + c * half + f * nk
                    out[at : at + nk] = piece[nq : nq + nk]
                    at = 3 * LANES + (2 * c + f) * nk
                    out[at : at + nk] = piece[nq + nk :]


def stack_kernel(*refs):
    out = refs[-1]
    at = 0
    for piece in refs[:-1]:
        out[at : at + piece.shape[0]] = piece[...]
        at += piece.shape[0]


def out_kernel(*refs):
    own, near, out = refs[:4], refs[4:8], refs[8]
    side = own_place()[1]
    rows = own[0].shape[0] // 2
    for n, j in enumerate(ARRIVAL):
        away = min(j, CHIPS - j)
        which = 3 if away in (0, CHIPS // 2) else away - 1
        here = slice(0, rows) if j in (0, 1, 2, 3) else slice(rows, 2 * rows)
        for source, f in ((own, side), (near, 1 - side)):
            at = pl.multiple_of((2 * n + f) * rows, rows)
            out[pl.ds(at, rows), :] = source[which][here, :]


def hidden_kernel(*refs):
    gate_up, down = refs[-2:]
    count = refs[0].shape[0]
    for n in range(4):
        gate, up, out = refs[3 * n : 3 * n + 3]
        start = (n // 2) * 4 * count + (n % 2) * count
        gate_up[start : start + count] = gate[...]
        gate_up[start + 2 * count : start + 3 * count] = up[...]
        down[n * count : (n + 1) * count] = out[...]


def project_kernel(*refs):
    blocks = refs[: CHIPS + 1]
    gain, weight, cosine, sine, normed_out, query_out, kv_out = refs[CHIPS + 1 :]
    for j in range(CHIPS):
        if j < CHIPS - 1:
            values = blocks[j][-TOK:].astype(jnp.float32)
        else:
            late = blocks[CHIPS][...].astype(jnp.float32)
            values = blocks[j][-(TOK - late.shape[0]) :].astype(jnp.float32)
            values = jnp.concatenate([values, late], axis=0)
        scale = lax.rsqrt(jnp.mean(values * values, axis=-1, keepdims=True) + EPS)
        normed_out[j * TOK : (j + 1) * TOK, :] = (values * scale * gain[...]).astype(jnp.bfloat16)
    pre = dot_nt(normed_out[...], weight[...])
    for head in range(3):
        part = pre[:, head * LANES : (head + 1) * LANES]
        turned = part * cosine[...] + pltpu.roll(part, LANES // 2, 1) * sine[...]
        if head < 2:
            query_out[:, head * LANES : (head + 1) * LANES] = turned.astype(jnp.bfloat16)
        else:
            kv_out[:, :LANES] = turned.astype(jnp.bfloat16)
    kv_out[:, LANES:] = pre[:, 3 * LANES :].astype(jnp.bfloat16)


def project(blocks, *arrays):
    rows = CHIPS * TOK
    width = blocks[0].shape[1]
    low = jnp.bfloat16
    assert len(blocks) == CHIPS + 1
    return call(
        project_kernel,
        "project",
        (((rows, width), low), ((rows, 2 * LANES), low), ((rows, 2 * LANES), low)),
        (*blocks, *arrays),
        far=range(CHIPS + 1),
        far_out=(0,),
    )


def key_index(core, count):
    row = lax.broadcasted_iota(jnp.int32, (count, 1), 0)
    return (row // TOK) * (2 * TOK) + core * TOK + row % TOK


def query_index(core, chip):
    lane = lax.broadcasted_iota(jnp.int32, (1, 2 * TOK), 1)
    return lane % TOK + (2 * chip + core) * TOK


def sequence_starts(segments):
    numbers = segments[...]
    starts = []
    for number in range(1, 4):
        below = (numbers < number).astype(jnp.float32)
        total = jnp.sum(jnp.sum(below, axis=1, keepdims=True), axis=0, keepdims=True)
        starts.append(total.astype(jnp.int32))
    return starts


def first_index(starts, at):
    first = jnp.zeros_like(at)
    for start in starts:
        first = jnp.where(at >= start, start, first)
    return first


def only_allowed(values, keys_at, at, first, chip):
    if chip in (0, CHIPS - 1):
        return jnp.where((keys_at <= at) & (keys_at >= first), values, NEG)
    low = jnp.where(keys_at[:TOK] >= first, values[:TOK], NEG)
    high = jnp.where(keys_at[chip * TOK :] <= at, values[chip * TOK :], NEG)
    parts = [low, values[TOK : chip * TOK], high] if chip > 1 else [low, high]
    return jnp.concatenate(parts, axis=0)


def both_heads(ref, rows):
    return jnp.concatenate([ref[rows, :LANES], ref[rows, LANES:]], axis=0)


def attend_kernel(
    segments, query_in, own_in, peer_in, attended, mixed, lse, query, own, peer
):
    core, _, _, spot = own_place()
    starts = sequence_starts(segments)
    factor = HD ** (-0.5) * LOG2E
    for source, target in ((query_in, query), (own_in, own), (peer_in, peer)):
        for chip in range(CHIPS):
            rows = pl.ds(pl.multiple_of(arrival_of(chip, spot) * TOK, TOK), TOK)
            target[chip * TOK : (chip + 1) * TOK, :] = source[rows, :]
    sides = ((own, core), (peer, 1 - core))
    values_t = [jnp.transpose(kv[:, LANES:]) for kv, _ in sides]
    for chip in range(CHIPS):
        count = (chip + 1) * TOK
        rows = slice(chip * TOK, count)
        queries = both_heads(query, rows)
        at = query_index(core, chip)
        first = first_index(starts, at)
        scores = []
        for kv, side in sides:
            raw = dot_nt(kv[:count, :LANES], queries) * factor
            scores.append(only_allowed(raw, key_index(side, count), at, first, chip))
        top = jnp.maximum(
            jnp.max(scores[0], axis=0, keepdims=True), jnp.max(scores[1], axis=0, keepdims=True)
        )
        weights = [jnp.exp2(part - top) for part in scores]
        total = jnp.sum(weights[0], axis=0, keepdims=True) + jnp.sum(
            weights[1], axis=0, keepdims=True
        )
        mix = dot_nn(values_t[0][:, :count], weights[0].astype(jnp.bfloat16)) + dot_nn(
            values_t[1][:, :count], weights[1].astype(jnp.bfloat16)
        )
        mix = mix / total
        mixed[chip] = mix
        lse[chip] = top + jnp.log2(total)
        attended[chip, :HD] = mix[:HD, :TOK].astype(jnp.bfloat16)
        attended[chip, HD:] = mix[:HD, TOK:].astype(jnp.bfloat16)


def attend_heads(segments, query, own, peer):
    tokens = CHIPS * TOK
    low = jnp.bfloat16
    return call(
        attend_kernel,
        "attend",
        (
            ((CHIPS, PAIR, TOK), low),
            ((CHIPS, LANES, 2 * TOK), jnp.float32),
            ((CHIPS, 1, 2 * TOK), jnp.float32),
            ((tokens, 2 * LANES), low),
            ((tokens, 2 * LANES), low),
            ((tokens, 2 * LANES), low),
        ),
        (segments, query, own, peer),
        far_out=(1, 2, 3, 4, 5),
    )


def attend_back_kernel(
    segments, query, own, peer, grad_out, mixed, lse, cosine, sine,
    grad_query, own_out, peer_out, grad_own, grad_peer,
):
    core, _, _, spot = own_place()
    starts = sequence_starts(segments)
    scale = HD ** (-0.5)
    factor = scale * LOG2E
    sides = ((own, core, grad_own), (peer, 1 - core, grad_peer))
    keys_t = [jnp.transpose(kv[:, :LANES]) for kv, _, _ in sides]
    grad_own[...] = jnp.zeros_like(grad_own)
    grad_peer[...] = jnp.zeros_like(grad_peer)
    pad = jnp.zeros((LANES - HD, 2 * TOK), jnp.bfloat16)
    for chip in range(CHIPS):
        count = (chip + 1) * TOK
        rows = slice(chip * TOK, count)
        kept = pl.ds(pl.multiple_of(arrival_of(chip, spot) * TOK, TOK), TOK)
        queries = both_heads(query, rows)
        grads = jnp.concatenate(
            [
                jnp.concatenate([grad_out[chip, :HD], grad_out[chip, HD:]], axis=1),
                pad,
            ],
            axis=0,
        )
        delta = jnp.sum(grads.astype(jnp.float32) * mixed[chip], axis=0, keepdims=True)
        at = query_index(core, chip)
        first = first_index(starts, at)
        level = lse[chip]
        grad_q = jnp.zeros((LANES, 2 * TOK), jnp.float32)
        for (kv, side, grad_kv), key_t in zip(sides, keys_t):
            raw = dot_nt(kv[:count, :LANES], queries) * factor
            keys_at = key_index(side, count)
            probs = jnp.exp2(only_allowed(raw - level, keys_at, at, first, chip))
            grad_probs = dot_nn(kv[:count, LANES:], grads)
            grad_scores = (probs * (grad_probs - delta)).astype(jnp.bfloat16)
            grad_kv[:count, LANES:] += dot_nt(probs.astype(jnp.bfloat16), grads)
            grad_kv[:count, :LANES] += dot_nn(grad_scores, queries)
            grad_q += dot_nn(key_t[:, :count], grad_scores)
        grad_q = jnp.transpose(grad_q) * scale
        cos = cosine[kept, :]
        sin = sine[kept, :]
        for head in range(2):
            part = grad_q[head * TOK : (head + 1) * TOK]
            turned = part * cos - pltpu.roll(part, LANES // 2, 1) * sin
            grad_query[kept, head * LANES : (head + 1) * LANES] = turned.astype(jnp.bfloat16)
    for chip in range(CHIPS):
        rows = slice(chip * TOK, (chip + 1) * TOK)
        kept = pl.ds(pl.multiple_of(arrival_of(chip, spot) * TOK, TOK), TOK)
        for grad_kv, out in ((grad_own, own_out), (grad_peer, peer_out)):
            out[kept, :LANES] = grad_kv[rows, :LANES] * scale
            out[kept, LANES:] = grad_kv[rows, LANES:]


def attend_back(segments, *arrays):
    tokens = CHIPS * TOK
    full = jnp.float32
    return call(
        attend_back_kernel,
        "attend_back",
        (
            ((tokens, 2 * LANES), jnp.bfloat16),
            ((tokens, 2 * LANES), full),
            ((tokens, 2 * LANES), full),
        ),
        (segments, *arrays),
        scratch=[pltpu.VMEM((tokens, 2 * LANES), full)] * 2,
        far=(1, 2, 3, 5, 6, 7, 8),
    )


def join_kernel(heads, *refs):
    weights = refs[:2]
    block, gain, middle_out, normed_out, attended_out, weight_out, held = refs[2:]
    core, _, _, spot = own_place()
    size = weights[0].shape[0] // CHIPS
    for n in range(CHIPS):
        for piece, side in zip(weights, (core, 1 - core)):
            at = pl.multiple_of((2 * arriving_chip(n, spot) + side) * size, size)
            weight_out[pl.ds(at, size), :] = piece[n * size : (n + 1) * size, :]
    for chip in range(CHIPS):
        held[chip * PAIR : (chip + 1) * PAIR, :] = heads[chip]
    attended_out[...] = jnp.transpose(held[...])
    middle = block[...].astype(jnp.float32) + dot_nt(attended_out[...], weight_out[...])
    middle_out[...] = middle
    scale = lax.rsqrt(jnp.mean(middle * middle, axis=-1, keepdims=True) + EPS)
    normed_out[...] = (middle * scale * gain[...]).astype(jnp.bfloat16)


def ffn_kernel(number, *refs):
    blocks = refs[:number]
    outers = refs[number : 2 * number]
    gate_up, down_rows = refs[2 * number : 2 * number + 2]
    rows, outer_rows, hidden, grad_gu = refs[2 * number + 2 : 2 * number + 6]
    wide = hidden.shape[1] // 2
    size = rows.shape[0] // number
    for n in range(number):
        rows[n * size : (n + 1) * size, :] = blocks[n][...]
        outer_rows[n * size : (n + 1) * size, :] = outers[n][...]
    grads = dot_nt(outer_rows[...], down_rows[...])
    pre = dot_nt(rows[...], gate_up[...])
    for part in range(2):
        at = part * 2 * wide
        gate = pre[:, at : at + wide]
        up = pre[:, at + wide : at + 2 * wide]
        back = grads[:, part * wide : (part + 1) * wide]
        sigma = 1.0 / (1.0 + jnp.exp(-gate))
        active = gate * sigma
        hidden[:, part * wide : (part + 1) * wide] = (active * up).astype(jnp.bfloat16)
        slope = back * up * sigma * (1.0 + gate * (1.0 - sigma))
        grad_gu[:, at : at + wide] = slope.astype(jnp.bfloat16)
        grad_gu[:, at + wide : at + 2 * wide] = (back * active).astype(jnp.bfloat16)
    outs = refs[2 * number + 6 :]
    back = dot_nn(grad_gu[...], gate_up[...])
    if len(outs) == 1:
        outs[0][...] = back
    else:
        outs[0][...] = back[: TOK // 2].astype(jnp.bfloat16)
        outs[1][...] = back[TOK // 2 :].astype(jnp.bfloat16)


def ffn(blocks, outers, gate_up, down):
    number = len(blocks)
    rows = number * blocks[0].shape[0]
    width = blocks[0].shape[1]
    units = down.shape[0]
    low = jnp.bfloat16
    if rows > TOK:
        terms = [((rows, width), jnp.float32)]
    else:
        terms = [((TOK // 2, width), low)] * 2
    return call(
        functools.partial(ffn_kernel, number),
        "ffn",
        [((rows, width), low)] * 2 + [((rows, units), low), ((rows, 2 * units), low)] + terms,
        (*blocks, *outers, gate_up, down),
    )


def add_terms(up_term, down_term, up, down, up_out, down_out):
    size = up.shape[0]
    rest = up_out.shape[0] - size
    low = jnp.bfloat16
    full = jnp.float32
    up_out[:size] = (up_term[:size] + up.astype(full)).astype(low)
    down_out[rest:] = (down_term[rest:] + down.astype(full)).astype(low)
    if rest:
        up_out[size:] = up_term[size:].astype(low)
        down_out[:rest] = down_term[:rest].astype(low)


def add_kernel(up_term, down_term, up, down, up_out, down_out):
    add_terms(up_term, down_term, up[...], down[...], up_out, down_out)


def leaving(width, rows=TOK):
    return [((rows, width), jnp.bfloat16)] * 2


STEP_ROWS = {1: 7 * TOK, 2: 5 * TOK, 3: 3 * TOK, 4: TOK}


def branch_kernel(hidden, down_rows, *outs):
    found = dot_nn(hidden[...], down_rows[...])
    at = 0
    for out in outs[:-2]:
        out[...] = found[at : at + out.shape[0]]
        at += out.shape[0]
    outs[-2][...] = found[at : at + TOK // 2].astype(jnp.bfloat16)
    outs[-1][...] = found[at + TOK // 2 :].astype(jnp.bfloat16)


def result_kernel(terms, up, down, middle, out):
    full = jnp.float32
    branch = terms[...] + (up[...].astype(full) + down[...].astype(full))
    out[...] = (middle[...] + branch).astype(jnp.bfloat16)


def grads_kernel(number, *refs):
    rows_in, outer_in, hidden_in, grads_in = (refs[n * number : (n + 1) * number] for n in range(4))
    keep_gu, keep_down, send_gu, send_down, hidden, rows, grads = refs[4 * number :]
    at = 0
    for block, hid, grad in zip(rows_in, hidden_in, grads_in):
        here = slice(at, at + block.shape[0])
        rows[here, :] = block[...]
        hidden[here, :] = hid[...]
        grads[here, :] = grad[...]
        at += block.shape[0]
    half = keep_gu.shape[0]
    send_gu[...] = dot_tn(grads[:, half:], rows[...])
    keep_gu[...] = dot_tn(grads[:, :half], rows[...])
    at = 0
    for block in outer_in:
        rows[at : at + block.shape[0], :] = block[...]
        at += block.shape[0]
    half = keep_down.shape[0]
    send_down[...] = dot_tn(hidden[:, half:], rows[...])
    keep_down[...] = dot_tn(hidden[:, :half], rows[...])


def owners_kernel(keep_gu, keep_down, other_gu, other_down, *outs):
    count = outs[0].shape[0]
    for n, (value, other, at) in enumerate(
        ((keep_gu, other_gu, 0), (keep_gu, other_gu, 2 * count), (keep_down, other_down, 0))
    ):
        near = at + count
        outs[n][...] = value[at:near] + other[at:near]
        given = value[near : near + count] + other[near : near + count]
        outs[3 + n][...] = given.astype(jnp.bfloat16)


def turn_kernel(*refs):
    own, up, down, middle_ref, outer, gain, weight, middle_out, branch_out, heads, gain_out = refs
    grad = own[...] + (up[...].astype(jnp.float32) + down[...].astype(jnp.float32))
    middle = middle_ref[...]
    scale = lax.rsqrt(jnp.mean(middle * middle, axis=-1, keepdims=True) + EPS)
    weighted = grad * gain[...]
    inner = jnp.mean(weighted * middle, axis=-1, keepdims=True)
    gain_out[...] = jnp.sum(grad * middle * scale, axis=0, keepdims=True)
    total = outer[...].astype(jnp.float32) + (scale * weighted - middle * (scale**3 * inner))
    middle_out[...] = total
    branch = total.astype(jnp.bfloat16)
    branch_out[...] = branch
    back = jnp.transpose(dot_nn(branch, weight[...]).astype(jnp.bfloat16))
    for chip in range(CHIPS):
        heads[chip] = back[chip * PAIR : (chip + 1) * PAIR]


def outer_kernel(branch, attended, keep, give, held):
    held[...] = dot_tn(branch[...], attended[...])
    core = own_place()[0]
    size = keep.shape[1]
    for chip in range(CHIPS):
        at = pl.multiple_of((2 * chip + core) * size, size)
        keep[chip] = held[pl.ds(at, size), :].astype(jnp.bfloat16)
        at = pl.multiple_of((2 * chip + 1 - core) * size, size)
        give[chip] = held[pl.ds(at, size), :].astype(jnp.bfloat16)


def settle_kernel(keep, other, total):
    spot = own_place()[3]
    rows = keep.shape[1]
    for n in range(CHIPS):
        chip = arriving_chip(n, spot)
        found = keep[chip].astype(jnp.float32) + other[chip].astype(jnp.float32)
        total[n * rows : (n + 1) * rows] = found.astype(jnp.bfloat16)


def product_kernel(up_left, down_left, right, up, down, up_out, down_out):
    terms = dot_nn(jnp.concatenate([up_left[...], down_left[...]], axis=0), right[...])
    add_terms(terms[:TOK], terms[TOK:], up[...], down[...], up_out, down_out)


def rows_kernel(up_term, down_term, up, down, up_out, down_out):
    full = jnp.float32
    add_terms(
        up_term[...].astype(full), down_term[...].astype(full), up[...], down[...], up_out, down_out
    )


def spread_kernel(
    query, own, other, cosine, sine, weight, second, joined, up_out, down_out, up_rows, down_rows
):
    joined[:, : 2 * LANES] = query[...]
    total = own[...] + other[...]
    part = total[:, :LANES]
    turned = part * cosine[...] - pltpu.roll(part, LANES // 2, 1) * sine[...]
    joined[:, 2 * LANES : 3 * LANES] = turned.astype(jnp.bfloat16)
    joined[:, 3 * LANES :] = total[:, LANES:].astype(jnp.bfloat16)
    begin = STEP_ROWS[1]
    terms = dot_nn(joined[begin : begin + TOK], weight[...]).astype(jnp.bfloat16)
    up_out[...] = terms[: TOK // 2]
    down_out[...] = terms[TOK // 2 :]
    rows = second.shape[0] // CHIPS
    up_rows[...] = second[(CHIPS - 1) * rows : (CHIPS - 1) * rows + rows // 2]
    down_rows[...] = second[(CHIPS - 1) * rows + rows // 2 :]


def heads_grad_kernel(*refs):
    own_core, own_side, _, _ = own_place()
    joined, weight, gain, second, normed, mine, send, gains, grad = refs
    grad[...] = dot_tn(joined[...], normed[...])
    first = jnp.sum(grad[...] * weight[...].astype(jnp.float32), axis=0, keepdims=True) / gain[...]
    nq = HD // 2
    nk = HD // 4
    half = LANES // 2
    gains[:1] = first
    gains[1:] = second[...]
    for core in range(2):
        for side in range(2):

            @pl.when((own_core == core) & (own_side == side))
            def _():
                for c in range(2):
                    for f in range(2):
                        out = mine if c == core else send
                        which = 0 if f == side else 1
                        at = c * LANES + f * half
                        out[which, :nq] = grad[at : at + nq]
                        at = 2 * LANES + c * half + f * nk
                        out[which, nq : nq + nk] = grad[at : at + nk]
                        at = 3 * LANES + (2 * c + f) * nk
                        out[which, nq + nk :] = grad[at : at + nk]


def owned_kernel(second, up, down, keep, give):
    side = own_place()[1]
    rows = keep.shape[0]
    full = jnp.float32
    total = second[...].astype(full) + (up[...].astype(full) + down[...].astype(full))
    keep[...] = jnp.where(side == 0, total[:rows], total[rows:])
    give[...] = jnp.where(side == 0, total[rows:], total[:rows]).astype(jnp.bfloat16)


def last_kernel(joined, weight, up, down, block, middle, gain, out):
    grad = dot_nn(joined[...], weight[...])
    grad = grad + (up[...].astype(jnp.float32) + down[...].astype(jnp.float32))
    values = block[...].astype(jnp.float32)
    scale = lax.rsqrt(jnp.mean(values * values, axis=-1, keepdims=True) + EPS)
    weighted = grad * gain[...]
    inner = jnp.mean(weighted * values, axis=-1, keepdims=True)
    out[...] = middle[...] + (scale * weighted - values * (scale**3 * inner))


def plane_shards(
    tokens,
    cotangent,
    segments,
    positions,
    gain_attn,
    gain_ffn,
    w_query,
    w_key,
    w_value,
    w_output,
    w_gate,
    w_up,
    w_down,
):
    full = jnp.float32
    low = jnp.bfloat16
    block = tokens[0]
    outer = cotangent[0]
    width = block.shape[1]
    index = lax.axis_index("blk")
    side = lax.axis_index("fsdp")
    core = index % 2
    chip = index // 2
    spot = jnp.where(chip % 2 == 0, chip // 2, CHIPS - 1 - chip // 2)

    segs = segments[0]
    numbers = segs.reshape(2 * CHIPS, TOK)
    starts = [jnp.sum((segs < number).astype(jnp.int32)) for number in range(1, 4)]
    row = lax.broadcasted_iota(jnp.int32, (CHIPS * TOK, LANES), 0)
    nth = row >> 7
    away = jnp.where((nth & 1) == 1, (nth + 1) >> 1, CHIPS - (nth >> 1))
    at = (spot + away) & (CHIPS - 1)
    token = jnp.where(at < CHIPS // 2, 2 * at, 2 * CHIPS - 1 - 2 * at) * (2 * TOK)
    token = token + core * TOK + (row & (TOK - 1))
    first = jnp.zeros_like(token)
    for start in starts:
        first = jnp.where(token >= start, start, first)
    half = HD // 2
    freqs = ROPE_BASE ** (-(jnp.arange(half, dtype=full) * 2.0 / HD))
    spare = jnp.zeros((LANES // 2 - half,), full)
    both = jnp.concatenate([freqs, spare, freqs, spare])
    angles = (token - first).astype(full) * both[None, :]
    sign = jnp.where(jnp.arange(LANES) < LANES // 2, -1.0, 1.0).astype(full)
    cosine = jnp.cos(angles)
    sine = jnp.sin(angles) * sign[None, :]

    ended = [()]

    def held(value):
        return after(value, *ended[-1])

    def close(*results):
        flat = []
        for result in results:
            flat += list(result) if isinstance(result, (list, tuple)) else [result]
        ended.append(tuple(flat))

    def to_chips(value):
        return lax.all_to_all(
            value, "blk", split_axis=0, concat_axis=0, axis_index_groups=SAME_CORE, tiled=True
        )

    nq = w_query.shape[0]
    nk = w_key.shape[0]
    count = w_gate.shape[0]
    units = 2 * count

    def wider(vector, bit):
        other = flipped(vector, bit) if bit else x_swap(vector)
        return jnp.where(
            ((index & bit) if bit else side) == 0,
            jnp.concatenate([vector, other], axis=1),
            jnp.concatenate([other, vector], axis=1),
        )

    both = call(
        stack_kernel, "stack_tokens", (((nq + TOK, width), low),), (w_output, block), far=(0, 1)
    )[0]
    tokens_ring = Gather(both)
    x1 = tokens_ring.step(1)
    gains = wider(wider(jnp.stack([gain_attn, gain_ffn]), 0), 1)
    close(x1, gains, cosine, sine)

    x2 = tokens_ring.step(2, *ended[-1])
    packed = call(
        stack_kernel,
        "stack_heads",
        (((nq + 2 * nk, width), low),),
        (w_query, w_key, held(w_value)),
        far=range(3),
    )[0]
    near = x_swap(packed)
    far = core_swap(packed)
    gains = wider(held(gains), 2)
    close(x2, near, far, gains)

    def out_pair(first, second):
        return call(
            stack_kernel,
            "stack_pair",
            (((2 * nq, width), low),),
            (first, second),
            far=(0, 1),
            windows={0: (nq, 0), 1: (nq, 0)},
        )[0]

    found = tokens_ring.found
    x3 = tokens_ring.step(3, *ended[-1])
    across = core_swap(held(near))
    gains = wider(held(gains), 4)
    own_outs = [out_pair(held(found[1]), found[7])]
    near_outs = [x_swap(own_outs[0])]
    close(x3, across, gains, near_outs)

    x4 = tokens_ring.step(4, *ended[-1])
    w_heads = call(
        heads_kernel,
        "head_rows",
        (((4 * LANES, width), low),),
        (packed, near, far, held(across)),
        far=range(4),
    )[0]
    own_outs.append(out_pair(held(found[2]), found[6]))
    own_outs.append(out_pair(held(found[3]), found[5]))
    gains = wider(held(gains), 8).astype(full)
    gain_one = gains[:1]
    gain_two = gains[1:]
    close(x4, gains, w_heads, own_outs[1:])

    outer_ring = Gather(held(outer))
    e1 = outer_ring.step(1)
    blocks = [found[j] for j in ARRIVAL[:-1]] + list(found[4])
    normed, query, kv = project(
        [held(blocks[0])] + blocks[1:], gain_one, w_heads, cosine, sine
    )
    near_outs += [x_swap(held(own_outs[1])), x_swap(held(own_outs[2]))]
    own_outs.append(out_pair(held(found[0]), found[4][0]))
    close(e1, near_outs[1:], kv, own_outs[3])

    kv_peer = core_swap(held(kv))
    close(kv_peer)

    e2 = outer_ring.step(2, *ended[-1])
    near_outs.append(x_swap(held(own_outs[3])))
    heads, mixed, lse, query_all, kv_all, kv_peer_all = attend_heads(
        numbers, query, kv, held(kv_peer)
    )
    close(e2, near_outs[3], heads)

    swapped = to_chips(held(heads))
    near_gate = x_swap(held(w_gate))
    out_rows = call(
        out_kernel,
        "stack_out",
        (((CHIPS * 2 * nq, width), low),),
        own_outs + near_outs[:3] + [held(near_outs[3])],
        far=range(8),
    )[0]
    far_ffn = [core_swap(held(w_gate)), core_swap(held(w_up)), core_swap(held(w_down))]
    close(swapped, near_gate, out_rows, far_ffn)

    e3 = outer_ring.step(3, *ended[-1])
    out_rows_peer = core_swap(held(out_rows))
    across_ffn = [core_swap(held(near_gate))]
    near_up = x_swap(held(w_up))
    middle, normed_two, attended, w_out = call(
        join_kernel,
        "join",
        (
            ((TOK, width), full),
            ((TOK, width), low),
            ((TOK, width), low),
            ((width, width), low),
        ),
        (held(swapped), out_rows, out_rows_peer, block, gain_two),
        scratch=[pltpu.VMEM((width, TOK), low)],
        far=(3,),
        far_out=(0, 2, 3),
    )
    close(e3, normed_two, across_ffn, near_up)

    normed_ring = Gather(held(normed_two))
    fed = []

    def ffn_group(n):
        group = GROUPS[n]
        if len(group) > 1:
            blocks, outers = ([ring.found[j] for j in group] for ring in (normed_ring, outer_ring))
        else:
            blocks, outers = (list(ring.found[group[0]]) for ring in (normed_ring, outer_ring))
        blocks[0] = held(blocks[0])
        fed.append(ffn(blocks, outers, w_gu, w_dn))
        return fed[-1][3]

    h1 = normed_ring.step(1)
    e4 = outer_ring.step(4, *ended[-1])
    near_down = x_swap(held(w_down))
    close(h1, e4, near_down)

    h2 = normed_ring.step(2, *ended[-1])
    across_ffn += [core_swap(held(near_up)), core_swap(held(near_down))]
    w_gu, w_dn = call(
        hidden_kernel,
        "hidden_rows",
        (((4 * units, width), low), ((2 * units, width), low)),
        (w_gate, w_up, w_down, near_gate, near_up, near_down, *far_ffn, *across_ffn),
        far=range(12),
    )
    close(h2, w_gu)

    h3 = normed_ring.step(3, *ended[-1])
    close(h3, ffn_group(0), ffn_group(1))

    h4 = normed_ring.step(4, *ended[-1])
    close(h4, ffn_group(2))

    ffn_group(3)

    def stored(terms, name, far=()):
        def make(number, up, down):
            if number == 1:
                return terms[3:]
            begin = 1 if number == 4 else 0
            part = terms[4 - number]
            return call(
                add_kernel,
                name,
                leaving(width),
                (part, part, up, down),
                far=far,
                windows={0: (TOK, begin), 1: (TOK, begin + 1)},
            )

        return make

    back_ring = Scatter(stored([part[4] for part in fed[:3]] + list(fed[3][4:]), "back_add"))
    close(back_ring.step(1))

    d2 = back_ring.step(2, *ended[-1])
    arrays = [part[n] for n in range(4) for part in fed]
    arrays[0] = held(arrays[0])
    sums = call(
        functools.partial(grads_kernel, len(GROUPS)),
        "ffn_grads",
        [((2 * units, width), full), ((units, width), full)] * 2 + [((CHIPS * TOK, 2 * units), low)],
        arrays,
        scratch=[
            pltpu.VMEM((CHIPS * TOK, width), low),
            pltpu.VMEM((CHIPS * TOK, 4 * units), low),
        ],
        far_out=(4,),
    )
    close(d2, sums[2])

    d3 = back_ring.step(3, *ended[-1])
    others = [core_swap(held(value)) for value in sums[2:4]]
    branch = call(
        branch_kernel,
        "branch",
        [((len(group) * TOK, width), full) for group in GROUPS[:3]] + leaving(width, TOK // 2),
        (held(sums[4]), w_dn),
        far_out=(0, 1, 2),
    )
    close(d3, others, branch[-1])

    d4 = back_ring.step(4, *ended[-1])
    kept = call(
        owners_kernel,
        "ffn_owners",
        [((count, width), full)] * 3 + [((count, width), low)] * 3,
        (*sums[:2], held(others[0]), others[1]),
        far_out=(0, 1, 2),
    )
    near_grads = [x_swap(kept[3])]
    close(d4, near_grads)

    branch_ring = Scatter(stored(branch, "branch_add", (0, 1)))
    z1 = branch_ring.step(1, *ended[-1])
    grad_middle, grad_branch, grad_heads, second_gain_grad = call(
        turn_kernel,
        "turn",
        (
            ((TOK, width), full),
            ((TOK, width), low),
            ((CHIPS, PAIR, TOK), low),
            ((1, width), full),
        ),
        (fed[0][4], *d4, middle, outer, gain_two, w_out),
        far=(3, 4, 6),
        far_out=(0,),
        windows={0: (TOK, 0)},
    )
    close(z1, grad_heads)

    grad_heads = to_chips(held(grad_heads))
    z2 = branch_ring.step(2, *ended[-1])
    near_grads.append(x_swap(held(kept[4])))
    keep, give = call(
        outer_kernel,
        "outer",
        (((CHIPS, 2 * nq, width), low), ((CHIPS, 2 * nq, width), low)),
        (held(grad_branch), attended),
        far=(1,),
        far_out=(0,),
        scratch=[pltpu.VMEM((width, width), full)],
    )
    close(grad_heads, z2, near_grads[1], give)

    z3 = branch_ring.step(3, *ended[-1])
    other = core_swap(held(give))
    grad_query, grad_own, grad_peer = attend_back(
        numbers, query_all, kv_all, kv_peer_all, held(grad_heads), mixed, lse, cosine, sine
    )
    close(z3, other, grad_query)

    z4 = branch_ring.step(4, *ended[-1])
    second = call(
        settle_kernel,
        "settle",
        (((CHIPS * 2 * nq, width), low),),
        (keep, held(other)),
        far=(0,),
    )[0]
    joined, *leave = call(
        spread_kernel,
        "spread",
        [((CHIPS * TOK, 4 * LANES), low)] + leaving(width, TOK // 2) + leaving(width, nq),
        (grad_query, grad_own, core_swap(held(grad_peer)), cosine, sine, w_heads, second),
        far=(3, 4, 5),
    )
    near_grads.append(x_swap(held(kept[5])))
    close(z4, leave, near_grads[2])

    def last_terms(number, up, down):
        if number == 1:
            return leave[:2]
        begin = STEP_ROWS[number] // TOK
        return call(
            product_kernel,
            "last_terms",
            leaving(width),
            (joined, joined, w_heads, up, down),
            far=(0, 1),
            windows={0: (TOK, begin), 1: (TOK, begin + 1)},
        )

    def out_terms(number, up, down):
        if number == 1:
            return leave[2:]
        begin = STEP_ROWS[number] // TOK
        return call(
            rows_kernel,
            "out_terms",
            leaving(width, 2 * nq),
            (second, second, up, down),
            far=(0, 1),
            windows={0: (2 * nq, begin), 1: (2 * nq, begin + 1)},
        )

    grad_ring = Scatter(out_terms)
    last_ring = Scatter(last_terms)
    t1 = last_ring.step(1, *ended[-1])
    g1 = grad_ring.step(1, *ended[-1])
    mine, send, gain_grads = call(
        heads_grad_kernel,
        "heads_grad",
        (((2, HD, width), full), ((2, HD, width), full), ((2, width), full)),
        (held(joined), w_heads, gain_one, second_gain_grad, normed),
        scratch=[pltpu.VMEM((4 * LANES, width), full)],
        far=range(1, 5),
    )
    t2 = last_ring.step(2)
    g2 = grad_ring.step(2)
    other = core_swap(send)
    result = call(
        result_kernel,
        "result",
        (((TOK, width), low),),
        (branch[0], after(z4[0], *t1), z4[1], middle),
        far=(0, 3),
        far_out=(0,),
        windows={0: (TOK, 0)},
    )[0]
    t3 = last_ring.step(3)
    g3 = grad_ring.step(3)
    mine = mine + other
    heads_grad = mine[0] + x_swap(mine[1].astype(low)).astype(full)
    t4 = last_ring.step(4)
    g4 = grad_ring.step(4)
    gain_grads = after(gain_grads, *t2).reshape(2, CHIPS, 4 * nq)
    gain_grads = jnp.sum(to_chips(jnp.transpose(gain_grads, (1, 0, 2))), axis=0)
    ffn_grad = [own + after(other, *t2).astype(full) for own, other in zip(kept[:3], near_grads)]
    keep, give = call(
        owned_kernel,
        "owned",
        (((nq, width), full), ((nq, width), low)),
        (second, *g4),
        far=(0,),
        windows={0: (2 * nq, 0)},
    )
    output_grad = keep + x_swap(give).astype(full)
    gain_grads = gain_grads + core_swap(gain_grads)
    gain_grads = gain_grads + x_swap(gain_grads)
    gain_grads = lax.dynamic_slice_in_dim(gain_grads, (2 * core + side) * nq, nq, 1)
    grad_tokens = call(
        last_kernel,
        "last",
        (((TOK, width), full),),
        (joined, w_heads, *t4, block, grad_middle, gain_one),
        far=(0, 1, 4, 5),
        far_out=(0,),
        windows={0: (TOK, 0)},
    )[0]
    return (
        result[None],
        grad_tokens[None],
        gain_grads[0],
        gain_grads[1],
        heads_grad[:nq],
        heads_grad[nq : nq + nk],
        heads_grad[nq + nk :],
        output_grad,
        ffn_grad[0],
        ffn_grad[1],
        ffn_grad[2],
    )


def by_plane(mesh):
    return dict(mesh.shape) == {"blk": 2 * CHIPS, "fsdp": 2} and KVH == CHIPS


def solution(mesh):
    in_specs = (
        P("fsdp", "blk", None),
        P("fsdp", "blk", None),
        P("fsdp", None),
        P("fsdp", "blk"),
        P(("blk", "fsdp")),
        P(("blk", "fsdp")),
        P(("blk", "fsdp"), None),
        P(("blk", "fsdp"), None),
        P(("blk", "fsdp"), None),
        P(("blk", "fsdp"), None),
        P(("blk", "fsdp"), None),
        P(("blk", "fsdp"), None),
        P(("blk", "fsdp"), None),
    )
    out_specs = (
        P("fsdp", "blk", None),
        P("fsdp", "blk", None),
        P(("blk", "fsdp")),
        P(("blk", "fsdp")),
        P(("blk", "fsdp"), None),
        P(("blk", "fsdp"), None),
        P(("blk", "fsdp"), None),
        P(("blk", "fsdp"), None),
        P(("blk", "fsdp"), None),
        P(("blk", "fsdp"), None),
        P(("blk", "fsdp"), None),
    )
    body = plane_shards if by_plane(mesh) else shards
    return jax.shard_map(body, mesh=mesh, in_specs=in_specs, out_specs=out_specs, check_vma=False)
```
